32 devices in a mesh: px: 4 (over z), py: 8 (over y, x, core).
Axes of the slice: x: 2, y: 2, z: 4, core: 2. Of those that a mesh axis runs over, the one named last changes fastest.
Arguments:
- vorticity: float32 [3, 192, 36864], P(None, 'px', 'py'), may hold values from -6 to 6
Outputs:
- velocity: float32 [3, 192, 36864], P(None, 'px', 'py')
- stretching: float32 [3, 192, 36864], P(None, 'px', 'py')
The draws below stay inside these ranges and needn't reach their ends.
All inputs are finite; a program needn't handle non-finite values.
Results may differ from the reference program's by a relative error of at most 0.0003.
Values sent between devices are 32-bit elements; how exact they have to be, the bound alone decides.
No kernel may reach another device: no remote copies, remote signals or barrier semaphores. Data moves between devices by JAX's collectives and lax.ppermute only.
A program may use at most 128 MiB of HBM per device.

```python
import math
import jax
import jax.numpy as jnp
from jax import lax

G = 192


def draw_vorticity(key, part):
    noise_key = jax.random.fold_in(key, 11)
    values = jax.random.normal(noise_key, (3, G, G, G), jnp.float32)
    return jnp.clip(values, -6.0, 6.0).reshape(3, G, G * G)


def setup_inputs(seed: int = 0) -> dict:
    streams_of = jax.random.split(jax.random.key(seed), 2)
    vorticity = draw_vorticity(jax.random.fold_in(streams_of[1], 71), 0)
    return {"vorticity": vorticity}


smoothing = 1.0


def window(padded, axis, offset):
    starts = [0, 2, 2, 2]
    limits = [padded.shape[0], padded.shape[1] - 2, padded.shape[2] - 2, padded.shape[3] - 2]
    starts[axis] = starts[axis] + offset
    limits[axis] = limits[axis] + offset
    return lax.slice(padded, starts, limits)


def derivative(padded, axis):
    near = window(padded, axis, 1) - window(padded, axis, -1)
    far = window(padded, axis, 2) - window(padded, axis, -2)
    return (8.0 * near - far) / 12.0


def reference(vorticity):
    field = vorticity.reshape(3, G, G, G)
    length = 2 * G
    index = jnp.arange(length, dtype=jnp.int32)
    signed = jnp.where(index < length // 2, index, index - length)
    wave = signed.astype(jnp.float32) * (2.0 * math.pi / length)
    slope = jnp.where(index == length // 2, 0.0, wave)
    keep = jnp.where(index == length // 2, 0.0, 1.0)
    half_index = jnp.arange(length // 2 + 1, dtype=jnp.int32)
    half_wave = half_index.astype(jnp.float32) * (2.0 * math.pi / length)
    half_slope = jnp.where(half_index == length // 2, 0.0, half_wave)
    half_keep = jnp.where(half_index == length // 2, 0.0, 1.0)
    square = wave[:, None, None] ** 2 + wave[None, :, None] ** 2 + half_wave[None, None, :] ** 2
    mask = keep[:, None, None] * keep[None, :, None] * half_keep[None, None, :]
    green = mask * jnp.exp(-0.5 * smoothing * smoothing * square) / (square + jnp.where(square == 0.0, 1.0, 0.0))
    slope_x = slope[:, None, None]
    slope_y = slope[None, :, None]
    slope_z = half_slope[None, None, :]
    potential = []
    for component in range(3):
        spread = jnp.pad(field[component], ((0, G), (0, G), (0, G)))
        potential.append(jnp.fft.rfftn(spread) * green)
    terms = [slope_y * potential[2] - slope_z * potential[1],
             slope_z * potential[0] - slope_x * potential[2],
             slope_x * potential[1] - slope_y * potential[0]]
    fields = []
    for component in range(3):
        back = jnp.fft.irfftn(1j * terms[component], s=(length, length, length))
        fields.append(back[:G, :G, :G].astype(jnp.float32))
    flow = jnp.stack(fields)
    padded = jnp.pad(flow, ((0, 0), (2, 2), (2, 2), (2, 2)))
    stretching = (field[0] * derivative(padded, 1) + field[1] * derivative(padded, 2)
                  + field[2] * derivative(padded, 3))
    return flow.reshape(3, G, G * G), stretching.reshape(3, G, G * G)
```

```python
import math

import jax
import jax.numpy as jnp
import numpy as np
from jax import lax
from jax.experimental import pallas as pl
from jax.experimental.pallas import tpu as pltpu
from jax.sharding import PartitionSpec as P

smoothing = 1.0
highest = lax.Precision.HIGHEST
f32 = jnp.float32
bf16 = jnp.bfloat16
CHUNKS = 2
LANES = 128


def split_table(table):
    high = table.astype(np.float32).astype(jnp.bfloat16)
    low = (table - high.astype(np.float64)).astype(np.float32).astype(jnp.bfloat16)
    return high, low


def waves(modes, length):
    return np.asarray(modes, np.float64) * (2.0 * math.pi / length)


def basis(points, modes, kinds, length):
    angle = (np.arange(points)[:, None] * np.asarray(modes)[None, :] % length) * (
        2.0 * math.pi / length
    )
    return np.where(np.asarray(kinds)[None, :] == 0, np.cos(angle), np.sin(angle))


def weights(modes, length):
    return np.where(np.asarray(modes) == 0, 1.0, 2.0) / length


def lane_order(modes):
    full = modes // LANES * LANES
    index, kind = [], []
    for start in range(0, full, LANES):
        for k in (0, 1):
            index += list(range(start, start + LANES))
            kind += [k] * LANES
    for k in (0, 1):
        index += list(range(full, modes))
        kind += [k] * (modes - full)
    return np.array(index), np.array(kind)


def dot(first, second, dims):
    return lax.dot_general(first, second, (dims, ((), ())), preferred_element_type=f32)


NN = ((1,), (0,))
NT = ((1,), (1,))
TN = ((0,), (0,))


def halves(value):
    high = value.astype(bf16)
    low = (value - high.astype(f32)).astype(bf16)
    return high, low


def depth_forward(shard, table, sizes, chunk):
    rows, cols, G, devices, kept, lanes = sizes
    units = 6 * kept
    block = 2 * kept * devices
    tiles = lanes // LANES

    def kernel(shard_ref, table_ref, out_ref, high_ref, low_ref, mid_ref):
        table_high, table_low = table_ref[0], table_ref[1]
        for c in range(3):
            for y in range(cols):
                high, low = halves(shard_ref[c, :, y * G : (y + 1) * G])
                high_ref[y * rows : (y + 1) * rows, :] = high
                low_ref[y * rows : (y + 1) * rows, :] = low
            mid_ref[c * block : (c + 1) * block, :] = (
                dot(table_high, high_ref[...], NT)
                + dot(table_high, low_ref[...], NT)
                + dot(table_low, high_ref[...], NT)
            )
        fill = [jnp.zeros((devices, lanes - units * rows), f32)] if lanes > units * rows else []
        for y in range(cols):
            pieces = [
                mid_ref[u * devices : (u + 1) * devices, y * rows : (y + 1) * rows]
                for u in range(units)
            ]
            line = jnp.concatenate(pieces + fill, axis=1)
            for t in range(tiles):
                at = pl.ds(t * cols + y, devices, stride=tiles * cols)
                out_ref[at, :] = line[:, t * LANES : (t + 1) * LANES]

    return pl.pallas_call(
        kernel,
        out_shape=jax.ShapeDtypeStruct((devices * tiles * cols, LANES), f32),
        scratch_shapes=[
            pltpu.VMEM((rows * cols, G), bf16),
            pltpu.VMEM((rows * cols, G), bf16),
            pltpu.VMEM((3 * block, rows * cols), f32),
        ],
        cost_estimate=pl.CostEstimate(
            flops=18 * block * G * rows * cols,
            bytes_accessed=4 * (3 * rows * cols * G + devices * cols * lanes),
            transcendentals=0,
        ),
        name="depth_forward",
    )(shard, table)


def depth_inverse(lines, table, before, sizes):
    rows, cols, G, devices, kept, lanes = sizes
    units = 6 * kept
    block = 2 * kept * devices
    tiles = lanes // LANES
    extra = [] if before is None else [before]

    def kernel(lines_ref, table_ref, *refs):
        before_ref = refs[0] if before is not None else None
        out_ref, mid_ref, done_ref = refs[len(extra) :]
        for y in range(cols):
            line = jnp.concatenate(
                [
                    lines_ref[pl.ds(t * cols + y, devices, stride=tiles * cols), :]
                    for t in range(tiles)
                ],
                axis=1,
            )
            for u in range(units):
                mid_ref[u * devices : (u + 1) * devices, y * rows : (y + 1) * rows] = line[
                    :, u * rows : (u + 1) * rows
                ]
        table_high, table_low = table_ref[0], table_ref[1]
        for c in range(3):
            high, low = halves(mid_ref[c * block : (c + 1) * block, :].T)
            done_ref[...] = (
                dot(high, table_high, NN) + dot(low, table_high, NN) + dot(high, table_low, NN)
            )
            for y in range(0, cols, 2):
                pair = jnp.concatenate(
                    [done_ref[y * rows : (y + 1) * rows, :], done_ref[(y + 1) * rows : (y + 2) * rows, :]],
                    axis=1,
                )
                if before_ref is not None:
                    pair = pair + before_ref[c, :, y * G : (y + 2) * G]
                out_ref[c, :, y * G : (y + 2) * G] = pair

    return pl.pallas_call(
        kernel,
        out_shape=jax.ShapeDtypeStruct((3, rows, cols * G), f32),
        scratch_shapes=[
            pltpu.VMEM((3 * block, rows * cols), f32),
            pltpu.VMEM((rows * cols, G), f32),
        ],
        cost_estimate=pl.CostEstimate(
            flops=18 * block * G * rows * cols,
            bytes_accessed=4 * (6 * rows * cols * G + devices * cols * lanes),
            transcendentals=0,
        ),
        name="depth_inverse",
    )(lines, table, *extra)


def planes(lines, place, tables, sizes, chunk, groups):
    rows, cols, G, devices, kept, lanes = sizes
    units = 6 * kept
    length = 2 * G
    step = 16
    unit_wave = 2.0 * math.pi / length
    full = G // LANES * LANES

    def kernel(place_ref, lines_ref, line_ref, wide_ref, inv_wide_ref, inv_line_ref,
               kx_ref, ky_ref, out_ref, left_ref, spec_ref, turned_ref, back_ref):
        line_high, line_low = line_ref[0], line_ref[1]
        for p in range(groups):
            high, low = halves(
                jnp.concatenate(
                    [lines_ref[p, :, t].reshape(G, LANES).T for t in range(lanes // LANES)], axis=0
                )
            )
            done = dot(high, line_high, NN) + dot(low, line_high, NN) + dot(high, line_low, NN)
            for u in range(units):
                c, j, k = u // (2 * kept), u // 2 % kept, u % 2
                at = (2 * c + k) * length
                high, low = halves(done[u * rows : (u + 1) * rows, :])
                for third, part in ((0, high), (1, low), (2, high)):
                    left_ref[j, third * G + p * rows : third * G + (p + 1) * rows, at : at + length] = part

        def one_depth(j, _):
            index = (chunk * kept + j) * devices + place_ref[0]
            kz = index.astype(f32) * unit_wave

            def widen(u, _):
                at = pl.multiple_of(u * length, LANES)
                spec_ref[:, pl.ds(at, length)] = dot(
                    wide_ref[...], left_ref[j, :, pl.ds(at, length)], NN
                )
                return 0

            lax.fori_loop(0, 6, widen, 0)

            def turn(r, _):
                top = pl.multiple_of(r * step, step)
                kx = kx_ref[pl.ds(top, step), :]

                def store(c, k, half, lane, value):
                    high, low = halves(value)
                    at = (2 * c + k) * length + lane
                    for third, part in ((0, high), (1, low), (2, high)):
                        turned_ref[pl.ds(third * length + half * G + top, step), at : at + LANES] = part

                def green_of(lane):
                    ky = ky_ref[0:1, lane : lane + LANES]
                    square = kx * kx + ky * ky + kz * kz
                    return jnp.exp(-0.5 * smoothing * smoothing * square) / (
                        square + jnp.where(square == 0.0, 1.0, 0.0)
                    )

                def load(c, k, half, lane):
                    at = (2 * c + k) * length + lane
                    return spec_ref[pl.ds(half * G + top, step), at : at + LANES]

                def curl(lane_of, count, dy_of, green):
                    gx = green * kx
                    gz = green * kz
                    got = {
                        (c, k, h, t): load(c, k, h, lane_of[t])
                        for c in range(3) for k in (0, 1) for h in (0, 1) for t in range(count)
                    }

                    def dx(c, k, h, t):
                        value = gx * got[c, k, 1 - h, t]
                        return value if h == 0 else -value

                    def dz(c, k, h, t):
                        value = gz * got[c, 1 - k, h, t]
                        return value if k == 0 else -value

                    def dy(c, k, h, t):
                        return dy_of(got, c, k, h, t)

                    for k in (0, 1):
                        for h in (0, 1):
                            for t in range(count):
                                store(0, k, h, lane_of[t], dy(2, k, h, t) - dz(1, k, h, t))
                                store(1, k, h, lane_of[t], dz(0, k, h, t) - dx(2, k, h, t))
                                store(2, k, h, lane_of[t], dx(1, k, h, t) - dy(0, k, h, t))

                for tile in range(full // LANES):
                    lane = 2 * tile * LANES
                    green = green_of(lane)
                    gy = green * ky_ref[0:1, lane : lane + LANES]

                    def dy_pair(got, c, k, h, t, gy=gy):
                        value = gy * got[c, k, h, 1 - t]
                        return value if t == 0 else -value

                    curl((lane, lane + LANES), 2, dy_pair, green)
                if full < G:
                    lane = 2 * full
                    green = green_of(lane)
                    gy = green * ky_ref[0:1, lane : lane + LANES]

                    def dy_roll(got, c, k, h, t):
                        return gy * pltpu.roll(got[c, k, h, t], LANES // 2, 1)

                    curl((lane,), 1, dy_roll, green)
                return 0

            lax.fori_loop(0, G // step, turn, 0)

            for c in range(3):
                for k in (0, 1):
                    at = (2 * c + k) * length
                    done = dot(inv_wide_ref[...], turned_ref[:, at : at + length], NN)
                    high, low = halves(done)
                    u = c * 2 * kept + k
                    for p in range(groups):
                        target = pl.ds(pl.multiple_of((u + 2 * j) * rows, 16), rows)
                        for third, part in ((0, high), (1, low), (2, high)):
                            back_ref[p, target, third * length : (third + 1) * length] = part[
                                p * rows : (p + 1) * rows, :
                            ]
            return 0

        lax.fori_loop(0, kept, one_depth, 0)
        if lanes > units * rows:
            back_ref[:, units * rows :, :] = jnp.zeros(
                (groups, lanes - units * rows, 3 * length), bf16
            )
        for p in range(groups):
            for t in range(lanes // LANES):
                done = dot(inv_line_ref[...], back_ref[p, t * LANES : (t + 1) * LANES, :], NT)
                out_ref[p, :, t] = done.reshape(G // cols, cols, LANES)

    vmem = pl.BlockSpec(memory_space=pltpu.VMEM)
    flops = 6 * (2 * groups * lanes * G * length + 12 * kept * length * G * length)
    return pl.pallas_call(
        kernel,
        out_shape=jax.ShapeDtypeStruct(lines.shape, f32),
        in_specs=[pl.BlockSpec(memory_space=pltpu.SMEM)] + [vmem] * 7,
        out_specs=vmem,
        scratch_shapes=[
            pltpu.VMEM((kept, 3 * G, 6 * length), bf16),
            pltpu.VMEM((length, 6 * length), f32),
            pltpu.VMEM((3 * length, 6 * length), bf16),
            pltpu.VMEM((groups, lanes, 3 * length), bf16),
        ],
        cost_estimate=pl.CostEstimate(
            flops=flops, bytes_accessed=8 * groups * G * lanes, transcendentals=kept * G * G
        ),
        compiler_params=pltpu.CompilerParams(vmem_limit_bytes=60 * 1024 * 1024),
        name="planes",
    )(place, lines, *tables)


def with_halo_parts(flow, cols, G):
    def shifted(piece, axis, up):
        devices = lax.axis_size(axis)
        pairs = [(i, i + 1) for i in range(devices - 1)]
        if not up:
            pairs = [(j, i) for i, j in pairs]
        return lax.ppermute(piece, axis, pairs)

    rows = flow.shape[1]
    return (
        shifted(lax.slice_in_dim(flow, rows - 2, rows, axis=1), "px", True),
        shifted(lax.slice_in_dim(flow, 0, 2, axis=1), "px", False),
        shifted(lax.slice_in_dim(flow, (cols - 2) * G, cols * G, axis=2), "py", True),
        shifted(lax.slice_in_dim(flow, 0, 2 * G, axis=2), "py", False),
    )


def stretch(field, flow, halos, sizes):
    rows, cols, G = sizes[:3]
    width = 2 * G

    def kernel(field_ref, flow_ref, up_ref, down_ref, left_ref, right_ref, out_ref, ext_ref, tall_ref):
        for c in range(3):
            ext_ref[c, :, 0:width] = left_ref[c]
            ext_ref[c, :, width : width + cols * G] = flow_ref[c]
            ext_ref[c, :, width + cols * G :] = right_ref[c]
            tall_ref[c, 6:8, :] = up_ref[c]
            tall_ref[c, 8 : 8 + rows, :] = flow_ref[c]
            tall_ref[c, 8 + rows : 10 + rows, :] = down_ref[c]
        depth = lax.broadcasted_iota(jnp.int32, (rows, width), 1) % G

        def combine(p1, m1, p2, m2):
            return (8.0 * (p1 - m1) - (p2 - m2)) * (1.0 / 12.0)

        def block(b, _):
            at = pl.multiple_of(b * width, LANES)
            for c in range(3):
                here = flow_ref[c, :, pl.ds(at, width)]

                def depth_shift(s):
                    moved = pltpu.roll(here, (-s) % width, 1)
                    inside = (depth + s >= 0) & (depth + s < G)
                    return jnp.where(inside, moved, 0.0)

                total = field_ref[2, :, pl.ds(at, width)] * combine(
                    depth_shift(1), depth_shift(-1), depth_shift(2), depth_shift(-2)
                )
                window = ext_ref[c, :, pl.ds(at, 3 * width)]
                total += field_ref[1, :, pl.ds(at, width)] * combine(
                    window[:, 3 * G : 5 * G], window[:, G : 3 * G], window[:, 4 * G :], window[:, : 2 * G]
                )
                total += field_ref[0, :, pl.ds(at, width)] * combine(
                    tall_ref[c, 9 : 9 + rows, pl.ds(at, width)],
                    tall_ref[c, 7 : 7 + rows, pl.ds(at, width)],
                    tall_ref[c, 10 : 10 + rows, pl.ds(at, width)],
                    tall_ref[c, 6 : 6 + rows, pl.ds(at, width)],
                )
                out_ref[c, :, pl.ds(at, width)] = total
            return 0

        lax.fori_loop(0, cols // 2, block, 0)

    return pl.pallas_call(
        kernel,
        out_shape=jax.ShapeDtypeStruct(flow.shape, f32),
        scratch_shapes=[
            pltpu.VMEM((3, rows, cols * G + 2 * width), f32),
            pltpu.VMEM((3, rows + 16, cols * G), f32),
        ],
        cost_estimate=pl.CostEstimate(
            flops=60 * flow.size, bytes_accessed=12 * flow.size, transcendentals=0
        ),
        name="stretch",
    )(field, flow, *halos)


def fast_sizes(vorticity):
    rows = vorticity.shape[1]
    G = rows * lax.axis_size("px")
    cols = vorticity.shape[2] // G
    devices = lax.axis_size("px") * lax.axis_size("py")
    if rows % 16 or cols % 8 or G % (CHUNKS * devices) or G % LANES not in (0, LANES // 2):
        return None
    kept = G // (CHUNKS * devices)
    lanes = -(-6 * kept * rows // LANES) * LANES
    return rows, cols, G, devices, kept, lanes


def triple(table, axis):
    high, low = split_table(table)
    return np.concatenate([high, high, low], axis=axis)


def fast(vorticity, sizes):
    rows, cols, G, devices, kept, lanes = sizes
    length = 2 * G
    groups = lax.axis_size("px")
    tiles = lanes // LANES
    axes = ("px", "py")
    place = lax.axis_index(axes).astype(jnp.int32).reshape(1)

    lane_modes, lane_kinds = lane_order(G)
    row_modes = np.concatenate([np.arange(G)] * 2)
    row_kinds = np.repeat([0, 1], G)
    line = np.stack(split_table(basis(G, lane_modes, lane_kinds, length)))
    wide = triple(basis(G, row_modes, row_kinds, length).T, 1)
    inv_wide = triple(basis(G, row_modes, row_kinds, length) * weights(row_modes, length), 1)
    inv_line = triple(basis(G, lane_modes, lane_kinds, length) * weights(lane_modes, length), 1)
    kx = np.broadcast_to(waves(np.arange(G), length)[:, None], (G, LANES)).astype(np.float32)
    signs = np.where(lane_kinds == 0, 1.0, -1.0)
    full = G // LANES * LANES
    signs[: 2 * full] = 1.0
    ky = np.broadcast_to((waves(lane_modes, length) * signs)[None, :], (8, length)).astype(np.float32)
    tables = tuple(jnp.asarray(t) for t in (line, wide, inv_wide, inv_line, kx, ky))

    def depth_tables(chunk):
        modes = np.array([
            (chunk * kept + j) * devices + d
            for j in range(kept) for k in (0, 1) for d in range(devices)
        ])
        kinds = np.array([k for j in range(kept) for k in (0, 1) for d in range(devices)])
        table = basis(G, modes, kinds, length)
        forward = np.stack(split_table(table.T))
        inverse = np.stack(split_table((table * weights(modes, length)).T))
        return jnp.asarray(forward), jnp.asarray(inverse)

    def exchange(value):
        value = value.reshape(devices, tiles * cols, LANES)
        return lax.all_to_all(value, axes, split_axis=0, concat_axis=0, tiled=True)

    arrived = []
    for chunk in range(CHUNKS):
        sent = depth_forward(vorticity, depth_tables(chunk)[0], sizes, chunk)
        arrived.append(exchange(sent))
    returned = []
    for chunk in range(CHUNKS):
        lines = arrived[chunk].reshape(groups, G // cols, tiles, cols, LANES)
        done = planes(lines, place, tables, sizes, chunk, groups)
        returned.append(exchange(done))
    flow = None
    for chunk in range(CHUNKS):
        flow = depth_inverse(
            returned[chunk].reshape(devices * tiles * cols, LANES), depth_tables(chunk)[1], flow, sizes
        )
    halos = with_halo_parts(flow, cols, G)
    return flow, stretch(vorticity, flow, halos, sizes)


def with_halo(shard, sides, width):
    for axis, dim in sides:
        devices, length = (lax.axis_size(axis), shard.shape[dim])
        up = [(i, (i + 1) % devices) for i in range(devices - 1)]
        down = [(j, i) for i, j in up]
        last = lax.slice_in_dim(shard, length - width, length, axis=dim)
        leading = lax.slice_in_dim(shard, 0, width, axis=dim)
        before = lax.ppermute(last, axis, up)
        after = lax.ppermute(leading, axis, down)
        shard = jnp.concatenate([before, shard, after], axis=dim)
    return shard


def twiddle(count_in, count_out, length, factor):
    source = lax.broadcasted_iota(jnp.int32, (count_in, count_out), 0)
    target = lax.broadcasted_iota(jnp.int32, (count_in, count_out), 1)
    angle = (source * target % length).astype(jnp.float32) * (2.0 * math.pi / length)
    cosine = jnp.cos(angle) * factor
    sine = jnp.sin(angle) * factor
    return (
        jnp.broadcast_to(cosine, (3, count_in, count_out)),
        jnp.broadcast_to(sine, (3, count_in, count_out)),
    )


def product(einsum_form, first, second):
    return jnp.einsum(einsum_form, first, second, precision=highest)


def forward_left(pair, einsum_form, tables):
    real_part, imag_part = pair
    cosine_table, sine_table = tables
    return (
        product(einsum_form, cosine_table, real_part) + product(einsum_form, sine_table, imag_part),
        product(einsum_form, cosine_table, imag_part) - product(einsum_form, sine_table, real_part),
    )


def forward_right(pair, einsum_form, tables):
    real_part, imag_part = pair
    cosine_table, sine_table = tables
    return (
        product(einsum_form, real_part, cosine_table) + product(einsum_form, imag_part, sine_table),
        product(einsum_form, imag_part, cosine_table) - product(einsum_form, real_part, sine_table),
    )


def backward_left(pair, einsum_form, tables):
    real_part, imag_part = pair
    cosine_table, sine_table = tables
    return (
        product(einsum_form, cosine_table, real_part) - product(einsum_form, sine_table, imag_part),
        product(einsum_form, cosine_table, imag_part) + product(einsum_form, sine_table, real_part),
    )


def wavenumbers(start, count, length, position):
    index = start + lax.iota(jnp.int32, count)
    signed = jnp.where(index < length // 2, index, index - length)
    wave = signed.astype(jnp.float32) * (2.0 * math.pi / length)
    slope = jnp.where(index == length // 2, 0.0, wave)
    keep = jnp.where(index == length // 2, 0.0, 1.0)
    shape = [1, 1, 1, 1]
    shape[position] = count
    return (wave.reshape(shape), slope.reshape(shape), keep.reshape(shape))


def velocity_spectrum(pair, waves_x, waves_y, waves_z):
    square = waves_x[0] ** 2 + waves_y[0] ** 2 + waves_z[0] ** 2
    mask = waves_x[2] * waves_y[2] * waves_z[2]
    green = (
        mask
        * jnp.exp(-0.5 * smoothing * smoothing * square)
        / (square + jnp.where(square == 0.0, 1.0, 0.0))
    )
    slope_x, slope_y, slope_z = (waves_x[1][0], waves_y[1][0], waves_z[1][0])

    def curl(field):
        return jnp.stack(
            [
                slope_y * field[2] - slope_z * field[1],
                slope_z * field[0] - slope_x * field[2],
                slope_x * field[1] - slope_y * field[0],
            ]
        )

    real_part = pair[0] * green
    imag_part = pair[1] * green
    return (jnp.swapaxes(-curl(imag_part), 1, 2), jnp.swapaxes(curl(real_part), 1, 2))


def window(padded, axis, offset):
    starts = [0, 2, 2, 2]
    limits = [padded.shape[0], padded.shape[1] - 2, padded.shape[2] - 2, padded.shape[3] - 2]
    starts[axis] = starts[axis] + offset
    limits[axis] = limits[axis] + offset
    return lax.slice(padded, starts, limits)


def derivative(padded, axis):
    near = window(padded, axis, 1) - window(padded, axis, -1)
    far = window(padded, axis, 2) - window(padded, axis, -2)
    return (8.0 * near - far) / 12.0


def general(vorticity):
    block_rows = vorticity.shape[1]
    G = block_rows * lax.axis_size("px")
    block_cols = vorticity.shape[2] // G
    field = vorticity.reshape(3, block_rows, block_cols, G)
    length = 2 * G
    depth_tables = twiddle(G, G, length, 1.0)
    line_tables = twiddle(G, length, length, 1.0)
    inverse_tables = twiddle(length, G, length, 1.0 / length)
    closing = twiddle(G, G, length, 1.0 / length)
    weights = jnp.where(lax.iota(jnp.int32, G) == 0, 1.0, 2.0)[None, :, None]
    closing_cos = closing[0] * weights
    closing_sin = closing[1] * weights
    pair = (
        product("czk,cxyz->ckxy", depth_tables[0], field),
        -product("czk,cxyz->ckxy", depth_tables[1], field),
    )
    pair = (
        lax.all_to_all(pair[0], "py", split_axis=1, concat_axis=3, tiled=True),
        lax.all_to_all(pair[1], "py", split_axis=1, concat_axis=3, tiled=True),
    )
    pair = forward_left(pair, "cyl,ckxy->clkx", line_tables)
    pair = (
        lax.all_to_all(pair[0], "px", split_axis=1, concat_axis=3, tiled=True),
        lax.all_to_all(pair[1], "px", split_axis=1, concat_axis=3, tiled=True),
    )
    pair = forward_right(pair, "clkx,cxm->clkm", line_tables)
    rows = pair[0].shape[1]
    depth = pair[0].shape[2]
    waves_y = wavenumbers(lax.axis_index("px") * rows, rows, length, 1)
    waves_z = wavenumbers(lax.axis_index("py") * depth, depth, length, 2)
    waves_x = wavenumbers(0, length, length, 3)
    pair = velocity_spectrum(pair, waves_x, waves_y, waves_z)
    pair = backward_left(pair, "cmx,cklm->cxkl", inverse_tables)
    pair = (
        lax.all_to_all(pair[0], "px", split_axis=1, concat_axis=3, tiled=True),
        lax.all_to_all(pair[1], "px", split_axis=1, concat_axis=3, tiled=True),
    )
    pair = backward_left(pair, "cly,cxkl->cyxk", inverse_tables)
    pair = (
        lax.all_to_all(pair[0], "py", split_axis=1, concat_axis=3, tiled=True),
        lax.all_to_all(pair[1], "py", split_axis=1, concat_axis=3, tiled=True),
    )
    flow = product("cyxk,ckz->cyxz", pair[0], closing_cos) - product(
        "cyxk,ckz->cyxz", pair[1], closing_sin
    )
    flow = jnp.swapaxes(flow, 1, 2)
    padded = with_halo(flow, (("px", 1), ("py", 2)), 2)
    padded = jnp.pad(padded, ((0, 0), (0, 0), (0, 0), (2, 2)))
    stretching = (
        field[0] * derivative(padded, 1)
        + field[1] * derivative(padded, 2)
        + field[2] * derivative(padded, 3)
    )
    return (
        flow.reshape(3, block_rows, block_cols * G),
        stretching.reshape(3, block_rows, block_cols * G),
    )


def on_device(vorticity):
    sizes = fast_sizes(vorticity)
    return general(vorticity) if sizes is None else fast(vorticity, sizes)


def solution(mesh):
    in_specs = (P(None, "px", "py"),)
    out_specs = (P(None, "px", "py"), P(None, "px", "py"))
    return jax.shard_map(
        on_device, mesh=mesh, in_specs=in_specs, out_specs=out_specs, check_vma=False
    )
```

```python
import math

import jax
import jax.numpy as jnp
import numpy as np
from jax import lax
from jax.experimental import pallas as pl
from jax.experimental.pallas import tpu as pltpu
from jax.sharding import PartitionSpec as P

smoothing = 1.0
highest = lax.Precision.HIGHEST
f32 = jnp.float32
bf16 = jnp.bfloat16
LANES = 128
SUB = 8
PLANES_VMEM = 44 * 1024 * 1024


def split_table(table):
    high = table.astype(np.float32).astype(jnp.bfloat16)
    low = (table - high.astype(np.float64)).astype(np.float32).astype(jnp.bfloat16)
    return high, low


def waves(modes, length):
    return np.asarray(modes, np.float64) * (2.0 * math.pi / length)


def basis(points, modes, kinds, length):
    angle = (np.arange(points)[:, None] * np.asarray(modes)[None, :] % length) * (
        2.0 * math.pi / length
    )
    return np.where(np.asarray(kinds)[None, :] == 0, np.cos(angle), np.sin(angle))


def weights(modes, length):
    return np.where(np.asarray(modes) == 0, 1.0, 2.0) / length


def lane_order(modes):
    full = modes // LANES * LANES
    index, kind = [], []
    for start in range(0, full, LANES):
        for k in (0, 1):
            index += list(range(start, start + LANES))
            kind += [k] * LANES
    for k in (0, 1):
        index += list(range(full, modes))
        kind += [k] * (modes - full)
    return np.array(index), np.array(kind)


def dot(first, second, dims):
    return lax.dot_general(first, second, (dims, ((), ())), preferred_element_type=f32)


NN = ((1,), (0,))
NT = ((1,), (1,))
TN = ((0,), (0,))


def halves(value):
    high = value.astype(bf16)
    low = (value - high.astype(f32)).astype(bf16)
    return high, low


class Sizes:
    def __init__(self, rows, cols, G, devices, groups):
        self.rows, self.cols, self.G = rows, cols, G
        self.devices, self.groups = devices, groups
        self.bands = cols // SUB
        self.length = 2 * G
        total = G // devices
        first = max(1, total * 2 // 3)
        self.chunks = [(0, first), (first, total - first)] if total > first else [(0, first)]

    def units(self, kept):
        return 6 * kept

    def tiles(self, kept):
        return -(-self.bands * self.units(kept) * self.rows // LANES)


def fast_sizes(vorticity):
    rows = vorticity.shape[1]
    groups = lax.axis_size("px")
    G = rows * groups
    cols = vorticity.shape[2] // G
    devices = groups * lax.axis_size("py")
    if rows % 16 or cols % (2 * SUB) not in (0, SUB) or cols % SUB or cols % 2:
        return None
    if G % devices or devices % SUB or G % LANES not in (0, LANES // 2):
        return None
    return Sizes(rows, cols, G, devices, groups)


def depth_forward(shard, table, size, kept):
    rows, cols, G, devices = size.rows, size.cols, size.G, size.devices
    units, tiles, bands = size.units(kept), size.tiles(kept), size.bands
    block = 2 * kept * devices
    used = bands * units * rows

    def kernel(shard_ref, table_ref, out_ref, high_ref, low_ref, mid_ref):
        def component(c, _):
            for y in range(cols):
                high, low = halves(shard_ref[c, :, y * G : (y + 1) * G])
                high_ref[y * rows : (y + 1) * rows, :] = high
                low_ref[y * rows : (y + 1) * rows, :] = low
            mid_ref[pl.ds(pl.multiple_of(c * block, SUB), block), :] = (
                dot(table_ref[0], high_ref[...], NT)
                + dot(table_ref[0], low_ref[...], NT)
                + dot(table_ref[1], high_ref[...], NT)
            )
            return 0

        lax.fori_loop(0, 3, component, 0)
        fill = [jnp.zeros((devices, tiles * LANES - used), f32)] if tiles * LANES > used else []
        for s in range(SUB):
            pieces = [
                mid_ref[
                    u * devices : (u + 1) * devices,
                    (SUB * band + s) * rows : (SUB * band + s + 1) * rows,
                ]
                for band in range(bands)
                for u in range(units)
            ]
            line = jnp.concatenate(pieces + fill, axis=1)
            for t in range(tiles):
                at = pl.ds(t * SUB + s, devices, stride=tiles * SUB)
                out_ref[at, :] = line[:, t * LANES : (t + 1) * LANES]

    return pl.pallas_call(
        kernel,
        out_shape=jax.ShapeDtypeStruct((devices * tiles * SUB, LANES), f32),
        scratch_shapes=[
            pltpu.VMEM((rows * cols, G), bf16),
            pltpu.VMEM((rows * cols, G), bf16),
            pltpu.VMEM((3 * block, rows * cols), f32),
        ],
        cost_estimate=pl.CostEstimate(
            flops=18 * block * G * rows * cols,
            bytes_accessed=4 * (3 * rows * cols * G + devices * tiles * SUB * LANES),
            transcendentals=0,
        ),
        name="depth_forward",
    )(shard, table)


def depth_inverse(lines, table, before, size, kept, slabs):
    rows, cols, G, devices = size.rows, size.cols, size.G, size.devices
    units, tiles, bands = size.units(kept), size.tiles(kept), size.bands
    block = 2 * kept * devices
    extra = [] if before is None else [before]
    outs = [jax.ShapeDtypeStruct((3, rows, cols * G), f32)]
    if slabs:
        outs += [jax.ShapeDtypeStruct((3, 2, cols * G), f32)] * 2
        outs += [jax.ShapeDtypeStruct((3, rows, 2 * G), f32)] * 2

    def kernel(lines_ref, table_ref, *refs):
        before_ref = refs[0] if before is not None else None
        out_ref, *slab_refs = refs[len(extra) : len(extra) + len(outs)]
        mid_ref, done_ref = refs[len(extra) + len(outs) :]
        for s in range(SUB):
            line = jnp.concatenate(
                [
                    lines_ref[pl.ds(t * SUB + s, devices, stride=tiles * SUB), :]
                    for t in range(tiles)
                ],
                axis=1,
            )
            for band in range(bands):
                y = SUB * band + s
                for u in range(units):
                    at = (band * units + u) * rows
                    mid_ref[u * devices : (u + 1) * devices, y * rows : (y + 1) * rows] = line[
                        :, at : at + rows
                    ]

        def component(c, _):
            high, low = halves(mid_ref[pl.ds(pl.multiple_of(c * block, SUB), block), :].T)
            done_ref[...] = (
                dot(high, table_ref[0], NN)
                + dot(low, table_ref[0], NN)
                + dot(high, table_ref[1], NN)
            )
            for y in range(0, cols, 2):
                pair = jnp.concatenate(
                    [
                        done_ref[y * rows : (y + 1) * rows, :],
                        done_ref[(y + 1) * rows : (y + 2) * rows, :],
                    ],
                    axis=1,
                )
                if before_ref is not None:
                    pair = pair + before_ref[c, :, y * G : (y + 2) * G]
                out_ref[c, :, y * G : (y + 2) * G] = pair
                if slabs:
                    slab_refs[0][c, :, y * G : (y + 2) * G] = pair[rows - 2 :, :]
                    slab_refs[1][c, :, y * G : (y + 2) * G] = pair[:2, :]
                if slabs and y == cols - 2:
                    slab_refs[2][c] = pair
                if slabs and y == 0:
                    slab_refs[3][c] = pair
            return 0

        lax.fori_loop(0, 3, component, 0)

    return pl.pallas_call(
        kernel,
        out_shape=outs,
        scratch_shapes=[
            pltpu.VMEM((3 * block, rows * cols), f32),
            pltpu.VMEM((rows * cols, G), f32),
        ],
        cost_estimate=pl.CostEstimate(
            flops=18 * block * G * rows * cols,
            bytes_accessed=4 * (6 * rows * cols * G + devices * tiles * SUB * LANES),
            transcendentals=0,
        ),
        name="depth_inverse",
    )(lines, table, *extra)


def planes(lines, place, tables, size, kept):
    rows, cols, G, devices, groups = size.rows, size.cols, size.G, size.devices, size.groups
    units, tiles, bands, length = size.units(kept), size.tiles(kept), size.bands, size.length
    width = units * rows
    step = 16
    unit_wave = 2.0 * math.pi / length
    full = G // LANES * LANES
    others = G // cols

    def kernel(place_ref, lines_ref, line_ref, wide_ref, inv_wide_ref, inv_line_ref,
               kx_ref, ky_ref, out_ref, left_ref, spec_ref, turned_ref, back_ref):
        def arrive(p, _):
            flat = jnp.concatenate(
                [lines_ref[p, :, t].reshape(others * SUB, LANES).T for t in range(tiles)], axis=0
            )
            side = jnp.concatenate(
                [flat[band * width : (band + 1) * width, :] for band in range(bands)], axis=1
            )
            high, low = halves(side)
            done = (
                dot(high, line_ref[0], NN) + dot(low, line_ref[0], NN) + dot(high, line_ref[1], NN)
            )
            for u in range(units):
                c, j, k = u // (2 * kept), u // 2 % kept, u % 2
                at = (2 * c + k) * length
                high, low = halves(done[u * rows : (u + 1) * rows, :])
                for part, value in ((0, high), (1, low)):
                    target = pl.ds(pl.multiple_of(part * G + p * rows, 16), rows)
                    left_ref[j, target, at : at + length] = value
            return 0

        lax.fori_loop(0, groups, arrive, 0)

        def one_depth(j, _):
            index = (place_ref[1] + j) * devices + place_ref[0]
            kz = index.astype(f32) * unit_wave

            def widen(u, _):
                at = pl.ds(pl.multiple_of(u * length, LANES), length)
                spec_ref[:, at] = dot(wide_ref[:, :length], left_ref[j, :, at], NN) + dot(
                    wide_ref[:, length:], left_ref[j, :G, at], NN
                )
                return 0

            lax.fori_loop(0, 6, widen, 0)

            def turn(r, _):
                top = pl.multiple_of(r * step, step)
                kx = kx_ref[pl.ds(top, step), :]

                def store(c, k, half, lane, value):
                    at = (2 * c + k) * length + lane
                    for part, piece in zip((0, 1), halves(value)):
                        target = pl.ds(pl.multiple_of(part * length + half * G + top, step), step)
                        turned_ref[target, at : at + LANES] = piece

                def green_of(lane):
                    ky = ky_ref[0:1, lane : lane + LANES]
                    square = kx * kx + ky * ky + kz * kz
                    return jnp.exp(-0.5 * smoothing * smoothing * square) / (
                        square + jnp.where(square == 0.0, 1.0, 0.0)
                    )

                def load(c, k, half, lane):
                    at = (2 * c + k) * length + lane
                    target = pl.ds(pl.multiple_of(half * G + top, step), step)
                    return spec_ref[target, at : at + LANES]

                def curl(lane_of, dy_of, green):
                    gx = green * kx
                    gz = green * kz
                    many = range(len(lane_of))
                    got = {
                        (c, k, h, t): load(c, k, h, lane_of[t])
                        for c in range(3) for k in (0, 1) for h in (0, 1) for t in many
                    }

                    def dx(c, k, h, t):
                        value = gx * got[c, k, 1 - h, t]
                        return value if h == 0 else -value

                    def dz(c, k, h, t):
                        value = gz * got[c, 1 - k, h, t]
                        return value if k == 0 else -value

                    def dy(c, k, h, t):
                        return dy_of(got, c, k, h, t)

                    for k in (0, 1):
                        for h in (0, 1):
                            for t in many:
                                store(0, k, h, lane_of[t], dy(2, k, h, t) - dz(1, k, h, t))
                                store(1, k, h, lane_of[t], dz(0, k, h, t) - dx(2, k, h, t))
                                store(2, k, h, lane_of[t], dx(1, k, h, t) - dy(0, k, h, t))

                for tile in range(full // LANES):
                    lane = 2 * tile * LANES
                    green = green_of(lane)
                    gy = green * ky_ref[0:1, lane : lane + LANES]

                    def dy_pair(got, c, k, h, t, gy=gy):
                        value = gy * got[c, k, h, 1 - t]
                        return value if t == 0 else -value

                    curl((lane, lane + LANES), dy_pair, green)
                if full < G:
                    lane = 2 * full
                    green = green_of(lane)
                    gy = green * ky_ref[0:1, lane : lane + LANES]

                    def dy_roll(got, c, k, h, t):
                        return gy * pltpu.roll(got[c, k, h, t], LANES // 2, 1)

                    curl((lane,), dy_roll, green)
                return 0

            lax.fori_loop(0, G // step, turn, 0)

            def narrow(u, _):
                at = pl.ds(pl.multiple_of(u * length, LANES), length)
                done = dot(inv_wide_ref[:, : 2 * length], turned_ref[:, at], NN) + dot(
                    inv_wide_ref[:, 2 * length :], turned_ref[:length, at], NN
                )
                high, low = halves(done)
                unit = (u // 2) * (2 * kept) + 2 * j + u % 2
                target = pl.ds(pl.multiple_of(unit * rows, 16), rows)
                for p in range(groups):
                    for part, value in ((0, high), (1, low)):
                        back_ref[p, target, part * length : (part + 1) * length] = value[
                            p * rows : (p + 1) * rows, :
                        ]
                return 0

            lax.fori_loop(0, 6, narrow, 0)
            return 0

        lax.fori_loop(0, kept, one_depth, 0)

        def leave(p, _):
            done = dot(inv_line_ref[:, : 2 * length], back_ref[p], NT) + dot(
                inv_line_ref[:, 2 * length :], back_ref[p, :, :length], NT
            )
            pieces = [
                done[band * others * SUB : (band + 1) * others * SUB, :] for band in range(bands)
            ]
            if tiles * LANES > bands * width:
                pieces += [jnp.zeros((others * SUB, tiles * LANES - bands * width), f32)]
            line = jnp.concatenate(pieces, axis=1)
            for t in range(tiles):
                out_ref[p, :, t] = line[:, t * LANES : (t + 1) * LANES].reshape(others, SUB, LANES)
            return 0

        lax.fori_loop(0, groups, leave, 0)

    vmem = pl.BlockSpec(memory_space=pltpu.VMEM)
    flops = 6 * (4 * groups * width * G * length + 24 * kept * length * G * length)
    return pl.pallas_call(
        kernel,
        out_shape=jax.ShapeDtypeStruct(lines.shape, f32),
        in_specs=[pl.BlockSpec(memory_space=pltpu.SMEM)] + [vmem] * 7,
        out_specs=vmem,
        scratch_shapes=[
            pltpu.VMEM((kept, 2 * G, 6 * length), bf16),
            pltpu.VMEM((length, 6 * length), f32),
            pltpu.VMEM((2 * length, 6 * length), bf16),
            pltpu.VMEM((groups, width, 2 * length), bf16),
        ],
        cost_estimate=pl.CostEstimate(
            flops=flops, bytes_accessed=8 * lines.size, transcendentals=kept * G * G
        ),
        compiler_params=pltpu.CompilerParams(vmem_limit_bytes=PLANES_VMEM),
        name="planes",
    )(place, lines, *tables)


def halo(slabs):
    def shifted(piece, axis, up):
        devices = lax.axis_size(axis)
        pairs = [(i, i + 1) for i in range(devices - 1)]
        if not up:
            pairs = [(j, i) for i, j in pairs]
        return lax.ppermute(piece, axis, pairs)

    last_rows, first_rows, last_cols, first_cols = slabs
    return (
        shifted(last_rows, "px", True),
        shifted(first_rows, "px", False),
        shifted(last_cols, "py", True),
        shifted(first_cols, "py", False),
    )


def stretch(field, flow, halos, size):
    rows, cols, G = size.rows, size.cols, size.G
    width = 2 * G
    step = 16

    def kernel(field_ref, flow_ref, up_ref, down_ref, left_ref, right_ref, out_ref, ext_ref):
        for c in range(3):
            ext_ref[c, SUB : SUB + rows, 0:width] = left_ref[c]
            ext_ref[c, SUB : SUB + rows, width : width + cols * G] = flow_ref[c]
            ext_ref[c, SUB : SUB + rows, width + cols * G :] = right_ref[c]
            ext_ref[c, SUB - 2 : SUB, width : width + cols * G] = up_ref[c]
            ext_ref[c, SUB + rows : SUB + rows + 2, width : width + cols * G] = down_ref[c]
        depth = lax.broadcasted_iota(jnp.int32, (step, width), 1) % G
        inside = {s: (depth + s >= 0) & (depth + s < G) for s in (-2, -1, 1, 2)}

        def combine(p1, m1, p2, m2):
            return (8.0 * (p1 - m1) - (p2 - m2)) * (1.0 / 12.0)

        def block(b, _):
            at = pl.multiple_of(b * width, LANES)
            here_at = pl.multiple_of((b + 1) * width, LANES)
            for r in range(rows // step):
                fields = [field_ref[d, r * step : (r + 1) * step, pl.ds(at, width)] for d in range(3)]
                for c in range(3):
                    top = SUB + r * step
                    window = ext_ref[c, top : top + step, pl.ds(at, 3 * width)]
                    here = window[:, width : 2 * width]

                    def depth_shift(s):
                        return jnp.where(inside[s], pltpu.roll(here, (-s) % width, 1), 0.0)

                    def row_shift(s):
                        return ext_ref[c, top + s : top + s + step, pl.ds(here_at, width)]

                    total = fields[2] * combine(
                        depth_shift(1), depth_shift(-1), depth_shift(2), depth_shift(-2)
                    )
                    total += fields[1] * combine(
                        window[:, 3 * G : 5 * G],
                        window[:, G : 3 * G],
                        window[:, 4 * G :],
                        window[:, : 2 * G],
                    )
                    total += fields[0] * combine(
                        row_shift(1), row_shift(-1), row_shift(2), row_shift(-2)
                    )
                    out_ref[c, r * step : (r + 1) * step, pl.ds(at, width)] = total
            return 0

        lax.fori_loop(0, cols // 2, block, 0)

    return pl.pallas_call(
        kernel,
        out_shape=jax.ShapeDtypeStruct(flow.shape, f32),
        scratch_shapes=[pltpu.VMEM((3, rows + 2 * SUB, cols * G + 2 * width), f32)],
        cost_estimate=pl.CostEstimate(
            flops=60 * flow.size, bytes_accessed=12 * flow.size, transcendentals=0
        ),
        name="stretch",
    )(field, flow, *halos)


def triple(table, axis):
    high, low = split_table(table)
    return np.concatenate([high, high, low], axis=axis)


def fast(vorticity, size):
    rows, cols, G, devices, groups = size.rows, size.cols, size.G, size.devices, size.groups
    length, bands, others = size.length, size.bands, size.G // size.cols
    axes = ("px", "py")
    place = lax.axis_index(axes).astype(jnp.int32)

    cells = np.array([
        q * cols + band * SUB + s for band in range(bands) for q in range(others) for s in range(SUB)
    ])
    lane_modes, lane_kinds = lane_order(G)
    row_modes = np.concatenate([np.arange(G)] * 2)
    row_kinds = np.repeat([0, 1], G)
    line_basis = basis(G, lane_modes, lane_kinds, length)[cells]
    wide_basis = basis(G, row_modes, row_kinds, length)
    line = np.stack(split_table(line_basis))
    wide = triple(wide_basis.T, 1)
    inv_wide = triple(wide_basis * weights(row_modes, length), 1)
    inv_line = triple(line_basis * weights(lane_modes, length), 1)
    kx = np.broadcast_to(waves(np.arange(G), length)[:, None], (G, LANES)).astype(np.float32)
    signs = np.where(lane_kinds == 0, 1.0, -1.0)
    signs[: 2 * (G // LANES * LANES)] = 1.0
    ky = np.broadcast_to((waves(lane_modes, length) * signs)[None, :], (8, length)).astype(np.float32)
    tables = tuple(jnp.asarray(t) for t in (line, wide, inv_wide, inv_line, kx, ky))

    def depth_tables(start, kept):
        modes = np.array([
            (start + j) * devices + d
            for j in range(kept) for k in (0, 1) for d in range(devices)
        ])
        kinds = np.array([k for j in range(kept) for k in (0, 1) for d in range(devices)])
        table = basis(G, modes, kinds, length)
        forward = np.stack(split_table(table.T))
        inverse = np.stack(split_table((table * weights(modes, length)).T))
        return jnp.asarray(forward), jnp.asarray(inverse)

    def exchange(value, kept):
        value = value.reshape(devices, size.tiles(kept) * SUB, LANES)
        return lax.all_to_all(value, axes, split_axis=0, concat_axis=0, tiled=True)

    arrived = []
    for start, kept in size.chunks:
        sent = depth_forward(vorticity, depth_tables(start, kept)[0], size, kept)
        arrived.append(exchange(sent, kept))
    returned = []
    for (start, kept), lines in zip(size.chunks, arrived):
        lines = lines.reshape(groups, others, size.tiles(kept), SUB, LANES)
        where = jnp.stack([place, jnp.int32(start)])
        returned.append(exchange(planes(lines, where, tables, size, kept), kept))
    flow, slabs = None, None
    for (start, kept), lines in zip(size.chunks, returned):
        last = start + kept == G // devices
        flow, *slabs = depth_inverse(
            lines.reshape(-1, LANES), depth_tables(start, kept)[1], flow, size, kept, last
        )
    return flow, stretch(vorticity, flow, halo(slabs), size)


def with_halo(shard, sides, width):
    for axis, dim in sides:
        devices, length = (lax.axis_size(axis), shard.shape[dim])
        up = [(i, (i + 1) % devices) for i in range(devices - 1)]
        down = [(j, i) for i, j in up]
        last = lax.slice_in_dim(shard, length - width, length, axis=dim)
        leading = lax.slice_in_dim(shard, 0, width, axis=dim)
        before = lax.ppermute(last, axis, up)
        after = lax.ppermute(leading, axis, down)
        shard = jnp.concatenate([before, shard, after], axis=dim)
    return shard


def twiddle(count_in, count_out, length, factor):
    source = lax.broadcasted_iota(jnp.int32, (count_in, count_out), 0)
    target = lax.broadcasted_iota(jnp.int32, (count_in, count_out), 1)
    angle = (source * target % length).astype(jnp.float32) * (2.0 * math.pi / length)
    cosine = jnp.cos(angle) * factor
    sine = jnp.sin(angle) * factor
    return (
        jnp.broadcast_to(cosine, (3, count_in, count_out)),
        jnp.broadcast_to(sine, (3, count_in, count_out)),
    )


def product(einsum_form, first, second):
    return jnp.einsum(einsum_form, first, second, precision=highest)


def forward_left(pair, einsum_form, tables):
    real_part, imag_part = pair
    cosine_table, sine_table = tables
    return (
        product(einsum_form, cosine_table, real_part) + product(einsum_form, sine_table, imag_part),
        product(einsum_form, cosine_table, imag_part) - product(einsum_form, sine_table, real_part),
    )


def forward_right(pair, einsum_form, tables):
    real_part, imag_part = pair
    cosine_table, sine_table = tables
    return (
        product(einsum_form, real_part, cosine_table) + product(einsum_form, imag_part, sine_table),
        product(einsum_form, imag_part, cosine_table) - product(einsum_form, real_part, sine_table),
    )


def backward_left(pair, einsum_form, tables):
    real_part, imag_part = pair
    cosine_table, sine_table = tables
    return (
        product(einsum_form, cosine_table, real_part) - product(einsum_form, sine_table, imag_part),
        product(einsum_form, cosine_table, imag_part) + product(einsum_form, sine_table, real_part),
    )


def wavenumbers(start, count, length, position):
    index = start + lax.iota(jnp.int32, count)
    signed = jnp.where(index < length // 2, index, index - length)
    wave = signed.astype(jnp.float32) * (2.0 * math.pi / length)
    slope = jnp.where(index == length // 2, 0.0, wave)
    keep = jnp.where(index == length // 2, 0.0, 1.0)
    shape = [1, 1, 1, 1]
    shape[position] = count
    return (wave.reshape(shape), slope.reshape(shape), keep.reshape(shape))


def velocity_spectrum(pair, waves_x, waves_y, waves_z):
    square = waves_x[0] ** 2 + waves_y[0] ** 2 + waves_z[0] ** 2
    mask = waves_x[2] * waves_y[2] * waves_z[2]
    green = (
        mask
        * jnp.exp(-0.5 * smoothing * smoothing * square)
        / (square + jnp.where(square == 0.0, 1.0, 0.0))
    )
    slope_x, slope_y, slope_z = (waves_x[1][0], waves_y[1][0], waves_z[1][0])

    def curl(field):
        return jnp.stack(
            [
                slope_y * field[2] - slope_z * field[1],
                slope_z * field[0] - slope_x * field[2],
                slope_x * field[1] - slope_y * field[0],
            ]
        )

    real_part = pair[0] * green
    imag_part = pair[1] * green
    return (jnp.swapaxes(-curl(imag_part), 1, 2), jnp.swapaxes(curl(real_part), 1, 2))


def window(padded, axis, offset):
    starts = [0, 2, 2, 2]
    limits = [padded.shape[0], padded.shape[1] - 2, padded.shape[2] - 2, padded.shape[3] - 2]
    starts[axis] = starts[axis] + offset
    limits[axis] = limits[axis] + offset
    return lax.slice(padded, starts, limits)


def derivative(padded, axis):
    near = window(padded, axis, 1) - window(padded, axis, -1)
    far = window(padded, axis, 2) - window(padded, axis, -2)
    return (8.0 * near - far) / 12.0


def general(vorticity):
    block_rows = vorticity.shape[1]
    G = block_rows * lax.axis_size("px")
    block_cols = vorticity.shape[2] // G
    field = vorticity.reshape(3, block_rows, block_cols, G)
    length = 2 * G
    depth_tables = twiddle(G, G, length, 1.0)
    line_tables = twiddle(G, length, length, 1.0)
    inverse_tables = twiddle(length, G, length, 1.0 / length)
    closing = twiddle(G, G, length, 1.0 / length)
    weights = jnp.where(lax.iota(jnp.int32, G) == 0, 1.0, 2.0)[None, :, None]
    closing_cos = closing[0] * weights
    closing_sin = closing[1] * weights
    pair = (
        product("czk,cxyz->ckxy", depth_tables[0], field),
        -product("czk,cxyz->ckxy", depth_tables[1], field),
    )
    pair = (
        lax.all_to_all(pair[0], "py", split_axis=1, concat_axis=3, tiled=True),
        lax.all_to_all(pair[1], "py", split_axis=1, concat_axis=3, tiled=True),
    )
    pair = forward_left(pair, "cyl,ckxy->clkx", line_tables)
    pair = (
        lax.all_to_all(pair[0], "px", split_axis=1, concat_axis=3, tiled=True),
        lax.all_to_all(pair[1], "px", split_axis=1, concat_axis=3, tiled=True),
    )
    pair = forward_right(pair, "clkx,cxm->clkm", line_tables)
    rows = pair[0].shape[1]
    depth = pair[0].shape[2]
    waves_y = wavenumbers(lax.axis_index("px") * rows, rows, length, 1)
    waves_z = wavenumbers(lax.axis_index("py") * depth, depth, length, 2)
    waves_x = wavenumbers(0, length, length, 3)
    pair = velocity_spectrum(pair, waves_x, waves_y, waves_z)
    pair = backward_left(pair, "cmx,cklm->cxkl", inverse_tables)
    pair = (
        lax.all_to_all(pair[0], "px", split_axis=1, concat_axis=3, tiled=True),
        lax.all_to_all(pair[1], "px", split_axis=1, concat_axis=3, tiled=True),
    )
    pair = backward_left(pair, "cly,cxkl->cyxk", inverse_tables)
    pair = (
        lax.all_to_all(pair[0], "py", split_axis=1, concat_axis=3, tiled=True),
        lax.all_to_all(pair[1], "py", split_axis=1, concat_axis=3, tiled=True),
    )
    flow = product("cyxk,ckz->cyxz", pair[0], closing_cos) - product(
        "cyxk,ckz->cyxz", pair[1], closing_sin
    )
    flow = jnp.swapaxes(flow, 1, 2)
    padded = with_halo(flow, (("px", 1), ("py", 2)), 2)
    padded = jnp.pad(padded, ((0, 0), (0, 0), (0, 0), (2, 2)))
    stretching = (
        field[0] * derivative(padded, 1)
        + field[1] * derivative(padded, 2)
        + field[2] * derivative(padded, 3)
    )
    return (
        flow.reshape(3, block_rows, block_cols * G),
        stretching.reshape(3, block_rows, block_cols * G),
    )


def on_device(vorticity):
    sizes = fast_sizes(vorticity)
    return general(vorticity) if sizes is None else fast(vorticity, sizes)


def solution(mesh):
    in_specs = (P(None, "px", "py"),)
    out_specs = (P(None, "px", "py"), P(None, "px", "py"))
    return jax.shard_map(
        on_device, mesh=mesh, in_specs=in_specs, out_specs=out_specs, check_vma=False
    )
```

```python
import math

import jax
import jax.numpy as jnp
import numpy as np
from jax import lax
from jax.experimental import pallas as pl
from jax.experimental.pallas import tpu as pltpu
from jax.sharding import PartitionSpec as P


smoothing = 1.0
highest = lax.Precision.HIGHEST
f32 = jnp.float32
bf16 = jnp.bfloat16
LANES = 128
SUB = 8
PLANES_VMEM = 44 * 1024 * 1024


def split_table(table):
    high = table.astype(np.float32).astype(jnp.bfloat16)
    low = (table - high.astype(np.float64)).astype(np.float32).astype(jnp.bfloat16)
    return high, low


def waves(modes, length):
    return np.asarray(modes, np.float64) * (2.0 * math.pi / length)


def basis(points, modes, kinds, length):
    angle = (np.arange(points)[:, None] * np.asarray(modes)[None, :] % length) * (
        2.0 * math.pi / length
    )
    return np.where(np.asarray(kinds)[None, :] == 0, np.cos(angle), np.sin(angle))


def weights(modes, length):
    return np.where(np.asarray(modes) == 0, 1.0, 2.0) / length


def lane_order(modes):
    full = modes // LANES * LANES
    index, kind = [], []
    for start in range(0, full, LANES):
        for k in (0, 1):
            index += list(range(start, start + LANES))
            kind += [k] * LANES
    for k in (0, 1):
        index += list(range(full, modes))
        kind += [k] * (modes - full)
    return np.array(index), np.array(kind)


def dot(first, second, dims):
    return lax.dot_general(first, second, (dims, ((), ())), preferred_element_type=f32)


NN = ((1,), (0,))
NT = ((1,), (1,))


def halves(value):
    high = value.astype(bf16)
    low = (value - high.astype(f32)).astype(bf16)
    return high, low


class Sizes:
    def __init__(self, rows, cols, G, devices, groups):
        self.rows, self.cols, self.G = rows, cols, G
        self.devices, self.groups = devices, groups
        self.bands = cols // SUB
        self.length = 2 * G
        total = G // devices
        first = max(1, total // 3)
        self.chunks = [(0, first), (first, total - first)] if total > first else [(0, first)]

    def units(self, kept, count=3):
        return 2 * count * kept

    def tiles(self, kept, count=3):
        return -(-self.bands * self.units(kept, count) * self.rows // LANES)


def fast_sizes(vorticity):
    rows = vorticity.shape[1]
    groups = lax.axis_size("px")
    G = rows * groups
    cols = vorticity.shape[2] // G
    devices = groups * lax.axis_size("py")
    if rows % 16 or cols % (2 * SUB) not in (0, SUB) or cols % SUB or cols % 2:
        return None
    if G % devices or devices % SUB or G % LANES not in (0, LANES // 2):
        return None
    return Sizes(rows, cols, G, devices, groups)


def depth_forward(shard, table, size, kept):
    rows, cols, G, devices = size.rows, size.cols, size.G, size.devices
    units, tiles, bands = size.units(kept), size.tiles(kept), size.bands
    block = 2 * kept * devices
    used = bands * units * rows

    def kernel(shard_ref, table_ref, out_ref, high_ref, low_ref, mid_ref):
        def component(c, _):
            for y in range(cols):
                high, low = halves(shard_ref[c, :, y * G : (y + 1) * G])
                high_ref[y * rows : (y + 1) * rows, :] = high
                low_ref[y * rows : (y + 1) * rows, :] = low
            mid_ref[pl.ds(pl.multiple_of(c * block, SUB), block), :] = (
                dot(table_ref[0], high_ref[...], NT)
                + dot(table_ref[0], low_ref[...], NT)
                + dot(table_ref[1], high_ref[...], NT)
            )
            return 0

        lax.fori_loop(0, 3, component, 0)
        fill = [jnp.zeros((devices, tiles * LANES - used), f32)] if tiles * LANES > used else []
        for s in range(SUB):
            pieces = [
                mid_ref[
                    u * devices : (u + 1) * devices,
                    (SUB * band + s) * rows : (SUB * band + s + 1) * rows,
                ]
                for band in range(bands)
                for u in range(units)
            ]
            line = jnp.concatenate(pieces + fill, axis=1)
            for t in range(tiles):
                at = pl.ds(t * SUB + s, devices, stride=tiles * SUB)
                out_ref[at, :] = line[:, t * LANES : (t + 1) * LANES]

    return pl.pallas_call(
        kernel,
        out_shape=jax.ShapeDtypeStruct((devices * tiles * SUB, LANES), f32),
        scratch_shapes=[
            pltpu.VMEM((rows * cols, G), bf16),
            pltpu.VMEM((rows * cols, G), bf16),
            pltpu.VMEM((3 * block, rows * cols), f32),
        ],
        cost_estimate=pl.CostEstimate(
            flops=18 * block * G * rows * cols,
            bytes_accessed=4 * (3 * rows * cols * G + devices * tiles * SUB * LANES),
            transcendentals=0,
        ),
        name="depth_forward",
    )(shard, table)


def depth_inverse(lines, table, before, size, kept, parts, slabs):
    rows, cols, G, devices = size.rows, size.cols, size.G, size.devices
    start, count = parts
    units, tiles, bands = size.units(kept, count), size.tiles(kept, count), size.bands
    block = 2 * kept * devices
    own = pl.BlockSpec((count, rows, cols * G), lambda i: (start // count, 0, 0))
    whole = pl.BlockSpec(memory_space=pltpu.VMEM)
    extra = [] if before is None else [before]
    outs = [jax.ShapeDtypeStruct((3, rows, cols * G), f32)]
    if slabs:
        outs += [jax.ShapeDtypeStruct((count, 2, cols * G), f32)] * 2
        outs += [jax.ShapeDtypeStruct((count, rows, 2 * G), f32)] * 2
        outs += [jax.ShapeDtypeStruct((count, rows, cols * G), f32)]

    def kernel(lines_ref, table_ref, *refs):
        before_ref = refs[0] if before is not None else None
        out_ref, *slab_refs = refs[len(extra) : len(extra) + len(outs)]
        mid_ref, done_ref = refs[len(extra) + len(outs) :]
        for s in range(SUB):
            line = jnp.concatenate(
                [
                    lines_ref[pl.ds(t * SUB + s, devices, stride=tiles * SUB), :]
                    for t in range(tiles)
                ],
                axis=1,
            )
            for band in range(bands):
                y = SUB * band + s
                for u in range(units):
                    at = (band * units + u) * rows
                    mid_ref[u * devices : (u + 1) * devices, y * rows : (y + 1) * rows] = line[
                        :, at : at + rows
                    ]

        def component(c, _):
            high, low = halves(mid_ref[pl.ds(pl.multiple_of(c * block, SUB), block), :].T)
            done_ref[...] = (
                dot(high, table_ref[0], NN)
                + dot(low, table_ref[0], NN)
                + dot(high, table_ref[1], NN)
            )
            for y in range(0, cols, 2):
                pair = jnp.concatenate(
                    [
                        done_ref[y * rows : (y + 1) * rows, :],
                        done_ref[(y + 1) * rows : (y + 2) * rows, :],
                    ],
                    axis=1,
                )
                if before_ref is not None:
                    pair = pair + before_ref[c, :, y * G : (y + 2) * G]
                out_ref[c, :, y * G : (y + 2) * G] = pair
                if slabs:
                    slab_refs[0][c, :, y * G : (y + 2) * G] = pair[rows - 2 :, :]
                    slab_refs[1][c, :, y * G : (y + 2) * G] = pair[:2, :]
                    slab_refs[4][c, :, y * G : (y + 2) * G] = pair
                if slabs and y == cols - 2:
                    slab_refs[2][c] = pair
                if slabs and y == 0:
                    slab_refs[3][c] = pair
            return 0

        lax.fori_loop(0, count, component, 0)

    return pl.pallas_call(
        kernel,
        grid=(1,),
        out_shape=outs,
        in_specs=[whole, whole] + [own] * len(extra),
        out_specs=[own] + [whole] * (len(outs) - 1),
        input_output_aliases={2: 0} if extra else {},
        scratch_shapes=[
            pltpu.VMEM((count * block, rows * cols), f32),
            pltpu.VMEM((rows * cols, G), f32),
        ],
        cost_estimate=pl.CostEstimate(
            flops=6 * count * block * G * rows * cols,
            bytes_accessed=4 * (3 * count * rows * cols * G + devices * tiles * SUB * LANES),
            transcendentals=0,
        ),
        name="depth_inverse",
    )(lines, table, *extra)


def planes(lines, place, tables, size, kept, splits):
    rows, cols, G, devices, groups = size.rows, size.cols, size.G, size.devices, size.groups
    units, tiles, bands, length = size.units(kept), size.tiles(kept), size.bands, size.length
    width = units * rows
    step = 16
    unit_wave = 2.0 * math.pi / length
    full = G // LANES * LANES
    others = G // cols

    def kernel(place_ref, lines_ref, line_ref, wide_ref, inv_wide_ref, inv_line_ref,
               kx_ref, ky_ref, *refs):
        out_refs, (left_ref, spec_ref, turned_ref, back_ref) = refs[: len(splits)], refs[len(splits) :]

        def arrive(p, _):
            flat = jnp.concatenate(
                [lines_ref[p, :, t].reshape(others * SUB, LANES).T for t in range(tiles)], axis=0
            )
            side = jnp.concatenate(
                [flat[band * width : (band + 1) * width, :] for band in range(bands)], axis=1
            )
            high, low = halves(side)
            done = (
                dot(high, line_ref[0], NN) + dot(low, line_ref[0], NN) + dot(high, line_ref[1], NN)
            )
            for u in range(units):
                c, j, k = u // (2 * kept), u // 2 % kept, u % 2
                at = (2 * c + k) * length
                high, low = halves(done[u * rows : (u + 1) * rows, :])
                for part, value in ((0, high), (1, low)):
                    target = pl.ds(pl.multiple_of(part * G + p * rows, 16), rows)
                    left_ref[j, target, at : at + length] = value
            return 0

        lax.fori_loop(0, groups, arrive, 0)

        def one_depth(j, _):
            index = (place_ref[1] + j) * devices + place_ref[0]
            kz = index.astype(f32) * unit_wave

            def widen(u, _):
                at = pl.ds(pl.multiple_of(u * length, LANES), length)
                spec_ref[:, at] = dot(wide_ref[:, :length], left_ref[j, :, at], NN) + dot(
                    wide_ref[:, length:], left_ref[j, :G, at], NN
                )
                return 0

            lax.fori_loop(0, 6, widen, 0)

            def turn(r, _):
                top = pl.multiple_of(r * step, step)
                kx = kx_ref[pl.ds(top, step), :]

                def store(c, k, half, lane, value):
                    at = (2 * c + k) * length + lane
                    for part, piece in zip((0, 1), halves(value)):
                        target = pl.ds(pl.multiple_of(part * length + half * G + top, step), step)
                        turned_ref[target, at : at + LANES] = piece

                def green_of(lane):
                    ky = ky_ref[0:1, lane : lane + LANES]
                    square = kx * kx + ky * ky + kz * kz
                    return jnp.exp(-0.5 * smoothing * smoothing * square) / (
                        square + jnp.where(square == 0.0, 1.0, 0.0)
                    )

                def load(c, k, half, lane):
                    at = (2 * c + k) * length + lane
                    target = pl.ds(pl.multiple_of(half * G + top, step), step)
                    return spec_ref[target, at : at + LANES]

                def curl(lane_of, dy_of, green):
                    gx = green * kx
                    gz = green * kz
                    many = range(len(lane_of))
                    got = {
                        (c, k, h, t): load(c, k, h, lane_of[t])
                        for c in range(3) for k in (0, 1) for h in (0, 1) for t in many
                    }

                    def dx(c, k, h, t):
                        value = gx * got[c, k, 1 - h, t]
                        return value if h == 0 else -value

                    def dz(c, k, h, t):
                        value = gz * got[c, 1 - k, h, t]
                        return value if k == 0 else -value

                    def dy(c, k, h, t):
                        return dy_of(got, c, k, h, t)

                    for k in (0, 1):
                        for h in (0, 1):
                            for t in many:
                                store(0, k, h, lane_of[t], dy(2, k, h, t) - dz(1, k, h, t))
                                store(1, k, h, lane_of[t], dz(0, k, h, t) - dx(2, k, h, t))
                                store(2, k, h, lane_of[t], dx(1, k, h, t) - dy(0, k, h, t))

                for tile in range(full // LANES):
                    lane = 2 * tile * LANES
                    green = green_of(lane)
                    gy = green * ky_ref[0:1, lane : lane + LANES]

                    def dy_pair(got, c, k, h, t, gy=gy):
                        value = gy * got[c, k, h, 1 - t]
                        return value if t == 0 else -value

                    curl((lane, lane + LANES), dy_pair, green)
                if full < G:
                    lane = 2 * full
                    green = green_of(lane)
                    gy = green * ky_ref[0:1, lane : lane + LANES]

                    def dy_roll(got, c, k, h, t):
                        return gy * pltpu.roll(got[c, k, h, t], LANES // 2, 1)

                    curl((lane,), dy_roll, green)
                return 0

            lax.fori_loop(0, G // step, turn, 0)

            def narrow(u, _):
                at = pl.ds(pl.multiple_of(u * length, LANES), length)
                done = dot(inv_wide_ref[:, : 2 * length], turned_ref[:, at], NN) + dot(
                    inv_wide_ref[:, 2 * length :], turned_ref[:length, at], NN
                )
                high, low = halves(done)
                unit = (u // 2) * (2 * kept) + 2 * j + u % 2
                target = pl.ds(pl.multiple_of(unit * rows, 16), rows)
                for p in range(groups):
                    for part, value in ((0, high), (1, low)):
                        back_ref[p, target, part * length : (part + 1) * length] = value[
                            p * rows : (p + 1) * rows, :
                        ]
                return 0

            lax.fori_loop(0, 6, narrow, 0)
            return 0

        lax.fori_loop(0, kept, one_depth, 0)

        def leave(p, _):
            for out_ref, (start, count) in zip(out_refs, splits):
                many, span = size.tiles(kept, count), size.units(kept, count) * rows
                at = size.units(kept, start) * rows
                done = dot(
                    inv_line_ref[:, : 2 * length], back_ref[p, at : at + span, :], NT
                ) + dot(inv_line_ref[:, 2 * length :], back_ref[p, at : at + span, :length], NT)
                pieces = [
                    done[band * others * SUB : (band + 1) * others * SUB, :] for band in range(bands)
                ]
                if many * LANES > bands * span:
                    pieces += [jnp.zeros((others * SUB, many * LANES - bands * span), f32)]
                line = jnp.concatenate(pieces, axis=1)
                for t in range(many):
                    out_ref[p, :, t] = line[:, t * LANES : (t + 1) * LANES].reshape(
                        others, SUB, LANES
                    )
            return 0

        lax.fori_loop(0, groups, leave, 0)

    vmem = pl.BlockSpec(memory_space=pltpu.VMEM)
    flops = 6 * (4 * groups * width * G * length + 24 * kept * length * G * length)
    return pl.pallas_call(
        kernel,
        out_shape=[
            jax.ShapeDtypeStruct((groups, others, size.tiles(kept, count), SUB, LANES), f32)
            for _, count in splits
        ],
        in_specs=[pl.BlockSpec(memory_space=pltpu.SMEM)] + [vmem] * 7,
        out_specs=[vmem] * len(splits),
        scratch_shapes=[
            pltpu.VMEM((kept, 2 * G, 6 * length), bf16),
            pltpu.VMEM((length, 6 * length), f32),
            pltpu.VMEM((2 * length, 6 * length), bf16),
            pltpu.VMEM((groups, width, 2 * length), bf16),
        ],
        cost_estimate=pl.CostEstimate(
            flops=flops, bytes_accessed=8 * lines.size, transcendentals=kept * G * G
        ),
        compiler_params=pltpu.CompilerParams(vmem_limit_bytes=PLANES_VMEM),
        name="planes",
    )(place, lines, *tables)


def halo(slabs):
    def shifted(piece, axis, up):
        devices = lax.axis_size(axis)
        pairs = [(i, i + 1) for i in range(devices - 1)]
        if not up:
            pairs = [(j, i) for i, j in pairs]
        return lax.ppermute(piece, axis, pairs)

    last_rows, first_rows, last_cols, first_cols = slabs
    return (
        shifted(last_rows, "px", True),
        shifted(first_rows, "px", False),
        shifted(last_cols, "py", True),
        shifted(first_cols, "py", False),
    )


def depth_weights(G):
    width = 2 * G
    at = np.arange(width) % G
    out = np.zeros((width // LANES * 4, LANES), np.float32)
    for i, (shift, weight) in enumerate(((1, 8.0), (-1, -8.0), (2, -1.0), (-2, 1.0))):
        row = np.where((at + shift >= 0) & (at + shift < G), weight / 12.0, 0.0)
        for k in range(width // LANES):
            out[4 * k + i] = row[k * LANES : (k + 1) * LANES]
    return out


def stretch(field, flow, halos, before, size, parts):
    rows, cols, G = size.rows, size.cols, size.G
    start, count = parts
    span = 2 * G // LANES
    many = cols * G // LANES
    half = LANES // 2
    extra = [] if before is None else [before]

    def kernel(field_ref, flow_ref, up_ref, down_ref, left_ref, right_ref, weight_ref, *refs):
        out_ref, ext_ref, mix_ref = refs[len(extra) :]
        for t in range(many):
            at = slice(t * LANES, (t + 1) * LANES)
            ext_ref[span + t, SUB : SUB + rows, :] = flow_ref[0, :, at]
            ext_ref[span + t, SUB - 2 : SUB, :] = up_ref[0, :, at]
            ext_ref[span + t, SUB + rows : SUB + rows + 2, :] = down_ref[0, :, at]
        for t in range(span):
            at = slice(t * LANES, (t + 1) * LANES)
            ext_ref[t, SUB : SUB + rows, :] = left_ref[0, :, at]
            ext_ref[span + many + t, SUB : SUB + rows, :] = right_ref[0, :, at]
        lane = lax.broadcasted_iota(jnp.int32, (rows, LANES), 1)

        def mix(t, turned):
            after = pltpu.roll(ext_ref[t + 1, SUB : SUB + rows, :], half, 1)
            mix_ref[t] = jnp.where(lane < half, turned, after)
            return after

        lax.fori_loop(
            0, many + 2 * span - 1, mix, pltpu.roll(ext_ref[0, SUB : SUB + rows, :], half, 1)
        )

        def block(b, _):
            base = span * (b + 1)
            own = [ext_ref[base + k, SUB : SUB + rows, :] for k in range(span)]
            moved = {
                (k, s): pltpu.roll(own[k], (-s) % LANES, 1)
                for k in range(span)
                for s in (1, -1, 2, -2)
            }
            for k in range(span):
                deep = 0.0
                for i, s in enumerate((1, -1, 2, -2)):
                    value = moved[k, s]
                    if s > 0 and k + 1 < span:
                        value = jnp.where(lane < LANES - s, value, moved[k + 1, s])
                    if s < 0 and k > 0:
                        value = jnp.where(lane >= -s, value, moved[k - 1, s])
                    deep = deep + weight_ref[4 * k + i : 4 * k + i + 1, :] * value
                t = base + k
                side = 8.0 * (mix_ref[t + 1] - mix_ref[t - 2]) - (
                    ext_ref[t + span, SUB : SUB + rows, :] - ext_ref[t - span, SUB : SUB + rows, :]
                )
                tall = 8.0 * (
                    ext_ref[t, SUB + 1 : SUB + 1 + rows, :] - ext_ref[t, SUB - 1 : SUB - 1 + rows, :]
                ) - (ext_ref[t, SUB + 2 : SUB + 2 + rows, :] - ext_ref[t, SUB - 2 : SUB - 2 + rows, :])
                at = pl.ds(pl.multiple_of((span * b + k) * LANES, LANES), LANES)
                out_ref[0, :, at] = field_ref[2, :, at] * deep + (1.0 / 12.0) * (
                    field_ref[1, :, at] * side + field_ref[0, :, at] * tall
                )
            return 0

        lax.fori_loop(0, cols // 2, block, 0)

    def part(*shape):
        return pl.BlockSpec((1,) + shape, lambda i: (i, 0, 0))

    return pl.pallas_call(
        kernel,
        grid=(count,),
        out_shape=jax.ShapeDtypeStruct((3, rows, cols * G), f32),
        in_specs=[
            pl.BlockSpec((3, rows, cols * G), lambda i: (0, 0, 0)),
            part(rows, cols * G),
            part(2, cols * G),
            part(2, cols * G),
            part(rows, 2 * G),
            part(rows, 2 * G),
            pl.BlockSpec((4 * span, LANES), lambda i: (0, 0)),
        ]
        + [pl.BlockSpec(memory_space=pl.ANY)] * len(extra),
        out_specs=pl.BlockSpec((1, rows, cols * G), lambda i: (start + i, 0, 0)),
        input_output_aliases={7: 0} if extra else {},
        scratch_shapes=[
            pltpu.VMEM((many + 2 * span, rows + 2 * SUB, LANES), f32),
            pltpu.VMEM((many + 2 * span - 1, rows, LANES), f32),
        ],
        cost_estimate=pl.CostEstimate(
            flops=60 * flow.size,
            bytes_accessed=8 * flow.size + 4 * field.size,
            transcendentals=0,
        ),
        name="stretch",
    )(field, flow, *halos, jnp.asarray(depth_weights(G)), *extra)


def triple(table, axis):
    high, low = split_table(table)
    return np.concatenate([high, high, low], axis=axis)


def fast(vorticity, size):
    cols, G, devices, groups = size.cols, size.G, size.devices, size.groups
    length, bands, others = size.length, size.bands, size.G // size.cols
    axes = ("px", "py")
    place = lax.axis_index(axes).astype(jnp.int32)

    cells = np.array([
        q * cols + band * SUB + s for band in range(bands) for q in range(others) for s in range(SUB)
    ])
    lane_modes, lane_kinds = lane_order(G)
    row_modes = np.concatenate([np.arange(G)] * 2)
    row_kinds = np.repeat([0, 1], G)
    line_basis = basis(G, lane_modes, lane_kinds, length)[cells]
    wide_basis = basis(G, row_modes, row_kinds, length)
    line = np.stack(split_table(line_basis))
    wide = triple(wide_basis.T, 1)
    inv_wide = triple(wide_basis * weights(row_modes, length), 1)
    inv_line = triple(line_basis * weights(lane_modes, length), 1)
    kx = np.broadcast_to(waves(np.arange(G), length)[:, None], (G, LANES)).astype(np.float32)
    signs = np.where(lane_kinds == 0, 1.0, -1.0)
    signs[: 2 * (G // LANES * LANES)] = 1.0
    ky = np.broadcast_to((waves(lane_modes, length) * signs)[None, :], (8, length)).astype(np.float32)
    tables = tuple(jnp.asarray(t) for t in (line, wide, inv_wide, inv_line, kx, ky))

    def depth_tables(start, kept):
        modes = np.array([
            (start + j) * devices + d
            for j in range(kept) for _ in range(2) for d in range(devices)
        ])
        kinds = np.array([k for _ in range(kept) for k in (0, 1) for _ in range(devices)])
        table = basis(G, modes, kinds, length)
        forward = np.stack(split_table(table.T))
        inverse = np.stack(split_table((table * weights(modes, length)).T))
        return jnp.asarray(forward), jnp.asarray(inverse)

    def exchange(value):
        value = value.reshape(devices, -1, LANES)
        return lax.all_to_all(value, axes, split_axis=0, concat_axis=0, tiled=True)

    arrived = []
    for start, kept in size.chunks:
        arrived.append(exchange(depth_forward(vorticity, depth_tables(start, kept)[0], size, kept)))
    returned = []
    for (start, kept), lines in zip(size.chunks, arrived):
        last = start + kept == G // devices
        splits = ((0, 2), (2, 1)) if last else ((0, 3),)
        lines = lines.reshape(groups, others, size.tiles(kept), SUB, LANES)
        where = jnp.stack([place, jnp.int32(start)])
        for parts, done in zip(splits, planes(lines, where, tables, size, kept, splits)):
            done = exchange(done)
            returned.append((start, kept, parts, last, done))
    flow, stretching = None, None
    for start, kept, parts, last, lines in returned:
        flow, *slabs = depth_inverse(
            lines.reshape(-1, LANES), depth_tables(start, kept)[1], flow, size, kept, parts, last
        )
        if last:
            *slabs, own = slabs
            stretching = stretch(vorticity, own, halo(slabs), stretching, size, parts)
    return flow, stretching


def with_halo(shard, sides, width):
    for axis, dim in sides:
        devices, length = (lax.axis_size(axis), shard.shape[dim])
        up = [(i, (i + 1) % devices) for i in range(devices - 1)]
        down = [(j, i) for i, j in up]
        last = lax.slice_in_dim(shard, length - width, length, axis=dim)
        leading = lax.slice_in_dim(shard, 0, width, axis=dim)
        before = lax.ppermute(last, axis, up)
        after = lax.ppermute(leading, axis, down)
        shard = jnp.concatenate([before, shard, after], axis=dim)
    return shard


def twiddle(count_in, count_out, length, factor):
    source = lax.broadcasted_iota(jnp.int32, (count_in, count_out), 0)
    target = lax.broadcasted_iota(jnp.int32, (count_in, count_out), 1)
    angle = (source * target % length).astype(jnp.float32) * (2.0 * math.pi / length)
    cosine = jnp.cos(angle) * factor
    sine = jnp.sin(angle) * factor
    return (
        jnp.broadcast_to(cosine, (3, count_in, count_out)),
        jnp.broadcast_to(sine, (3, count_in, count_out)),
    )


def product(einsum_form, first, second):
    return jnp.einsum(einsum_form, first, second, precision=highest)


def forward_left(pair, einsum_form, tables):
    real_part, imag_part = pair
    cosine_table, sine_table = tables
    return (
        product(einsum_form, cosine_table, real_part) + product(einsum_form, sine_table, imag_part),
        product(einsum_form, cosine_table, imag_part) - product(einsum_form, sine_table, real_part),
    )


def forward_right(pair, einsum_form, tables):
    real_part, imag_part = pair
    cosine_table, sine_table = tables
    return (
        product(einsum_form, real_part, cosine_table) + product(einsum_form, imag_part, sine_table),
        product(einsum_form, imag_part, cosine_table) - product(einsum_form, real_part, sine_table),
    )


def backward_left(pair, einsum_form, tables):
    real_part, imag_part = pair
    cosine_table, sine_table = tables
    return (
        product(einsum_form, cosine_table, real_part) - product(einsum_form, sine_table, imag_part),
        product(einsum_form, cosine_table, imag_part) + product(einsum_form, sine_table, real_part),
    )


def wavenumbers(start, count, length, position):
    index = start + lax.iota(jnp.int32, count)
    signed = jnp.where(index < length // 2, index, index - length)
    wave = signed.astype(jnp.float32) * (2.0 * math.pi / length)
    slope = jnp.where(index == length // 2, 0.0, wave)
    keep = jnp.where(index == length // 2, 0.0, 1.0)
    shape = [1, 1, 1, 1]
    shape[position] = count
    return (wave.reshape(shape), slope.reshape(shape), keep.reshape(shape))


def velocity_spectrum(pair, waves_x, waves_y, waves_z):
    square = waves_x[0] ** 2 + waves_y[0] ** 2 + waves_z[0] ** 2
    mask = waves_x[2] * waves_y[2] * waves_z[2]
    green = (
        mask
        * jnp.exp(-0.5 * smoothing * smoothing * square)
        / (square + jnp.where(square == 0.0, 1.0, 0.0))
    )
    slope_x, slope_y, slope_z = (waves_x[1][0], waves_y[1][0], waves_z[1][0])

    def curl(field):
        return jnp.stack(
            [
                slope_y * field[2] - slope_z * field[1],
                slope_z * field[0] - slope_x * field[2],
                slope_x * field[1] - slope_y * field[0],
            ]
        )

    real_part = pair[0] * green
    imag_part = pair[1] * green
    return (jnp.swapaxes(-curl(imag_part), 1, 2), jnp.swapaxes(curl(real_part), 1, 2))


def window(padded, axis, offset):
    starts = [0, 2, 2, 2]
    limits = [padded.shape[0], padded.shape[1] - 2, padded.shape[2] - 2, padded.shape[3] - 2]
    starts[axis] = starts[axis] + offset
    limits[axis] = limits[axis] + offset
    return lax.slice(padded, starts, limits)


def derivative(padded, axis):
    near = window(padded, axis, 1) - window(padded, axis, -1)
    far = window(padded, axis, 2) - window(padded, axis, -2)
    return (8.0 * near - far) / 12.0


def general(vorticity):
    block_rows = vorticity.shape[1]
    G = block_rows * lax.axis_size("px")
    block_cols = vorticity.shape[2] // G
    field = vorticity.reshape(3, block_rows, block_cols, G)
    length = 2 * G
    depth_tables = twiddle(G, G, length, 1.0)
    line_tables = twiddle(G, length, length, 1.0)
    inverse_tables = twiddle(length, G, length, 1.0 / length)
    closing = twiddle(G, G, length, 1.0 / length)
    weights = jnp.where(lax.iota(jnp.int32, G) == 0, 1.0, 2.0)[None, :, None]
    closing_cos = closing[0] * weights
    closing_sin = closing[1] * weights
    pair = (
        product("czk,cxyz->ckxy", depth_tables[0], field),
        -product("czk,cxyz->ckxy", depth_tables[1], field),
    )
    pair = (
        lax.all_to_all(pair[0], "py", split_axis=1, concat_axis=3, tiled=True),
        lax.all_to_all(pair[1], "py", split_axis=1, concat_axis=3, tiled=True),
    )
    pair = forward_left(pair, "cyl,ckxy->clkx", line_tables)
    pair = (
        lax.all_to_all(pair[0], "px", split_axis=1, concat_axis=3, tiled=True),
        lax.all_to_all(pair[1], "px", split_axis=1, concat_axis=3, tiled=True),
    )
    pair = forward_right(pair, "clkx,cxm->clkm", line_tables)
    rows = pair[0].shape[1]
    depth = pair[0].shape[2]
    waves_y = wavenumbers(lax.axis_index("px") * rows, rows, length, 1)
    waves_z = wavenumbers(lax.axis_index("py") * depth, depth, length, 2)
    waves_x = wavenumbers(0, length, length, 3)
    pair = velocity_spectrum(pair, waves_x, waves_y, waves_z)
    pair = backward_left(pair, "cmx,cklm->cxkl", inverse_tables)
    pair = (
        lax.all_to_all(pair[0], "px", split_axis=1, concat_axis=3, tiled=True),
        lax.all_to_all(pair[1], "px", split_axis=1, concat_axis=3, tiled=True),
    )
    pair = backward_left(pair, "cly,cxkl->cyxk", inverse_tables)
    pair = (
        lax.all_to_all(pair[0], "py", split_axis=1, concat_axis=3, tiled=True),
        lax.all_to_all(pair[1], "py", split_axis=1, concat_axis=3, tiled=True),
    )
    flow = product("cyxk,ckz->cyxz", pair[0], closing_cos) - product(
        "cyxk,ckz->cyxz", pair[1], closing_sin
    )
    flow = jnp.swapaxes(flow, 1, 2)
    padded = with_halo(flow, (("px", 1), ("py", 2)), 2)
    padded = jnp.pad(padded, ((0, 0), (0, 0), (0, 0), (2, 2)))
    stretching = (
        field[0] * derivative(padded, 1)
        + field[1] * derivative(padded, 2)
        + field[2] * derivative(padded, 3)
    )
    return (
        flow.reshape(3, block_rows, block_cols * G),
        stretching.reshape(3, block_rows, block_cols * G),
    )


def on_device(vorticity):
    sizes = fast_sizes(vorticity)
    if sizes is None:
        return general(vorticity)
    return fast(vorticity, sizes)


def solution(mesh):
    in_specs = (P(None, "px", "py"),)
    out_specs = (P(None, "px", "py"), P(None, "px", "py"))
    return jax.shard_map(
        on_device, mesh=mesh, in_specs=in_specs, out_specs=out_specs, check_vma=False
    )
```

```python
import math

import jax
import jax.numpy as jnp
import numpy as np
from jax import lax
from jax.experimental import pallas as pl
from jax.experimental.pallas import tpu as pltpu
from jax.sharding import PartitionSpec as P


smoothing = 1.0
highest = lax.Precision.HIGHEST
f32 = jnp.float32
bf16 = jnp.bfloat16
LANES = 128
SUB = 8
ROWS = 16
PLANES_VMEM = 44 * 1024 * 1024


def split_table(table):
    high = table.astype(np.float32).astype(jnp.bfloat16)
    low = (table - high.astype(np.float64)).astype(np.float32).astype(jnp.bfloat16)
    return high, low


def waves(modes, length):
    return np.asarray(modes, np.float64) * (2.0 * math.pi / length)


def basis(points, modes, kinds, length):
    angle = (np.arange(points)[:, None] * np.asarray(modes)[None, :] % length) * (
        2.0 * math.pi / length
    )
    return np.where(np.asarray(kinds)[None, :] == 0, np.cos(angle), np.sin(angle))


def weights(modes, length):
    return np.where(np.asarray(modes) == 0, 1.0, 2.0) / length


def lane_order(modes):
    full = modes // LANES * LANES
    index, kind = [], []
    for start in range(0, full, LANES):
        for k in (0, 1):
            index += list(range(start, start + LANES))
            kind += [k] * LANES
    for k in (0, 1):
        index += list(range(full, modes))
        kind += [k] * (modes - full)
    return np.array(index), np.array(kind)


def dot(first, second, dims):
    return lax.dot_general(first, second, (dims, ((), ())), preferred_element_type=f32)


NN = ((1,), (0,))
NT = ((1,), (1,))


def halves(value):
    high = value.astype(bf16)
    low = (value - high.astype(f32)).astype(bf16)
    return high, low


class Sizes:
    def __init__(self, rows, cols, G, devices, groups):
        self.rows, self.cols, self.G = rows, cols, G
        self.devices, self.groups = devices, groups
        self.bands = cols // SUB
        self.length = 2 * G
        total = G // devices
        first = max(1, total // 3)
        self.chunks = [(0, first), (first, total - first)] if total > first else [(0, first)]

    def units(self, kept, count=3):
        return 2 * count * kept

    def tiles(self, kept, count=3):
        return -(-self.bands * self.units(kept, count) * self.rows // LANES)


def fast_sizes(vorticity):
    rows = vorticity.shape[1]
    groups = lax.axis_size("px")
    G = rows * groups
    cols = vorticity.shape[2] // G
    devices = groups * lax.axis_size("py")
    if rows % 16 or cols % (2 * SUB) not in (0, SUB) or cols % SUB or cols % 2:
        return None
    if G % devices or devices % SUB or G % LANES not in (0, LANES // 2):
        return None
    return Sizes(rows, cols, G, devices, groups)


def depth_forward(shard, table, size, kept):
    rows, cols, G, devices = size.rows, size.cols, size.G, size.devices
    units, tiles, bands = size.units(kept), size.tiles(kept), size.bands
    block = 2 * kept * devices
    used = bands * units * rows

    def kernel(shard_ref, table_ref, out_ref, high_ref, low_ref, mid_ref):
        def component(c, _):
            for y in range(cols):
                high, low = halves(shard_ref[c, :, y * G : (y + 1) * G])
                high_ref[y * rows : (y + 1) * rows, :] = high
                low_ref[y * rows : (y + 1) * rows, :] = low
            mid_ref[pl.ds(pl.multiple_of(c * block, SUB), block), :] = (
                dot(table_ref[0], high_ref[...], NT)
                + dot(table_ref[0], low_ref[...], NT)
                + dot(table_ref[1], high_ref[...], NT)
            )
            return 0

        lax.fori_loop(0, 3, component, 0)
        fill = [jnp.zeros((devices, tiles * LANES - used), f32)] if tiles * LANES > used else []
        for s in range(SUB):
            pieces = [
                mid_ref[
                    u * devices : (u + 1) * devices,
                    (SUB * band + s) * rows : (SUB * band + s + 1) * rows,
                ]
                for band in range(bands)
                for u in range(units)
            ]
            line = jnp.concatenate(pieces + fill, axis=1)
            for t in range(tiles):
                at = pl.ds(t * SUB + s, devices, stride=tiles * SUB)
                out_ref[at, :] = line[:, t * LANES : (t + 1) * LANES]

    return pl.pallas_call(
        kernel,
        out_shape=jax.ShapeDtypeStruct((devices * tiles * SUB, LANES), f32),
        scratch_shapes=[
            pltpu.VMEM((rows * cols, G), bf16),
            pltpu.VMEM((rows * cols, G), bf16),
            pltpu.VMEM((3 * block, rows * cols), f32),
        ],
        cost_estimate=pl.CostEstimate(
            flops=18 * block * G * rows * cols,
            bytes_accessed=4 * (3 * rows * cols * G + devices * tiles * SUB * LANES),
            transcendentals=0,
        ),
        name="depth_forward",
    )(shard, table)


def depth_inverse(lines, table, before, size, kept, parts, slabs):
    rows, cols, G, devices = size.rows, size.cols, size.G, size.devices
    start, count = parts
    units, tiles, bands = size.units(kept, count), size.tiles(kept, count), size.bands
    block = 2 * kept * devices
    own = pl.BlockSpec((count, rows, cols * G), lambda i: (start // count, 0, 0))
    whole = pl.BlockSpec(memory_space=pltpu.VMEM)
    extra = [] if before is None else [before]
    outs = [jax.ShapeDtypeStruct((3, rows, cols * G), f32)]
    if slabs:
        outs += [jax.ShapeDtypeStruct((count, 2, cols * G), f32)] * 2
        outs += [jax.ShapeDtypeStruct((count, rows, 2 * G), f32)] * 2
        outs += [jax.ShapeDtypeStruct((count, rows, cols * G), f32)]

    def kernel(lines_ref, table_ref, *refs):
        before_ref = refs[0] if before is not None else None
        out_ref, *slab_refs = refs[len(extra) : len(extra) + len(outs)]
        mid_ref, done_ref = refs[len(extra) + len(outs) :]
        for s in range(SUB):
            line = jnp.concatenate(
                [
                    lines_ref[pl.ds(t * SUB + s, devices, stride=tiles * SUB), :]
                    for t in range(tiles)
                ],
                axis=1,
            )
            for band in range(bands):
                y = SUB * band + s
                for u in range(units):
                    at = (band * units + u) * rows
                    mid_ref[u * devices : (u + 1) * devices, y * rows : (y + 1) * rows] = line[
                        :, at : at + rows
                    ]

        def component(c, _):
            high, low = halves(mid_ref[pl.ds(pl.multiple_of(c * block, SUB), block), :].T)
            done_ref[...] = (
                dot(high, table_ref[0], NN)
                + dot(low, table_ref[0], NN)
                + dot(high, table_ref[1], NN)
            )
            for y in range(0, cols, 2):
                pair = jnp.concatenate(
                    [
                        done_ref[y * rows : (y + 1) * rows, :],
                        done_ref[(y + 1) * rows : (y + 2) * rows, :],
                    ],
                    axis=1,
                )
                if before_ref is not None:
                    pair = pair + before_ref[c, :, y * G : (y + 2) * G]
                out_ref[c, :, y * G : (y + 2) * G] = pair
                if slabs:
                    slab_refs[0][c, :, y * G : (y + 2) * G] = pair[rows - 2 :, :]
                    slab_refs[1][c, :, y * G : (y + 2) * G] = pair[:2, :]
                    slab_refs[4][c, :, y * G : (y + 2) * G] = pair
                if slabs and y == cols - 2:
                    slab_refs[2][c] = pair
                if slabs and y == 0:
                    slab_refs[3][c] = pair
            return 0

        lax.fori_loop(0, count, component, 0)

    return pl.pallas_call(
        kernel,
        grid=(1,),
        out_shape=outs,
        in_specs=[whole, whole] + [own] * len(extra),
        out_specs=[own] + [whole] * (len(outs) - 1),
        input_output_aliases={2: 0} if extra else {},
        scratch_shapes=[
            pltpu.VMEM((count * block, rows * cols), f32),
            pltpu.VMEM((rows * cols, G), f32),
        ],
        cost_estimate=pl.CostEstimate(
            flops=6 * count * block * G * rows * cols,
            bytes_accessed=4 * (3 * count * rows * cols * G + devices * tiles * SUB * LANES),
            transcendentals=0,
        ),
        name="depth_inverse",
    )(lines, table, *extra)


def planes(lines, place, tables, size, kept, splits):
    rows, cols, G, devices, groups = size.rows, size.cols, size.G, size.devices, size.groups
    units, tiles, bands, length = size.units(kept), size.tiles(kept), size.bands, size.length
    width = units * rows
    step = 16
    unit_wave = 2.0 * math.pi / length
    full = G // LANES * LANES
    others = G // cols

    def kernel(place_ref, lines_ref, line_ref, wide_ref, inv_wide_ref, inv_line_ref,
               kx_ref, ky_ref, *refs):
        out_refs, (left_ref, spec_ref, turned_ref, back_ref) = refs[: len(splits)], refs[len(splits) :]

        def arrive(p, _):
            flat = jnp.concatenate(
                [lines_ref[p, :, t].reshape(others * SUB, LANES).T for t in range(tiles)], axis=0
            )
            side = jnp.concatenate(
                [flat[band * width : (band + 1) * width, :] for band in range(bands)], axis=1
            )
            high, low = halves(side)
            done = (
                dot(high, line_ref[0], NN) + dot(low, line_ref[0], NN) + dot(high, line_ref[1], NN)
            )
            for u in range(units):
                c, j, k = u // (2 * kept), u // 2 % kept, u % 2
                at = (2 * c + k) * length
                high, low = halves(done[u * rows : (u + 1) * rows, :])
                for part, value in ((0, high), (1, low)):
                    target = pl.ds(pl.multiple_of(part * G + p * rows, 16), rows)
                    left_ref[j, target, at : at + length] = value
            return 0

        lax.fori_loop(0, groups, arrive, 0)

        def one_depth(j, _):
            index = (place_ref[1] + j) * devices + place_ref[0]
            kz = index.astype(f32) * unit_wave

            def widen(u, _):
                at = pl.ds(pl.multiple_of(u * length, LANES), length)
                spec_ref[:, at] = dot(wide_ref[:, :length], left_ref[j, :, at], NN) + dot(
                    wide_ref[:, length:], left_ref[j, :G, at], NN
                )
                return 0

            lax.fori_loop(0, 6, widen, 0)

            def turn(r, _):
                top = pl.multiple_of(r * step, step)
                kx = kx_ref[pl.ds(top, step), :]

                def store(c, k, half, lane, value):
                    at = (2 * c + k) * length + lane
                    for part, piece in zip((0, 1), halves(value)):
                        target = pl.ds(pl.multiple_of(part * length + half * G + top, step), step)
                        turned_ref[target, at : at + LANES] = piece

                def green_of(lane):
                    ky = ky_ref[0:1, lane : lane + LANES]
                    square = kx * kx + ky * ky + kz * kz
                    return jnp.exp(-0.5 * smoothing * smoothing * square) / (
                        square + jnp.where(square == 0.0, 1.0, 0.0)
                    )

                def load(c, k, half, lane):
                    at = (2 * c + k) * length + lane
                    target = pl.ds(pl.multiple_of(half * G + top, step), step)
                    return spec_ref[target, at : at + LANES]

                def curl(lane_of, dy_of, green):
                    gx = green * kx
                    gz = green * kz
                    many = range(len(lane_of))
                    got = {
                        (c, k, h, t): load(c, k, h, lane_of[t])
                        for c in range(3) for k in (0, 1) for h in (0, 1) for t in many
                    }

                    def dx(c, k, h, t):
                        value = gx * got[c, k, 1 - h, t]
                        return value if h == 0 else -value

                    def dz(c, k, h, t):
                        value = gz * got[c, 1 - k, h, t]
                        return value if k == 0 else -value

                    def dy(c, k, h, t):
                        return dy_of(got, c, k, h, t)

                    for k in (0, 1):
                        for h in (0, 1):
                            for t in many:
                                store(0, k, h, lane_of[t], dy(2, k, h, t) - dz(1, k, h, t))
                                store(1, k, h, lane_of[t], dz(0, k, h, t) - dx(2, k, h, t))
                                store(2, k, h, lane_of[t], dx(1, k, h, t) - dy(0, k, h, t))

                for tile in range(full // LANES):
                    lane = 2 * tile * LANES
                    green = green_of(lane)
                    gy = green * ky_ref[0:1, lane : lane + LANES]

                    def dy_pair(got, c, k, h, t, gy=gy):
                        value = gy * got[c, k, h, 1 - t]
                        return value if t == 0 else -value

                    curl((lane, lane + LANES), dy_pair, green)
                if full < G:
                    lane = 2 * full
                    green = green_of(lane)
                    gy = green * ky_ref[0:1, lane : lane + LANES]

                    def dy_roll(got, c, k, h, t):
                        return gy * pltpu.roll(got[c, k, h, t], LANES // 2, 1)

                    curl((lane,), dy_roll, green)
                return 0

            lax.fori_loop(0, G // step, turn, 0)

            def narrow(u, _):
                at = pl.ds(pl.multiple_of(u * length, LANES), length)
                done = dot(inv_wide_ref[:, : 2 * length], turned_ref[:, at], NN) + dot(
                    inv_wide_ref[:, 2 * length :], turned_ref[:length, at], NN
                )
                high, low = halves(done)
                unit = (u // 2) * (2 * kept) + 2 * j + u % 2
                target = pl.ds(pl.multiple_of(unit * rows, 16), rows)
                for p in range(groups):
                    for part, value in ((0, high), (1, low)):
                        back_ref[p, target, part * length : (part + 1) * length] = value[
                            p * rows : (p + 1) * rows, :
                        ]
                return 0

            lax.fori_loop(0, 6, narrow, 0)
            return 0

        lax.fori_loop(0, kept, one_depth, 0)

        def leave(p, _):
            for out_ref, (start, count) in zip(out_refs, splits):
                many, span = size.tiles(kept, count), size.units(kept, count) * rows
                at = size.units(kept, start) * rows
                done = dot(
                    inv_line_ref[:, : 2 * length], back_ref[p, at : at + span, :], NT
                ) + dot(inv_line_ref[:, 2 * length :], back_ref[p, at : at + span, :length], NT)
                pieces = [
                    done[band * others * SUB : (band + 1) * others * SUB, :] for band in range(bands)
                ]
                if many * LANES > bands * span:
                    pieces += [jnp.zeros((others * SUB, many * LANES - bands * span), f32)]
                line = jnp.concatenate(pieces, axis=1)
                for t in range(many):
                    out_ref[p, :, t] = line[:, t * LANES : (t + 1) * LANES].reshape(
                        others, SUB, LANES
                    )
            return 0

        lax.fori_loop(0, groups, leave, 0)

    vmem = pl.BlockSpec(memory_space=pltpu.VMEM)
    flops = 6 * (4 * groups * width * G * length + 24 * kept * length * G * length)
    return pl.pallas_call(
        kernel,
        out_shape=[
            jax.ShapeDtypeStruct((groups, others, size.tiles(kept, count), SUB, LANES), f32)
            for _, count in splits
        ],
        in_specs=[pl.BlockSpec(memory_space=pltpu.SMEM)] + [vmem] * 7,
        out_specs=[vmem] * len(splits),
        scratch_shapes=[
            pltpu.VMEM((kept, 2 * G, 6 * length), bf16),
            pltpu.VMEM((length, 6 * length), f32),
            pltpu.VMEM((2 * length, 6 * length), bf16),
            pltpu.VMEM((groups, width, 2 * length), bf16),
        ],
        cost_estimate=pl.CostEstimate(
            flops=flops, bytes_accessed=8 * lines.size, transcendentals=kept * G * G
        ),
        compiler_params=pltpu.CompilerParams(vmem_limit_bytes=PLANES_VMEM),
        name="planes",
    )(place, lines, *tables)


def halo(slabs):
    def shifted(piece, axis, up):
        devices = lax.axis_size(axis)
        pairs = [(i, i + 1) for i in range(devices - 1)]
        if not up:
            pairs = [(j, i) for i, j in pairs]
        return lax.ppermute(piece, axis, pairs)

    last_rows, first_rows, last_cols, first_cols = slabs
    return (
        shifted(last_rows, "px", True),
        shifted(first_rows, "px", False),
        shifted(last_cols, "py", True),
        shifted(first_cols, "py", False),
    )


def depth_weights(G):
    width = 2 * G
    at = np.arange(width) % G
    rows = []
    for k in range(width // LANES):
        for shift, weight in ((1, 8.0), (-1, -8.0), (2, -1.0), (-2, 1.0)):
            inside = (at + shift >= 0) & (at + shift < G)
            rows.append(np.where(inside, weight / 12.0, 0.0)[k * LANES : (k + 1) * LANES])
    rows = np.stack(rows).astype(np.float32)
    return np.broadcast_to(rows[:, None, :], (len(rows), ROWS, LANES))


def stretch(field, flow, halos, before, size, parts):
    rows, cols, G = size.rows, size.cols, size.G
    start, count = parts
    span = 2 * G // LANES
    many = cols * G // LANES
    half = LANES // 2
    extra = [] if before is None else [before]

    def kernel(field_ref, flow_ref, up_ref, down_ref, left_ref, right_ref, weight_ref, *refs):
        out_ref, ext_ref, turned_ref = refs[len(extra) :]

        def put(t, value):
            ext_ref[t, SUB : SUB + rows, :] = value
            turned_ref[t] = pltpu.roll(value, half, 1)

        for t in range(many):
            at = slice(t * LANES, (t + 1) * LANES)
            put(span + t, flow_ref[0, :, at])
            ext_ref[span + t, SUB - 2 : SUB, :] = up_ref[0, :, at]
            ext_ref[span + t, SUB + rows : SUB + rows + 2, :] = down_ref[0, :, at]
        for t in range(span):
            at = slice(t * LANES, (t + 1) * LANES)
            put(t, left_ref[0, :, at])
            put(span + many + t, right_ref[0, :, at])
        lane = lax.broadcasted_iota(jnp.int32, (ROWS, LANES), 1)

        def block(b, _):
            base = span * (b + 1)
            for top in range(0, rows, ROWS):
                these = slice(top, top + ROWS)

                def tall_at(t, s):
                    return ext_ref[t, SUB + top + s : SUB + top + s + ROWS, :]

                def side_at(t):
                    return jnp.where(lane < half, turned_ref[t, these, :], turned_ref[t + 1, these, :])

                own = [tall_at(base + k, 0) for k in range(span)]
                for k in range(span):
                    t = base + k
                    deep = 0.0
                    for i, s in enumerate((1, -1, 2, -2)):
                        value = pltpu.roll(own[k], (-s) % LANES, 1)
                        if s > 0 and k + 1 < span:
                            value = jnp.where(
                                lane < LANES - s, value, pltpu.roll(own[k + 1], (-s) % LANES, 1)
                            )
                        if s < 0 and k > 0:
                            value = jnp.where(
                                lane >= -s, value, pltpu.roll(own[k - 1], (-s) % LANES, 1)
                            )
                        deep = deep + weight_ref[4 * k + i] * value
                    side = 8.0 * (side_at(t + 1) - side_at(t - 2)) - (
                        tall_at(t + span, 0) - tall_at(t - span, 0)
                    )
                    tall = 8.0 * (tall_at(t, 1) - tall_at(t, -1)) - (tall_at(t, 2) - tall_at(t, -2))
                    at = pl.ds(pl.multiple_of((span * b + k) * LANES, LANES), LANES)
                    out_ref[0, these, at] = field_ref[2, these, at] * deep + (1.0 / 12.0) * (
                        field_ref[1, these, at] * side + field_ref[0, these, at] * tall
                    )
            return 0

        lax.fori_loop(0, cols // 2, block, 0)

    def part(*shape):
        return pl.BlockSpec((1,) + shape, lambda i: (i, 0, 0))

    return pl.pallas_call(
        kernel,
        grid=(count,),
        out_shape=jax.ShapeDtypeStruct((3, rows, cols * G), f32),
        in_specs=[
            pl.BlockSpec((3, rows, cols * G), lambda i: (0, 0, 0)),
            part(rows, cols * G),
            part(2, cols * G),
            part(2, cols * G),
            part(rows, 2 * G),
            part(rows, 2 * G),
            pl.BlockSpec((4 * span, ROWS, LANES), lambda i: (0, 0, 0)),
        ]
        + [pl.BlockSpec(memory_space=pl.ANY)] * len(extra),
        out_specs=pl.BlockSpec((1, rows, cols * G), lambda i: (start + i, 0, 0)),
        input_output_aliases={7: 0} if extra else {},
        scratch_shapes=[
            pltpu.VMEM((many + 2 * span, rows + 2 * SUB, LANES), f32),
            pltpu.VMEM((many + 2 * span, rows, LANES), f32),
        ],
        cost_estimate=pl.CostEstimate(
            flops=60 * flow.size,
            bytes_accessed=8 * flow.size + 4 * field.size,
            transcendentals=0,
        ),
        name="stretch",
    )(field, flow, *halos, jnp.asarray(depth_weights(G)), *extra)


def triple(table, axis):
    high, low = split_table(table)
    return np.concatenate([high, high, low], axis=axis)


def fast(vorticity, size):
    cols, G, devices, groups = size.cols, size.G, size.devices, size.groups
    length, bands, others = size.length, size.bands, size.G // size.cols
    axes = ("px", "py")
    place = lax.axis_index(axes).astype(jnp.int32)

    cells = np.array([
        q * cols + band * SUB + s for band in range(bands) for q in range(others) for s in range(SUB)
    ])
    lane_modes, lane_kinds = lane_order(G)
    row_modes = np.concatenate([np.arange(G)] * 2)
    row_kinds = np.repeat([0, 1], G)
    line_basis = basis(G, lane_modes, lane_kinds, length)[cells]
    wide_basis = basis(G, row_modes, row_kinds, length)
    line = np.stack(split_table(line_basis))
    wide = triple(wide_basis.T, 1)
    inv_wide = triple(wide_basis * weights(row_modes, length), 1)
    inv_line = triple(line_basis * weights(lane_modes, length), 1)
    kx = np.broadcast_to(waves(np.arange(G), length)[:, None], (G, LANES)).astype(np.float32)
    signs = np.where(lane_kinds == 0, 1.0, -1.0)
    signs[: 2 * (G // LANES * LANES)] = 1.0
    ky = np.broadcast_to((waves(lane_modes, length) * signs)[None, :], (8, length)).astype(np.float32)
    tables = tuple(jnp.asarray(t) for t in (line, wide, inv_wide, inv_line, kx, ky))

    def depth_tables(start, kept):
        modes = np.array([
            (start + j) * devices + d
            for j in range(kept) for _ in range(2) for d in range(devices)
        ])
        kinds = np.array([k for _ in range(kept) for k in (0, 1) for _ in range(devices)])
        table = basis(G, modes, kinds, length)
        forward = np.stack(split_table(table.T))
        inverse = np.stack(split_table((table * weights(modes, length)).T))
        return jnp.asarray(forward), jnp.asarray(inverse)

    def exchange(value):
        value = value.reshape(devices, -1, LANES)
        return lax.all_to_all(value, axes, split_axis=0, concat_axis=0, tiled=True)

    arrived = []
    for start, kept in size.chunks:
        arrived.append(exchange(depth_forward(vorticity, depth_tables(start, kept)[0], size, kept)))
    returned = []
    for (start, kept), lines in zip(size.chunks, arrived):
        last = start + kept == G // devices
        splits = ((0, 2), (2, 1)) if last else ((0, 3),)
        lines = lines.reshape(groups, others, size.tiles(kept), SUB, LANES)
        where = jnp.stack([place, jnp.int32(start)])
        for parts, done in zip(splits, planes(lines, where, tables, size, kept, splits)):
            done = exchange(done)
            returned.append((start, kept, parts, last, done))
    flow, stretching = None, None
    for start, kept, parts, last, lines in returned:
        flow, *slabs = depth_inverse(
            lines.reshape(-1, LANES), depth_tables(start, kept)[1], flow, size, kept, parts, last
        )
        if last:
            *slabs, own = slabs
            stretching = stretch(vorticity, own, halo(slabs), stretching, size, parts)
    return flow, stretching


def with_halo(shard, sides, width):
    for axis, dim in sides:
        devices, length = (lax.axis_size(axis), shard.shape[dim])
        up = [(i, (i + 1) % devices) for i in range(devices - 1)]
        down = [(j, i) for i, j in up]
        last = lax.slice_in_dim(shard, length - width, length, axis=dim)
        leading = lax.slice_in_dim(shard, 0, width, axis=dim)
        before = lax.ppermute(last, axis, up)
        after = lax.ppermute(leading, axis, down)
        shard = jnp.concatenate([before, shard, after], axis=dim)
    return shard


def twiddle(count_in, count_out, length, factor):
    source = lax.broadcasted_iota(jnp.int32, (count_in, count_out), 0)
    target = lax.broadcasted_iota(jnp.int32, (count_in, count_out), 1)
    angle = (source * target % length).astype(jnp.float32) * (2.0 * math.pi / length)
    cosine = jnp.cos(angle) * factor
    sine = jnp.sin(angle) * factor
    return (
        jnp.broadcast_to(cosine, (3, count_in, count_out)),
        jnp.broadcast_to(sine, (3, count_in, count_out)),
    )


def product(einsum_form, first, second):
    return jnp.einsum(einsum_form, first, second, precision=highest)


def forward_left(pair, einsum_form, tables):
    real_part, imag_part = pair
    cosine_table, sine_table = tables
    return (
        product(einsum_form, cosine_table, real_part) + product(einsum_form, sine_table, imag_part),
        product(einsum_form, cosine_table, imag_part) - product(einsum_form, sine_table, real_part),
    )


def forward_right(pair, einsum_form, tables):
    real_part, imag_part = pair
    cosine_table, sine_table = tables
    return (
        product(einsum_form, real_part, cosine_table) + product(einsum_form, imag_part, sine_table),
        product(einsum_form, imag_part, cosine_table) - product(einsum_form, real_part, sine_table),
    )


def backward_left(pair, einsum_form, tables):
    real_part, imag_part = pair
    cosine_table, sine_table = tables
    return (
        product(einsum_form, cosine_table, real_part) - product(einsum_form, sine_table, imag_part),
        product(einsum_form, cosine_table, imag_part) + product(einsum_form, sine_table, real_part),
    )


def wavenumbers(start, count, length, position):
    index = start + lax.iota(jnp.int32, count)
    signed = jnp.where(index < length // 2, index, index - length)
    wave = signed.astype(jnp.float32) * (2.0 * math.pi / length)
    slope = jnp.where(index == length // 2, 0.0, wave)
    keep = jnp.where(index == length // 2, 0.0, 1.0)
    shape = [1, 1, 1, 1]
    shape[position] = count
    return (wave.reshape(shape), slope.reshape(shape), keep.reshape(shape))


def velocity_spectrum(pair, waves_x, waves_y, waves_z):
    square = waves_x[0] ** 2 + waves_y[0] ** 2 + waves_z[0] ** 2
    mask = waves_x[2] * waves_y[2] * waves_z[2]
    green = (
        mask
        * jnp.exp(-0.5 * smoothing * smoothing * square)
        / (square + jnp.where(square == 0.0, 1.0, 0.0))
    )
    slope_x, slope_y, slope_z = (waves_x[1][0], waves_y[1][0], waves_z[1][0])

    def curl(field):
        return jnp.stack(
            [
                slope_y * field[2] - slope_z * field[1],
                slope_z * field[0] - slope_x * field[2],
                slope_x * field[1] - slope_y * field[0],
            ]
        )

    real_part = pair[0] * green
    imag_part = pair[1] * green
    return (jnp.swapaxes(-curl(imag_part), 1, 2), jnp.swapaxes(curl(real_part), 1, 2))


def window(padded, axis, offset):
    starts = [0, 2, 2, 2]
    limits = [padded.shape[0], padded.shape[1] - 2, padded.shape[2] - 2, padded.shape[3] - 2]
    starts[axis] = starts[axis] + offset
    limits[axis] = limits[axis] + offset
    return lax.slice(padded, starts, limits)


def derivative(padded, axis):
    near = window(padded, axis, 1) - window(padded, axis, -1)
    far = window(padded, axis, 2) - window(padded, axis, -2)
    return (8.0 * near - far) / 12.0


def general(vorticity):
    block_rows = vorticity.shape[1]
    G = block_rows * lax.axis_size("px")
    block_cols = vorticity.shape[2] // G
    field = vorticity.reshape(3, block_rows, block_cols, G)
    length = 2 * G
    depth_tables = twiddle(G, G, length, 1.0)
    line_tables = twiddle(G, length, length, 1.0)
    inverse_tables = twiddle(length, G, length, 1.0 / length)
    closing = twiddle(G, G, length, 1.0 / length)
    weights = jnp.where(lax.iota(jnp.int32, G) == 0, 1.0, 2.0)[None, :, None]
    closing_cos = closing[0] * weights
    closing_sin = closing[1] * weights
    pair = (
        product("czk,cxyz->ckxy", depth_tables[0], field),
        -product("czk,cxyz->ckxy", depth_tables[1], field),
    )
    pair = (
        lax.all_to_all(pair[0], "py", split_axis=1, concat_axis=3, tiled=True),
        lax.all_to_all(pair[1], "py", split_axis=1, concat_axis=3, tiled=True),
    )
    pair = forward_left(pair, "cyl,ckxy->clkx", line_tables)
    pair = (
        lax.all_to_all(pair[0], "px", split_axis=1, concat_axis=3, tiled=True),
        lax.all_to_all(pair[1], "px", split_axis=1, concat_axis=3, tiled=True),
    )
    pair = forward_right(pair, "clkx,cxm->clkm", line_tables)
    rows = pair[0].shape[1]
    depth = pair[0].shape[2]
    waves_y = wavenumbers(lax.axis_index("px") * rows, rows, length, 1)
    waves_z = wavenumbers(lax.axis_index("py") * depth, depth, length, 2)
    waves_x = wavenumbers(0, length, length, 3)
    pair = velocity_spectrum(pair, waves_x, waves_y, waves_z)
    pair = backward_left(pair, "cmx,cklm->cxkl", inverse_tables)
    pair = (
        lax.all_to_all(pair[0], "px", split_axis=1, concat_axis=3, tiled=True),
        lax.all_to_all(pair[1], "px", split_axis=1, concat_axis=3, tiled=True),
    )
    pair = backward_left(pair, "cly,cxkl->cyxk", inverse_tables)
    pair = (
        lax.all_to_all(pair[0], "py", split_axis=1, concat_axis=3, tiled=True),
        lax.all_to_all(pair[1], "py", split_axis=1, concat_axis=3, tiled=True),
    )
    flow = product("cyxk,ckz->cyxz", pair[0], closing_cos) - product(
        "cyxk,ckz->cyxz", pair[1], closing_sin
    )
    flow = jnp.swapaxes(flow, 1, 2)
    padded = with_halo(flow, (("px", 1), ("py", 2)), 2)
    padded = jnp.pad(padded, ((0, 0), (0, 0), (0, 0), (2, 2)))
    stretching = (
        field[0] * derivative(padded, 1)
        + field[1] * derivative(padded, 2)
        + field[2] * derivative(padded, 3)
    )
    return (
        flow.reshape(3, block_rows, block_cols * G),
        stretching.reshape(3, block_rows, block_cols * G),
    )


def on_device(vorticity):
    sizes = fast_sizes(vorticity)
    if sizes is None:
        return general(vorticity)
    return fast(vorticity, sizes)


def solution(mesh):
    in_specs = (P(None, "px", "py"),)
    out_specs = (P(None, "px", "py"), P(None, "px", "py"))
    return jax.shard_map(
        on_device, mesh=mesh, in_specs=in_specs, out_specs=out_specs, check_vma=False
    )
```

```python
import math

import jax
import jax.numpy as jnp
import numpy as np
from jax import lax
from jax.experimental import pallas as pl
from jax.experimental.pallas import tpu as pltpu
from jax.sharding import PartitionSpec as P


smoothing = 1.0
highest = lax.Precision.HIGHEST
f32 = jnp.float32
bf16 = jnp.bfloat16
LANES = 128
SUB = 8
ROWS = 16
ALL_VMEM, MOST_VMEM = 67_000_000, 24_000_000


def split_table(table):
    high = table.astype(np.float32).astype(jnp.bfloat16)
    low = (table - high.astype(np.float64)).astype(np.float32).astype(jnp.bfloat16)
    return high, low


def waves(modes, length):
    return np.asarray(modes, np.float64) * (2.0 * math.pi / length)


def basis(points, modes, kinds, length):
    angle = (np.arange(points)[:, None] * np.asarray(modes)[None, :] % length) * (
        2.0 * math.pi / length
    )
    return np.where(np.asarray(kinds)[None, :] == 0, np.cos(angle), np.sin(angle))


def weights(modes, length):
    return np.where(np.asarray(modes) == 0, 1.0, 2.0) / length


def lane_order(modes):
    full = modes // LANES * LANES
    index, kind = [], []
    for start in range(0, full, LANES):
        for k in (0, 1):
            index += list(range(start, start + LANES))
            kind += [k] * LANES
    for k in (0, 1):
        index += list(range(full, modes))
        kind += [k] * (modes - full)
    return np.array(index), np.array(kind)


def dot(first, second, dims):
    return lax.dot_general(first, second, (dims, ((), ())), preferred_element_type=f32)


NN = ((1,), (0,))
NT = ((1,), (1,))
TN = ((0,), (0,))


def halves(value):
    high = value.astype(bf16)
    low = (value - high.astype(f32)).astype(bf16)
    return high, low


class Sizes:
    def __init__(self, rows, cols, G, devices, groups):
        self.rows, self.cols, self.G = rows, cols, G
        self.devices, self.groups = devices, groups
        self.bands = cols // SUB
        self.length = 2 * G
        total = G // devices
        first = max(1, total // 3)
        self.chunks = [(0, first), (first, total - first)] if total > first else [(0, first)]

    def units(self, kept):
        return 6 * kept

    def tiles(self, kept):
        return -(-self.bands * self.units(kept) * self.rows // LANES)


def fast_sizes(vorticity):
    rows = vorticity.shape[1]
    groups = lax.axis_size("px")
    G = rows * groups
    cols = vorticity.shape[2] // G
    devices = groups * lax.axis_size("py")
    if rows % 16 or cols % (2 * SUB) not in (0, SUB) or cols % SUB or cols % 2:
        return None
    if G % devices or devices % SUB or G % LANES not in (0, LANES // 2):
        return None
    return Sizes(rows, cols, G, devices, groups)


def depth_forward(shard, table, size, kept):
    rows, cols, G, devices = size.rows, size.cols, size.G, size.devices
    units, tiles, bands = size.units(kept), size.tiles(kept), size.bands
    block = 2 * kept * devices
    used = bands * units * rows

    def kernel(shard_ref, table_ref, out_ref, held_ref, sems, high_ref, low_ref, mid_ref):
        def fetch(c):
            return pltpu.make_async_copy(shard_ref.at[c], held_ref.at[c], sems.at[c])

        for c in range(3):
            fetch(c).start()

        def component(c, _):
            fetch(c).wait()
            for y in range(cols):
                high, low = halves(held_ref[c, :, y * G : (y + 1) * G])
                high_ref[y * rows : (y + 1) * rows, :] = high
                low_ref[y * rows : (y + 1) * rows, :] = low
            mid_ref[pl.ds(pl.multiple_of(c * block, SUB), block), :] = (
                dot(table_ref[0], high_ref[...], NT)
                + dot(table_ref[0], low_ref[...], NT)
                + dot(table_ref[1], high_ref[...], NT)
            )
            return 0

        lax.fori_loop(0, 3, component, 0)
        fill = [jnp.zeros((devices, tiles * LANES - used), f32)] if tiles * LANES > used else []
        for s in range(SUB):
            pieces = [
                mid_ref[
                    u * devices : (u + 1) * devices,
                    (SUB * band + s) * rows : (SUB * band + s + 1) * rows,
                ]
                for band in range(bands)
                for u in range(units)
            ]
            line = jnp.concatenate(pieces + fill, axis=1)
            for t in range(tiles):
                at = pl.ds(t * SUB + s, devices, stride=tiles * SUB)
                out_ref[at, :] = line[:, t * LANES : (t + 1) * LANES]

    return pl.pallas_call(
        kernel,
        out_shape=jax.ShapeDtypeStruct((devices * tiles * SUB, LANES), f32),
        in_specs=[pl.BlockSpec(memory_space=pltpu.HBM), pl.BlockSpec(memory_space=pltpu.VMEM)],
        out_specs=pl.BlockSpec(memory_space=pltpu.VMEM),
        scratch_shapes=[
            pltpu.VMEM((3, rows, cols * G), f32),
            pltpu.SemaphoreType.DMA((3,)),
            pltpu.VMEM((rows * cols, G), bf16),
            pltpu.VMEM((rows * cols, G), bf16),
            pltpu.VMEM((3 * block, rows * cols), f32),
        ],
        cost_estimate=pl.CostEstimate(
            flops=18 * block * G * rows * cols,
            bytes_accessed=4 * (3 * rows * cols * G + devices * tiles * SUB * LANES),
            transcendentals=0,
        ),
        compiler_params=pltpu.CompilerParams(vmem_limit_bytes=ALL_VMEM),
        name="depth_forward",
    )(shard, table)


def depth_inverse(lines, table, before, size, kept, slabs):
    rows, cols, G, devices = size.rows, size.cols, size.G, size.devices
    units, tiles, bands = size.units(kept), size.tiles(kept), size.bands
    block = 2 * kept * devices
    share = SUB * tiles * SUB
    extra = [] if before is None else [before]
    anywhere = pl.BlockSpec(memory_space=pltpu.HBM)
    whole = pl.BlockSpec(memory_space=pltpu.VMEM)
    outs = [jax.ShapeDtypeStruct((3, rows, cols * G), f32)]
    if slabs:
        outs += [jax.ShapeDtypeStruct((3, 2, cols * G), f32)] * 2
        outs += [jax.ShapeDtypeStruct((3, rows, 2 * G), f32)] * 2

    def kernel(lines_ref, table_ref, *refs):
        out_ref, *slab_refs = refs[len(extra) : len(extra) + len(outs)]
        held_ref, ready_ref, mid_ref, done_ref, came, had, gone = refs[len(extra) + len(outs) :]

        def arrive(g):
            at = pl.ds(g * share, share)
            return pltpu.make_async_copy(lines_ref.at[at], held_ref.at[at], came.at[g])

        def earlier(c):
            return pltpu.make_async_copy(refs[0].at[c], ready_ref.at[c], had.at[c])

        def leave(c):
            return pltpu.make_async_copy(ready_ref.at[c], out_ref.at[c], gone.at[c])

        for g in range(devices // SUB):
            arrive(g).start()
        if extra:
            for c in range(3):
                earlier(c).start()
        for g in range(devices // SUB):
            arrive(g).wait()
            for s in range(SUB):
                line = jnp.concatenate(
                    [
                        held_ref[pl.ds(g * share + t * SUB + s, SUB, stride=tiles * SUB), :]
                        for t in range(tiles)
                    ],
                    axis=1,
                )
                for band in range(bands):
                    y = SUB * band + s
                    for u in range(units):
                        at = (band * units + u) * rows
                        to = u * devices + g * SUB
                        mid_ref[to : to + SUB, y * rows : (y + 1) * rows] = line[:, at : at + rows]

        def component(c, _):
            high, low = halves(mid_ref[pl.ds(pl.multiple_of(c * block, SUB), block), :].T)
            if 2 * block <= 2 * LANES:
                done_ref[...] = dot(
                    jnp.concatenate([high, low], axis=1),
                    jnp.concatenate([table_ref[0], table_ref[0]], axis=0),
                    NN,
                ) + dot(high, table_ref[1], NN)
            else:
                done_ref[...] = (
                    dot(high, table_ref[0], NN)
                    + dot(low, table_ref[0], NN)
                    + dot(high, table_ref[1], NN)
                )
            if extra:
                earlier(c).wait()
            for y in range(0, cols, 2):
                pair = jnp.concatenate(
                    [
                        done_ref[y * rows : (y + 1) * rows, :],
                        done_ref[(y + 1) * rows : (y + 2) * rows, :],
                    ],
                    axis=1,
                )
                if extra:
                    pair = pair + ready_ref[c, :, y * G : (y + 2) * G]
                ready_ref[c, :, y * G : (y + 2) * G] = pair
                if slabs:
                    slab_refs[0][c, :, y * G : (y + 2) * G] = pair[rows - 2 :, :]
                    slab_refs[1][c, :, y * G : (y + 2) * G] = pair[:2, :]
                if slabs and y == cols - 2:
                    slab_refs[2][c] = pair
                if slabs and y == 0:
                    slab_refs[3][c] = pair
            leave(c).start()
            return 0

        lax.fori_loop(0, 3, component, 0)
        for c in range(3):
            leave(c).wait()

    return pl.pallas_call(
        kernel,
        out_shape=outs,
        in_specs=[anywhere, whole] + [anywhere] * len(extra),
        out_specs=[anywhere] + [whole] * (len(outs) - 1),
        scratch_shapes=[
            pltpu.VMEM((devices * tiles * SUB, LANES), f32),
            pltpu.VMEM((3, rows, cols * G), f32),
            pltpu.VMEM((3 * block, rows * cols), f32),
            pltpu.VMEM((rows * cols, G), f32),
            pltpu.SemaphoreType.DMA((devices // SUB,)),
            pltpu.SemaphoreType.DMA((3,)),
            pltpu.SemaphoreType.DMA((3,)),
        ],
        cost_estimate=pl.CostEstimate(
            flops=18 * block * G * rows * cols,
            bytes_accessed=4 * (9 * rows * cols * G + devices * tiles * SUB * LANES),
            transcendentals=0,
        ),
        compiler_params=pltpu.CompilerParams(vmem_limit_bytes=ALL_VMEM),
        name="depth_inverse",
    )(lines, table, *extra)


def planes(lines, place, tables, size, kept):
    rows, cols, G, devices, groups = size.rows, size.cols, size.G, size.devices, size.groups
    units, tiles, bands, length = size.units(kept), size.tiles(kept), size.bands, size.length
    width = units * rows
    step = 16
    unit_wave = 2.0 * math.pi / length
    full = G // LANES * LANES
    others = G // cols

    def kernel(place_ref, lines_ref, narrow_hbm, wide_hbm, waves_hbm, out_ref, held_ref, narrow_ref,
               wide_ref, waves_ref, came, told, left_ref, spec_ref, turned_ref, back_ref):
        inv_wide_ref = narrow_ref.at[:, : 3 * length]
        inv_line_ref = narrow_ref.at[:, 3 * length : 6 * length]
        line_high = narrow_ref.at[:, 6 * length : 7 * length]
        line_low = narrow_ref.at[:, 7 * length :]
        kx_ref = waves_ref.at[:, :LANES]
        ky_ref = waves_ref.at[:, LANES:]

        def come(p):
            return pltpu.make_async_copy(lines_ref.at[p], held_ref.at[p], came.at[p])

        def tell(i):
            source = (narrow_hbm, wide_hbm, waves_hbm)[i]
            return pltpu.make_async_copy(source, (narrow_ref, wide_ref, waves_ref)[i], told.at[i])

        tell(0).start()
        for p in range(groups):
            come(p).start()
        tell(1).start()
        tell(2).start()
        tell(0).wait()

        def arrive(p, _):
            come(p).wait()
            flat = jnp.concatenate(
                [held_ref[p, :, t].reshape(others * SUB, LANES).T for t in range(tiles)], axis=0
            )
            side = jnp.concatenate(
                [flat[band * width : (band + 1) * width, :] for band in range(bands)], axis=1
            )
            high, low = halves(side)
            done = (
                dot(high, line_high[...], NN)
                + dot(low, line_high[...], NN)
                + dot(high, line_low[...], NN)
            )
            for u in range(units):
                c, j, k = u // (2 * kept), u // 2 % kept, u % 2
                at = (2 * c + k) * length
                high, low = halves(done[u * rows : (u + 1) * rows, :])
                for part, value in ((0, high), (1, low)):
                    target = pl.ds(pl.multiple_of(part * G + p * rows, 16), rows)
                    left_ref[j, target, at : at + length] = value
            return 0

        lax.fori_loop(0, groups, arrive, 0)
        tell(1).wait()
        tell(2).wait()

        def one_depth(j, _):
            index = (place_ref[1] + j) * devices + place_ref[0]
            kz = index.astype(f32) * unit_wave

            def widen(u, _):
                at = pl.ds(pl.multiple_of(u * length, LANES), length)
                spec_ref[:, at] = dot(wide_ref[:, :length], left_ref[j, :, at], NN) + dot(
                    wide_ref[:, length:], left_ref[j, :G, at], NN
                )
                return 0

            lax.fori_loop(0, 6, widen, 0)

            def turn(r, _):
                top = pl.multiple_of(r * step, step)
                kx = kx_ref[pl.ds(top, step), :]

                def store(c, k, half, lane, value):
                    at = (2 * c + k) * length + lane
                    for part, piece in zip((0, 1), halves(value)):
                        target = pl.ds(pl.multiple_of(part * length + half * G + top, step), step)
                        turned_ref[target, at : at + LANES] = piece

                def green_of(lane):
                    ky = ky_ref[0:1, lane : lane + LANES]
                    square = kx * kx + ky * ky + kz * kz
                    return jnp.exp(-0.5 * smoothing * smoothing * square) / (
                        square + jnp.where(square == 0.0, 1.0, 0.0)
                    )

                def load(c, k, half, lane):
                    at = (2 * c + k) * length + lane
                    target = pl.ds(pl.multiple_of(half * G + top, step), step)
                    return spec_ref[target, at : at + LANES]

                def curl(lane_of, dy_of, green):
                    gx = green * kx
                    gz = green * kz
                    many = range(len(lane_of))
                    got = {
                        (c, k, h, t): load(c, k, h, lane_of[t])
                        for c in range(3) for k in (0, 1) for h in (0, 1) for t in many
                    }

                    def dx(c, k, h, t):
                        value = gx * got[c, k, 1 - h, t]
                        return value if h == 0 else -value

                    def dz(c, k, h, t):
                        value = gz * got[c, 1 - k, h, t]
                        return value if k == 0 else -value

                    def dy(c, k, h, t):
                        return dy_of(got, c, k, h, t)

                    for k in (0, 1):
                        for h in (0, 1):
                            for t in many:
                                store(0, k, h, lane_of[t], dy(2, k, h, t) - dz(1, k, h, t))
                                store(1, k, h, lane_of[t], dz(0, k, h, t) - dx(2, k, h, t))
                                store(2, k, h, lane_of[t], dx(1, k, h, t) - dy(0, k, h, t))

                for tile in range(full // LANES):
                    lane = 2 * tile * LANES
                    green = green_of(lane)
                    gy = green * ky_ref[0:1, lane : lane + LANES]

                    def dy_pair(got, c, k, h, t, gy=gy):
                        value = gy * got[c, k, h, 1 - t]
                        return value if t == 0 else -value

                    curl((lane, lane + LANES), dy_pair, green)
                if full < G:
                    lane = 2 * full
                    green = green_of(lane)
                    gy = green * ky_ref[0:1, lane : lane + LANES]

                    def dy_roll(got, c, k, h, t):
                        return gy * pltpu.roll(got[c, k, h, t], LANES // 2, 1)

                    curl((lane,), dy_roll, green)
                return 0

            lax.fori_loop(0, G // step, turn, 0)

            def narrow(u, _):
                at = pl.ds(pl.multiple_of(u * length, LANES), length)
                done = dot(inv_wide_ref[:, : 2 * length], turned_ref[:, at], NN) + dot(
                    inv_wide_ref[:, 2 * length :], turned_ref[:length, at], NN
                )
                high, low = halves(done)
                unit = (u // 2) * (2 * kept) + 2 * j + u % 2
                target = pl.ds(pl.multiple_of(unit * rows, 16), rows)
                for p in range(groups):
                    for part, value in ((0, high), (1, low)):
                        back_ref[p, target, part * length : (part + 1) * length] = value[
                            p * rows : (p + 1) * rows, :
                        ]
                return 0

            lax.fori_loop(0, 6, narrow, 0)
            return 0

        lax.fori_loop(0, kept, one_depth, 0)

        def depart(p):
            return pltpu.make_async_copy(held_ref.at[p], out_ref.at[p], came.at[p])

        def leave(p, _):
            done = dot(inv_line_ref[:, : 2 * length], back_ref[p], NT) + dot(
                inv_line_ref[:, 2 * length :], back_ref[p, :, :length], NT
            )
            pieces = [
                done[band * others * SUB : (band + 1) * others * SUB, :] for band in range(bands)
            ]
            if tiles * LANES > bands * width:
                pieces += [jnp.zeros((others * SUB, tiles * LANES - bands * width), f32)]
            line = jnp.concatenate(pieces, axis=1)
            for t in range(tiles):
                held_ref[p, :, t] = line[:, t * LANES : (t + 1) * LANES].reshape(others, SUB, LANES)
            depart(p).start()
            return 0

        lax.fori_loop(0, groups, leave, 0)
        for p in range(groups):
            depart(p).wait()

    anywhere = pl.BlockSpec(memory_space=pltpu.HBM)
    flops = 6 * (4 * groups * width * G * length + 24 * kept * length * G * length)
    return pl.pallas_call(
        kernel,
        out_shape=jax.ShapeDtypeStruct(lines.shape, f32),
        in_specs=[pl.BlockSpec(memory_space=pltpu.SMEM)] + [anywhere] * 4,
        out_specs=anywhere,
        scratch_shapes=[
            pltpu.VMEM(lines.shape, f32),
            *(pltpu.VMEM(table.shape, table.dtype) for table in tables),
            pltpu.SemaphoreType.DMA((groups,)),
            pltpu.SemaphoreType.DMA((3,)),
            pltpu.VMEM((kept, 2 * G, 6 * length), bf16),
            pltpu.VMEM((length, 6 * length), f32),
            pltpu.VMEM((2 * length, 6 * length), bf16),
            pltpu.VMEM((groups, width, 2 * length), bf16),
        ],
        cost_estimate=pl.CostEstimate(
            flops=flops, bytes_accessed=8 * lines.size, transcendentals=kept * G * G
        ),
        compiler_params=pltpu.CompilerParams(vmem_limit_bytes=ALL_VMEM),
        name="planes",
    )(place, lines, *tables)


def halo(slabs):
    def shifted(piece, axis, up):
        devices = lax.axis_size(axis)
        pairs = [(i, i + 1) for i in range(devices - 1)]
        if not up:
            pairs = [(j, i) for i, j in pairs]
        return lax.ppermute(piece, axis, pairs)

    last_rows, first_rows, last_cols, first_cols = slabs
    return (
        shifted(last_cols, "py", True),
        shifted(first_cols, "py", False),
        shifted(last_rows, "px", True),
        shifted(first_rows, "px", False),
    )


def depth_weights(G):
    width = 2 * G
    at = np.arange(width) % G
    rows = []
    for k in range(width // LANES):
        for shift, weight in ((1, 8.0), (-1, -8.0), (2, -1.0), (-2, 1.0)):
            inside = (at + shift >= 0) & (at + shift < G)
            rows.append(np.where(inside, weight / 12.0, 0.0)[k * LANES : (k + 1) * LANES])
    return np.stack(rows).astype(np.float32)


def stretch(field, flow, left, right, size):
    rows, cols, G = size.rows, size.cols, size.G
    span = 2 * G // LANES
    many = cols * G // LANES
    half = LANES // 2

    def kernel(field_hbm, flow_ref, left_ref, right_ref, weight_ref, out_ref, field_ref, sem,
               ext_ref, turned_ref):
        whole = pltpu.make_async_copy(field_hbm, field_ref, sem)

        @pl.when(pl.program_id(0) == 0)
        def _():
            whole.start()
            ext_ref[:, 0:SUB, :] = jnp.zeros((many + 2 * span, SUB, LANES), f32)
            ext_ref[:, SUB + rows :, :] = jnp.zeros((many + 2 * span, SUB, LANES), f32)

        def put(t, value):
            ext_ref[t, SUB : SUB + rows, :] = value
            turned_ref[t] = pltpu.roll(value, half, 1)

        for t in range(many):
            at = slice(t * LANES, (t + 1) * LANES)
            put(span + t, flow_ref[0, :, at])
        for t in range(span):
            at = slice(t * LANES, (t + 1) * LANES)
            put(t, left_ref[0, :, at])
            put(span + many + t, right_ref[0, :, at])
        lane = lax.broadcasted_iota(jnp.int32, (ROWS, LANES), 1)

        @pl.when(pl.program_id(0) == 0)
        def _():
            whole.wait()

        def block(b, _):
            base = span * (b + 1)
            for top in range(0, rows, ROWS):
                these = slice(top, top + ROWS)

                def tall_at(t, s):
                    return ext_ref[t, SUB + top + s : SUB + top + s + ROWS, :]

                def side_at(t):
                    return jnp.where(lane < half, turned_ref[t, these, :], turned_ref[t + 1, these, :])

                own = [tall_at(base + k, 0) for k in range(span)]
                for k in range(span):
                    t = base + k
                    deep = 0.0
                    for i, s in enumerate((1, -1, 2, -2)):
                        value = pltpu.roll(own[k], (-s) % LANES, 1)
                        if s > 0 and k + 1 < span:
                            value = jnp.where(
                                lane < LANES - s, value, pltpu.roll(own[k + 1], (-s) % LANES, 1)
                            )
                        if s < 0 and k > 0:
                            value = jnp.where(
                                lane >= -s, value, pltpu.roll(own[k - 1], (-s) % LANES, 1)
                            )
                        deep = deep + weight_ref[4 * k + i : 4 * k + i + 1, :] * value
                    side = 8.0 * (side_at(t + 1) - side_at(t - 2)) - (
                        tall_at(t + span, 0) - tall_at(t - span, 0)
                    )
                    tall = 8.0 * (tall_at(t, 1) - tall_at(t, -1)) - (tall_at(t, 2) - tall_at(t, -2))
                    at = pl.ds(pl.multiple_of((span * b + k) * LANES, LANES), LANES)
                    out_ref[0, these, at] = field_ref[2, these, at] * deep + (1.0 / 12.0) * (
                        field_ref[1, these, at] * side + field_ref[0, these, at] * tall
                    )
            return 0

        lax.fori_loop(0, cols // 2, block, 0)

    def part(*shape):
        return pl.BlockSpec((1,) + shape, lambda i: (i, 0, 0))

    return pl.pallas_call(
        kernel,
        grid=(3,),
        out_shape=jax.ShapeDtypeStruct((3, rows, cols * G), f32),
        in_specs=[
            pl.BlockSpec(memory_space=pltpu.HBM),
            part(rows, cols * G),
            part(rows, 2 * G),
            part(rows, 2 * G),
            pl.BlockSpec((4 * span, LANES), lambda i: (0, 0)),
        ],
        out_specs=part(rows, cols * G),
        scratch_shapes=[
            pltpu.VMEM((3, rows, cols * G), f32),
            pltpu.SemaphoreType.DMA,
            pltpu.VMEM((many + 2 * span, rows + 2 * SUB, LANES), f32),
            pltpu.VMEM((many + 2 * span, rows, LANES), f32),
        ],
        cost_estimate=pl.CostEstimate(
            flops=60 * flow.size, bytes_accessed=12 * flow.size, transcendentals=0
        ),
        compiler_params=pltpu.CompilerParams(vmem_limit_bytes=MOST_VMEM),
        name="stretch",
    )(field, flow, left, right, jnp.asarray(depth_weights(G)))


def add_rows(field, part, up, down, size):
    rows, width = size.rows, size.cols * size.G
    last = rows // SUB - 1

    def kernel(field_ref, part_ref, up_ref, down_ref, out_ref):
        out_ref[...] = part_ref[...]

        def add(c, row, value):
            at = slice(row, row + 1)
            out_ref[c, at, :] = part_ref[c, at, :] + (1.0 / 12.0) * field_ref[0, at, :] * value

        @pl.when(pl.program_id(0) == 0)
        def _():
            for c in range(3):
                far, near = up_ref[c, 0:1, :], up_ref[c, 1:2, :]
                add(c, 0, far - 8.0 * near)
                add(c, 1, near)

        @pl.when(pl.program_id(0) == 1)
        def _():
            for c in range(3):
                near, far = down_ref[c, 0:1, :], down_ref[c, 1:2, :]
                add(c, SUB - 1, 8.0 * near - far)
                add(c, SUB - 2, -near)

    edge = pl.BlockSpec((3, SUB, width), lambda i: (0, i * last, 0))
    whole = pl.BlockSpec((3, 2, width), lambda i: (0, 0, 0))
    return pl.pallas_call(
        kernel,
        grid=(2,),
        out_shape=jax.ShapeDtypeStruct((3, rows, width), f32),
        in_specs=[pl.BlockSpec((1, SUB, width), lambda i: (0, i * last, 0)), edge, whole, whole],
        out_specs=edge,
        input_output_aliases={1: 0},
        cost_estimate=pl.CostEstimate(
            flops=60 * width, bytes_accessed=4 * 40 * 3 * width, transcendentals=0
        ),
        compiler_params=pltpu.CompilerParams(vmem_limit_bytes=MOST_VMEM),
        name="add_rows",
    )(field, part, up, down)


def triple(table, axis):
    high, low = split_table(table)
    return np.concatenate([high, high, low], axis=axis)


def fast(vorticity, size):
    rows, cols, G, devices, groups = size.rows, size.cols, size.G, size.devices, size.groups
    length, bands, others = size.length, size.bands, size.G // size.cols
    axes = ("px", "py")
    place = lax.axis_index(axes).astype(jnp.int32)

    cells = np.array([
        q * cols + band * SUB + s for band in range(bands) for q in range(others) for s in range(SUB)
    ])
    lane_modes, lane_kinds = lane_order(G)
    row_modes = np.concatenate([np.arange(G)] * 2)
    row_kinds = np.repeat([0, 1], G)
    line_basis = basis(G, lane_modes, lane_kinds, length)[cells]
    wide_basis = basis(G, row_modes, row_kinds, length)
    line = split_table(line_basis)
    wide = triple(wide_basis.T, 1)
    inv_wide = triple(wide_basis * weights(row_modes, length), 1)
    inv_line = triple(line_basis * weights(lane_modes, length), 1)
    kx = np.broadcast_to(waves(np.arange(G), length)[:, None], (G, LANES)).astype(np.float32)
    signs = np.where(lane_kinds == 0, 1.0, -1.0)
    signs[: 2 * (G // LANES * LANES)] = 1.0
    ky = (waves(lane_modes, length) * signs).astype(np.float32)
    waves_of = np.zeros((G, LANES + length), np.float32)
    waves_of[:, :LANES] = kx
    waves_of[:, LANES:] = ky
    narrow = np.concatenate([inv_wide, inv_line, *line], axis=1)
    tables = tuple(jnp.asarray(t) for t in (narrow, wide, waves_of))

    def depth_tables(start, kept):
        modes = np.array([
            (start + j) * devices + d
            for j in range(kept) for k in (0, 1) for d in range(devices)
        ])
        kinds = np.array([k for j in range(kept) for k in (0, 1) for d in range(devices)])
        table = basis(G, modes, kinds, length)
        forward = np.stack(split_table(table.T))
        inverse = np.stack(split_table((table * weights(modes, length)).T))
        return jnp.asarray(forward), jnp.asarray(inverse)

    def exchange(value):
        value = value.reshape(devices, -1, LANES)
        return lax.all_to_all(value, axes, split_axis=0, concat_axis=0, tiled=True)

    arrived = []
    for start, kept in size.chunks:
        arrived.append(exchange(depth_forward(vorticity, depth_tables(start, kept)[0], size, kept)))
    returned = []
    for (start, kept), lines in zip(size.chunks, arrived):
        lines = lines.reshape(groups, others, size.tiles(kept), SUB, LANES)
        where = jnp.stack([place, jnp.int32(start)])
        returned.append(exchange(planes(lines, where, tables, size, kept)))
    flow = None
    for (start, kept), lines in zip(size.chunks, returned):
        last = start + kept == G // devices
        flow, *slabs = depth_inverse(
            lines.reshape(-1, LANES), depth_tables(start, kept)[1], flow, size, kept, last
        )
    left, right, up, down = halo(slabs)
    part = stretch(vorticity, flow, left, right, size)
    return flow, add_rows(vorticity, part, up, down, size)


def with_halo(shard, sides, width):
    for axis, dim in sides:
        devices, length = (lax.axis_size(axis), shard.shape[dim])
        up = [(i, (i + 1) % devices) for i in range(devices - 1)]
        down = [(j, i) for i, j in up]
        last = lax.slice_in_dim(shard, length - width, length, axis=dim)
        leading = lax.slice_in_dim(shard, 0, width, axis=dim)
        before = lax.ppermute(last, axis, up)
        after = lax.ppermute(leading, axis, down)
        shard = jnp.concatenate([before, shard, after], axis=dim)
    return shard


def twiddle(count_in, count_out, length, factor):
    source = lax.broadcasted_iota(jnp.int32, (count_in, count_out), 0)
    target = lax.broadcasted_iota(jnp.int32, (count_in, count_out), 1)
    angle = (source * target % length).astype(jnp.float32) * (2.0 * math.pi / length)
    cosine = jnp.cos(angle) * factor
    sine = jnp.sin(angle) * factor
    return (
        jnp.broadcast_to(cosine, (3, count_in, count_out)),
        jnp.broadcast_to(sine, (3, count_in, count_out)),
    )


def product(einsum_form, first, second):
    return jnp.einsum(einsum_form, first, second, precision=highest)


def forward_left(pair, einsum_form, tables):
    real_part, imag_part = pair
    cosine_table, sine_table = tables
    return (
        product(einsum_form, cosine_table, real_part) + product(einsum_form, sine_table, imag_part),
        product(einsum_form, cosine_table, imag_part) - product(einsum_form, sine_table, real_part),
    )


def forward_right(pair, einsum_form, tables):
    real_part, imag_part = pair
    cosine_table, sine_table = tables
    return (
        product(einsum_form, real_part, cosine_table) + product(einsum_form, imag_part, sine_table),
        product(einsum_form, imag_part, cosine_table) - product(einsum_form, real_part, sine_table),
    )


def backward_left(pair, einsum_form, tables):
    real_part, imag_part = pair
    cosine_table, sine_table = tables
    return (
        product(einsum_form, cosine_table, real_part) - product(einsum_form, sine_table, imag_part),
        product(einsum_form, cosine_table, imag_part) + product(einsum_form, sine_table, real_part),
    )


def wavenumbers(start, count, length, position):
    index = start + lax.iota(jnp.int32, count)
    signed = jnp.where(index < length // 2, index, index - length)
    wave = signed.astype(jnp.float32) * (2.0 * math.pi / length)
    slope = jnp.where(index == length // 2, 0.0, wave)
    keep = jnp.where(index == length // 2, 0.0, 1.0)
    shape = [1, 1, 1, 1]
    shape[position] = count
    return (wave.reshape(shape), slope.reshape(shape), keep.reshape(shape))


def velocity_spectrum(pair, waves_x, waves_y, waves_z):
    square = waves_x[0] ** 2 + waves_y[0] ** 2 + waves_z[0] ** 2
    mask = waves_x[2] * waves_y[2] * waves_z[2]
    green = (
        mask
        * jnp.exp(-0.5 * smoothing * smoothing * square)
        / (square + jnp.where(square == 0.0, 1.0, 0.0))
    )
    slope_x, slope_y, slope_z = (waves_x[1][0], waves_y[1][0], waves_z[1][0])

    def curl(field):
        return jnp.stack(
            [
                slope_y * field[2] - slope_z * field[1],
                slope_z * field[0] - slope_x * field[2],
                slope_x * field[1] - slope_y * field[0],
            ]
        )

    real_part = pair[0] * green
    imag_part = pair[1] * green
    return (jnp.swapaxes(-curl(imag_part), 1, 2), jnp.swapaxes(curl(real_part), 1, 2))


def window(padded, axis, offset):
    starts = [0, 2, 2, 2]
    limits = [padded.shape[0], padded.shape[1] - 2, padded.shape[2] - 2, padded.shape[3] - 2]
    starts[axis] = starts[axis] + offset
    limits[axis] = limits[axis] + offset
    return lax.slice(padded, starts, limits)


def derivative(padded, axis):
    near = window(padded, axis, 1) - window(padded, axis, -1)
    far = window(padded, axis, 2) - window(padded, axis, -2)
    return (8.0 * near - far) / 12.0


def general(vorticity):
    block_rows = vorticity.shape[1]
    G = block_rows * lax.axis_size("px")
    block_cols = vorticity.shape[2] // G
    field = vorticity.reshape(3, block_rows, block_cols, G)
    length = 2 * G
    depth_tables = twiddle(G, G, length, 1.0)
    line_tables = twiddle(G, length, length, 1.0)
    inverse_tables = twiddle(length, G, length, 1.0 / length)
    closing = twiddle(G, G, length, 1.0 / length)
    weights = jnp.where(lax.iota(jnp.int32, G) == 0, 1.0, 2.0)[None, :, None]
    closing_cos = closing[0] * weights
    closing_sin = closing[1] * weights
    pair = (
        product("czk,cxyz->ckxy", depth_tables[0], field),
        -product("czk,cxyz->ckxy", depth_tables[1], field),
    )
    pair = (
        lax.all_to_all(pair[0], "py", split_axis=1, concat_axis=3, tiled=True),
        lax.all_to_all(pair[1], "py", split_axis=1, concat_axis=3, tiled=True),
    )
    pair = forward_left(pair, "cyl,ckxy->clkx", line_tables)
    pair = (
        lax.all_to_all(pair[0], "px", split_axis=1, concat_axis=3, tiled=True),
        lax.all_to_all(pair[1], "px", split_axis=1, concat_axis=3, tiled=True),
    )
    pair = forward_right(pair, "clkx,cxm->clkm", line_tables)
    rows = pair[0].shape[1]
    depth = pair[0].shape[2]
    waves_y = wavenumbers(lax.axis_index("px") * rows, rows, length, 1)
    waves_z = wavenumbers(lax.axis_index("py") * depth, depth, length, 2)
    waves_x = wavenumbers(0, length, length, 3)
    pair = velocity_spectrum(pair, waves_x, waves_y, waves_z)
    pair = backward_left(pair, "cmx,cklm->cxkl", inverse_tables)
    pair = (
        lax.all_to_all(pair[0], "px", split_axis=1, concat_axis=3, tiled=True),
        lax.all_to_all(pair[1], "px", split_axis=1, concat_axis=3, tiled=True),
    )
    pair = backward_left(pair, "cly,cxkl->cyxk", inverse_tables)
    pair = (
        lax.all_to_all(pair[0], "py", split_axis=1, concat_axis=3, tiled=True),
        lax.all_to_all(pair[1], "py", split_axis=1, concat_axis=3, tiled=True),
    )
    flow = product("cyxk,ckz->cyxz", pair[0], closing_cos) - product(
        "cyxk,ckz->cyxz", pair[1], closing_sin
    )
    flow = jnp.swapaxes(flow, 1, 2)
    padded = with_halo(flow, (("px", 1), ("py", 2)), 2)
    padded = jnp.pad(padded, ((0, 0), (0, 0), (0, 0), (2, 2)))
    stretching = (
        field[0] * derivative(padded, 1)
        + field[1] * derivative(padded, 2)
        + field[2] * derivative(padded, 3)
    )
    return (
        flow.reshape(3, block_rows, block_cols * G),
        stretching.reshape(3, block_rows, block_cols * G),
    )


def on_device(vorticity):
    sizes = fast_sizes(vorticity)
    if sizes is None:
        return general(vorticity)
    return fast(vorticity, sizes)


def solution(mesh):
    in_specs = (P(None, "px", "py"),)
    out_specs = (P(None, "px", "py"), P(None, "px", "py"))
    return jax.shard_map(
        on_device, mesh=mesh, in_specs=in_specs, out_specs=out_specs, check_vma=False
    )
```

```python
import math

import jax
import jax.numpy as jnp
import numpy as np
from jax import lax
from jax.experimental import pallas as pl
from jax.experimental.pallas import tpu as pltpu
from jax.sharding import PartitionSpec as P


smoothing = 1.0
highest = lax.Precision.HIGHEST
f32 = jnp.float32
bf16 = jnp.bfloat16
LANES = 128
SUB = 8
ROWS = 16
ALL_VMEM, MOST_VMEM = 67_000_000, 64_000_000


def split_table(table):
    high = table.astype(np.float32).astype(jnp.bfloat16)
    low = (table - high.astype(np.float64)).astype(np.float32).astype(jnp.bfloat16)
    return high, low


def waves(modes, length):
    return np.asarray(modes, np.float64) * (2.0 * math.pi / length)


def basis(points, modes, kinds, length):
    angle = (np.arange(points)[:, None] * np.asarray(modes)[None, :] % length) * (
        2.0 * math.pi / length
    )
    return np.where(np.asarray(kinds)[None, :] == 0, np.cos(angle), np.sin(angle))


def weights(modes, length):
    return np.where(np.asarray(modes) == 0, 1.0, 2.0) / length


def lane_order(modes):
    full = modes // LANES * LANES
    index, kind = [], []
    for start in range(0, full, LANES):
        for k in (0, 1):
            index += list(range(start, start + LANES))
            kind += [k] * LANES
    for k in (0, 1):
        index += list(range(full, modes))
        kind += [k] * (modes - full)
    return np.array(index), np.array(kind)


def dot(first, second, dims):
    return lax.dot_general(first, second, (dims, ((), ())), preferred_element_type=f32)


NN = ((1,), (0,))
NT = ((1,), (1,))
TN = ((0,), (0,))


def halves(value):
    high = value.astype(bf16)
    low = (value - high.astype(f32)).astype(bf16)
    return high, low


class Sizes:
    def __init__(self, rows, cols, G, devices, groups):
        self.rows, self.cols, self.G = rows, cols, G
        self.devices, self.groups = devices, groups
        self.bands = cols // SUB
        self.spare = G % LANES
        self.span = G + self.spare
        self.side = -(-cols // 2 * rows // LANES) * LANES
        self.length = 2 * G
        total = G // devices
        first = max(1, total // 3)
        self.chunks = [(0, first), (first, total - first)] if total > first else [(0, first)]

    def line(self, y):
        return (y // 2 + SUB // 2 * (y % 2)) % (self.cols // 2) * self.rows

    def slot(self, y):
        return y % 2 * self.side + self.line(y)

    def units(self, kept):
        return 6 * kept

    def tiles(self, kept):
        return -(-self.bands * self.units(kept) * self.rows // LANES)


def fast_sizes(vorticity):
    rows = vorticity.shape[1]
    groups = lax.axis_size("px")
    G = rows * groups
    cols = vorticity.shape[2] // G
    devices = groups * lax.axis_size("py")
    if rows % 16 or rows * cols % LANES or cols % (2 * SUB) not in (0, SUB) or cols % SUB or cols % 2:
        return None
    if G % devices or devices % SUB or G % LANES != LANES // 2:
        return None
    return Sizes(rows, cols, G, devices, groups)


class LaneMoves:
    def __init__(self, fragments):
        self.merged = []
        self.wanted = {}
        open_groups = {}
        for dest, to, source, start, width in fragments:
            at = to
            shift = (to - start) % LANES
            while at < to + width:
                origin = at - to + start
                take = min(to + width - at, LANES - origin % LANES)
                group = self._place(open_groups, origin // LANES, shift, origin % LANES, take, source)
                end = at + take
                while at < end:
                    part = min(end - at, LANES - at % LANES)
                    self.wanted.setdefault((dest, at // LANES), []).append((at % LANES, group))
                    at += part

    def _place(self, open_groups, tile, shift, lane, width, source):
        for group in open_groups.setdefault((tile, shift), []):
            pieces = self.merged[group][2]
            if all(lane >= at + wide or at >= lane + width for at, wide, _ in pieces):
                pieces.append((lane, width, source))
                return group
        self.merged.append((tile, shift, [(lane, width, source)]))
        open_groups[tile, shift].append(len(self.merged) - 1)
        return len(self.merged) - 1

    def run(self, load, store, held, shape):
        lane = lax.broadcasted_iota(jnp.int32, shape, 1)

        def choose(parts):
            value = None
            for at, part in sorted(parts, key=lambda pair: pair[0]):
                value = part() if value is None else jnp.where(lane >= at, part(), value)
            return value

        for index, (tile, shift, pieces) in enumerate(self.merged):
            value = choose(
                [(at, lambda source=source, tile=tile: load(source, tile)) for at, _, source in pieces]
            )
            held[index] = pltpu.roll(value, shift, 1) if shift else value
        for (dest, tile), parts in self.wanted.items():
            store(dest, tile, choose([(at, lambda index=index: held[index]) for at, index in parts]))


def depth_forward(shard, table, size, kept):
    rows, cols, G, devices = size.rows, size.cols, size.G, size.devices
    units, tiles, bands = size.units(kept), size.tiles(kept), size.bands
    block = 2 * kept * devices
    half = cols // 2 * rows
    moves = LaneMoves([
        (s, (band * units + u) * rows, u, size.slot(SUB * band + s), rows)
        for s in range(SUB)
        for band in range(bands)
        for u in range(units)
    ])

    def kernel(shard_ref, table_ref, out_ref, held_ref, sems, high_ref, low_ref, mid_ref, turned_ref):
        def fetch(c):
            return pltpu.make_async_copy(shard_ref.at[c], held_ref.at[c], sems.at[c])

        for c in range(3):
            fetch(c).start()

        for c in range(3):
            fetch(c).wait()
            for y in range(cols):
                odd, to = y % 2, size.line(y)
                start = y * G - odd * size.spare
                high, low = halves(held_ref[c, :, start : start + size.span])
                high_ref[c, odd, to : to + rows, :] = high
                low_ref[c, odd, to : to + rows, :] = low
        for c in range(3):
            for odd in (0, 1):
                at = odd * size.side
                mid_ref[c * block : (c + 1) * block, at : at + half] = (
                    dot(table_ref[odd, 0], high_ref[c, odd], NT)
                    + dot(table_ref[odd, 0], low_ref[c, odd], NT)
                    + dot(table_ref[odd, 1], high_ref[c, odd], NT)
                )

        def load(u, t):
            return mid_ref[u * devices : (u + 1) * devices, t * LANES : (t + 1) * LANES]

        def store(s, t, value):
            out_ref[pl.ds(t * SUB + s, devices, stride=tiles * SUB), :] = value

        moves.run(load, store, turned_ref, (devices, LANES))

    return pl.pallas_call(
        kernel,
        out_shape=jax.ShapeDtypeStruct((devices * tiles * SUB, LANES), f32),
        in_specs=[pl.BlockSpec(memory_space=pltpu.HBM), pl.BlockSpec(memory_space=pltpu.VMEM)],
        out_specs=pl.BlockSpec(memory_space=pltpu.VMEM),
        scratch_shapes=[
            pltpu.VMEM((3, rows, cols * G), f32),
            pltpu.SemaphoreType.DMA((3,)),
            pltpu.VMEM((3, 2, half, size.span), bf16),
            pltpu.VMEM((3, 2, half, size.span), bf16),
            pltpu.VMEM((3 * block, 2 * size.side), f32),
            pltpu.VMEM((len(moves.merged), devices, LANES), f32),
        ],
        cost_estimate=pl.CostEstimate(
            flops=18 * block * G * rows * cols,
            bytes_accessed=4 * (3 * rows * cols * G + devices * tiles * SUB * LANES),
            transcendentals=0,
        ),
        compiler_params=pltpu.CompilerParams(vmem_limit_bytes=ALL_VMEM),
        name="depth_forward",
    )(shard, table)


def depth_inverse(lines, table, before, size, kept, slabs):
    rows, cols, G, devices = size.rows, size.cols, size.G, size.devices
    units, tiles, bands = size.units(kept), size.tiles(kept), size.bands
    block = 2 * kept * devices
    half = cols // 2 * rows
    share = SUB * tiles * SUB
    extra = [] if before is None else [before]
    anywhere = pl.BlockSpec(memory_space=pltpu.HBM)
    whole = pl.BlockSpec(memory_space=pltpu.VMEM)
    moves = LaneMoves([
        (u, size.slot(SUB * band + s), s, (band * units + u) * rows, rows)
        for u in range(units)
        for band in range(bands)
        for s in range(SUB)
    ])
    outs = [jax.ShapeDtypeStruct((3, rows, cols * G), f32)]
    if slabs:
        outs += [jax.ShapeDtypeStruct((3, 2, cols * G), f32)] * 2
        outs += [jax.ShapeDtypeStruct((3, rows, 2 * G), f32)] * 2

    def kernel(lines_ref, table_ref, *refs):
        out_ref, *slab_refs = refs[len(extra) : len(extra) + len(outs)]
        held_ref, ready_ref, mid_ref, turned_ref, done_ref, came, had, gone = refs[
            len(extra) + len(outs) :
        ]

        def arrive(g):
            at = pl.ds(g * share, share)
            return pltpu.make_async_copy(lines_ref.at[at], held_ref.at[at], came.at[g])

        def earlier(c):
            return pltpu.make_async_copy(refs[0].at[c], ready_ref.at[c], had.at[c])

        def leave(c):
            return pltpu.make_async_copy(ready_ref.at[c], out_ref.at[c], gone.at[c])

        for g in range(devices // SUB):
            arrive(g).start()
        if extra:
            for c in range(3):
                earlier(c).start()
        for g in range(devices // SUB):
            arrive(g).wait()

            def load(s, t):
                return held_ref[pl.ds(g * share + t * SUB + s, SUB, stride=tiles * SUB), :]

            def store(u, t, value):
                to = u * devices + g * SUB
                mid_ref[to : to + SUB, t * LANES : (t + 1) * LANES] = value

            moves.run(load, store, turned_ref.at[g], (SUB, LANES))

        if extra:
            for c in range(3):
                earlier(c).wait()
        for c in range(3):
            for odd in (0, 1):
                at = odd * size.side
                high, low = halves(mid_ref[c * block : (c + 1) * block, at : at + half].T)
                done_ref[c, odd] = (
                    dot(high, table_ref[odd, 0], NN)
                    + dot(low, table_ref[odd, 0], NN)
                    + dot(high, table_ref[odd, 1], NN)
                )
            for y in range(0, cols, 2):
                even = done_ref[c, 0, size.line(y) : size.line(y) + rows, :]
                odd = done_ref[c, 1, size.line(y + 1) : size.line(y + 1) + rows, :]
                shared = size.span - 2 * size.spare
                pair = jnp.concatenate(
                    [
                        even[:, :shared],
                        even[:, shared:] + odd[:, : 2 * size.spare],
                        odd[:, 2 * size.spare :],
                    ],
                    axis=1,
                )
                if extra:
                    pair = pair + ready_ref[c, :, y * G : (y + 2) * G]
                ready_ref[c, :, y * G : (y + 2) * G] = pair
                if slabs:
                    slab_refs[0][c, :, y * G : (y + 2) * G] = pair[rows - 2 :, :]
                    slab_refs[1][c, :, y * G : (y + 2) * G] = pair[:2, :]
                if slabs and y == cols - 2:
                    slab_refs[2][c] = pair
                if slabs and y == 0:
                    slab_refs[3][c] = pair
            leave(c).start()
        for c in range(3):
            leave(c).wait()

    return pl.pallas_call(
        kernel,
        out_shape=outs,
        in_specs=[anywhere, whole] + [anywhere] * len(extra),
        out_specs=[anywhere] + [whole] * (len(outs) - 1),
        scratch_shapes=[
            pltpu.VMEM((devices * tiles * SUB, LANES), f32),
            pltpu.VMEM((3, rows, cols * G), f32),
            pltpu.VMEM((3 * block, 2 * size.side), f32),
            pltpu.VMEM((devices // SUB, len(moves.merged), SUB, LANES), f32),
            pltpu.VMEM((3, 2, half, size.span), f32),
            pltpu.SemaphoreType.DMA((devices // SUB,)),
            pltpu.SemaphoreType.DMA((3,)),
            pltpu.SemaphoreType.DMA((3,)),
        ],
        cost_estimate=pl.CostEstimate(
            flops=18 * block * G * rows * cols,
            bytes_accessed=4 * (9 * rows * cols * G + devices * tiles * SUB * LANES),
            transcendentals=0,
        ),
        compiler_params=pltpu.CompilerParams(vmem_limit_bytes=ALL_VMEM),
        name="depth_inverse",
    )(lines, table, *extra)


def planes(lines, place, tables, size, kept):
    rows, cols, G, devices, groups = size.rows, size.cols, size.G, size.devices, size.groups
    units, tiles, bands, length = size.units(kept), size.tiles(kept), size.bands, size.length
    width = units * rows
    step = 16
    unit_wave = 2.0 * math.pi / length
    full = G // LANES * LANES
    others = G // cols

    def kernel(place_ref, lines_ref, narrow_hbm, wide_hbm, waves_hbm, out_ref, held_ref, narrow_ref,
               wide_ref, waves_ref, came, told, left_ref, spec_ref, turned_ref, back_ref):
        inv_wide_ref = narrow_ref.at[:, : 3 * length]
        inv_line_ref = narrow_ref.at[:, 3 * length : 6 * length]
        line_high = narrow_ref.at[:, 6 * length : 7 * length]
        line_low = narrow_ref.at[:, 7 * length :]
        kx_ref = waves_ref.at[:, :LANES]
        ky_ref = waves_ref.at[:, LANES:]

        def come(p):
            return pltpu.make_async_copy(lines_ref.at[p], held_ref.at[p], came.at[p])

        def tell(i):
            source = (narrow_hbm, wide_hbm, waves_hbm)[i]
            return pltpu.make_async_copy(source, (narrow_ref, wide_ref, waves_ref)[i], told.at[i])

        tell(0).start()
        for p in range(groups):
            come(p).start()
        tell(1).start()
        tell(2).start()
        tell(0).wait()

        def arrive(p, _):
            come(p).wait()
            flat = jnp.concatenate(
                [held_ref[p, :, t].reshape(others * SUB, LANES).T for t in range(tiles)], axis=0
            )
            side = jnp.concatenate(
                [flat[band * width : (band + 1) * width, :] for band in range(bands)], axis=1
            )
            high, low = halves(side)
            done = (
                dot(high, line_high[...], NN)
                + dot(low, line_high[...], NN)
                + dot(high, line_low[...], NN)
            )
            for u in range(units):
                c, j, k = u // (2 * kept), u // 2 % kept, u % 2
                at = (2 * c + k) * length
                high, low = halves(done[u * rows : (u + 1) * rows, :])
                for part, value in ((0, high), (1, low)):
                    target = pl.ds(pl.multiple_of(part * G + p * rows, 16), rows)
                    left_ref[j, target, at : at + length] = value
            return 0

        lax.fori_loop(0, groups, arrive, 0)
        tell(1).wait()
        tell(2).wait()

        def one_depth(j, _):
            index = (place_ref[1] + j) * devices + place_ref[0]
            kz = index.astype(f32) * unit_wave

            def widen(u, _):
                at = pl.ds(pl.multiple_of(u * length, LANES), length)
                spec_ref[:, at] = dot(wide_ref[:, :length], left_ref[j, :, at], NN) + dot(
                    wide_ref[:, length:], left_ref[j, :G, at], NN
                )
                return 0

            lax.fori_loop(0, 6, widen, 0)

            def turn(r, _):
                top = pl.multiple_of(r * step, step)
                kx = kx_ref[pl.ds(top, step), :]

                def store(c, k, half, lane, value):
                    at = (2 * c + k) * length + lane
                    for part, piece in zip((0, 1), halves(value)):
                        target = pl.ds(pl.multiple_of(part * length + half * G + top, step), step)
                        turned_ref[target, at : at + LANES] = piece

                def green_of(lane):
                    ky = ky_ref[0:1, lane : lane + LANES]
                    square = kx * kx + ky * ky + kz * kz
                    return jnp.exp(-0.5 * smoothing * smoothing * square) / (
                        square + jnp.where(square == 0.0, 1.0, 0.0)
                    )

                def load(c, k, half, lane):
                    at = (2 * c + k) * length + lane
                    target = pl.ds(pl.multiple_of(half * G + top, step), step)
                    return spec_ref[target, at : at + LANES]

                def curl(lane_of, dy_of, green):
                    gx = green * kx
                    gz = green * kz
                    many = range(len(lane_of))
                    got = {
                        (c, k, h, t): load(c, k, h, lane_of[t])
                        for c in range(3) for k in (0, 1) for h in (0, 1) for t in many
                    }

                    def dx(c, k, h, t):
                        value = gx * got[c, k, 1 - h, t]
                        return value if h == 0 else -value

                    def dz(c, k, h, t):
                        value = gz * got[c, 1 - k, h, t]
                        return value if k == 0 else -value

                    def dy(c, k, h, t):
                        return dy_of(got, c, k, h, t)

                    for k in (0, 1):
                        for h in (0, 1):
                            for t in many:
                                store(0, k, h, lane_of[t], dy(2, k, h, t) - dz(1, k, h, t))
                                store(1, k, h, lane_of[t], dz(0, k, h, t) - dx(2, k, h, t))
                                store(2, k, h, lane_of[t], dx(1, k, h, t) - dy(0, k, h, t))

                for tile in range(full // LANES):
                    lane = 2 * tile * LANES
                    green = green_of(lane)
                    gy = green * ky_ref[0:1, lane : lane + LANES]

                    def dy_pair(got, c, k, h, t, gy=gy):
                        value = gy * got[c, k, h, 1 - t]
                        return value if t == 0 else -value

                    curl((lane, lane + LANES), dy_pair, green)
                if full < G:
                    lane = 2 * full
                    green = green_of(lane)
                    gy = green * ky_ref[0:1, lane : lane + LANES]

                    def dy_roll(got, c, k, h, t):
                        return gy * pltpu.roll(got[c, k, h, t], LANES // 2, 1)

                    curl((lane,), dy_roll, green)
                return 0

            lax.fori_loop(0, G // step, turn, 0)

            def narrow(u, _):
                at = pl.ds(pl.multiple_of(u * length, LANES), length)
                done = dot(inv_wide_ref[:, : 2 * length], turned_ref[:, at], NN) + dot(
                    inv_wide_ref[:, 2 * length :], turned_ref[:length, at], NN
                )
                high, low = halves(done)
                unit = (u // 2) * (2 * kept) + 2 * j + u % 2
                target = pl.ds(pl.multiple_of(unit * rows, 16), rows)
                for p in range(groups):
                    for part, value in ((0, high), (1, low)):
                        back_ref[p, target, part * length : (part + 1) * length] = value[
                            p * rows : (p + 1) * rows, :
                        ]
                return 0

            lax.fori_loop(0, 6, narrow, 0)
            return 0

        lax.fori_loop(0, kept, one_depth, 0)

        def depart(p):
            return pltpu.make_async_copy(held_ref.at[p], out_ref.at[p], came.at[p])

        def leave(p, _):
            done = dot(inv_line_ref[:, : 2 * length], back_ref[p], NT) + dot(
                inv_line_ref[:, 2 * length :], back_ref[p, :, :length], NT
            )
            pieces = [
                done[band * others * SUB : (band + 1) * others * SUB, :] for band in range(bands)
            ]
            if tiles * LANES > bands * width:
                pieces += [jnp.zeros((others * SUB, tiles * LANES - bands * width), f32)]
            line = jnp.concatenate(pieces, axis=1)
            for t in range(tiles):
                held_ref[p, :, t] = line[:, t * LANES : (t + 1) * LANES].reshape(others, SUB, LANES)
            depart(p).start()
            return 0

        lax.fori_loop(0, groups, leave, 0)
        for p in range(groups):
            depart(p).wait()

    anywhere = pl.BlockSpec(memory_space=pltpu.HBM)
    flops = 6 * (4 * groups * width * G * length + 24 * kept * length * G * length)
    return pl.pallas_call(
        kernel,
        out_shape=jax.ShapeDtypeStruct(lines.shape, f32),
        in_specs=[pl.BlockSpec(memory_space=pltpu.SMEM)] + [anywhere] * 4,
        out_specs=anywhere,
        scratch_shapes=[
            pltpu.VMEM(lines.shape, f32),
            *(pltpu.VMEM(table.shape, table.dtype) for table in tables),
            pltpu.SemaphoreType.DMA((groups,)),
            pltpu.SemaphoreType.DMA((3,)),
            pltpu.VMEM((kept, 2 * G, 6 * length), bf16),
            pltpu.VMEM((length, 6 * length), f32),
            pltpu.VMEM((2 * length, 6 * length), bf16),
            pltpu.VMEM((groups, width, 2 * length), bf16),
        ],
        cost_estimate=pl.CostEstimate(
            flops=flops, bytes_accessed=8 * lines.size, transcendentals=kept * G * G
        ),
        compiler_params=pltpu.CompilerParams(vmem_limit_bytes=ALL_VMEM),
        name="planes",
    )(place, lines, *tables)


def halo(slabs):
    def shifted(piece, axis, up):
        devices = lax.axis_size(axis)
        pairs = [(i, i + 1) for i in range(devices - 1)]
        if not up:
            pairs = [(j, i) for i, j in pairs]
        return lax.ppermute(piece, axis, pairs)

    last_rows, first_rows, last_cols, first_cols = slabs
    return (
        shifted(last_cols, "py", True),
        shifted(first_cols, "py", False),
        shifted(last_rows, "px", True),
        shifted(first_rows, "px", False),
    )


def depth_weights(G):
    width = 2 * G
    at = np.arange(width) % G
    rows = []
    for k in range(width // LANES):
        for shift, weight in ((1, 8.0), (-1, -8.0), (2, -1.0), (-2, 1.0)):
            inside = (at + shift >= 0) & (at + shift < G)
            rows.append(np.where(inside, weight / 12.0, 0.0)[k * LANES : (k + 1) * LANES])
    return np.stack(rows).astype(np.float32)


def stretch(field, flow, left, right, size):
    rows, cols, G = size.rows, size.cols, size.G
    span = 2 * G // LANES
    many = cols * G // LANES
    half = LANES // 2

    def kernel(field_hbm, flow_ref, left_ref, right_ref, weight_ref, out_ref, field_ref, sem,
               ext_ref, turned_ref):
        whole = pltpu.make_async_copy(field_hbm, field_ref, sem)

        @pl.when(pl.program_id(0) == 0)
        def _():
            whole.start()
            ext_ref[:, 0:SUB, :] = jnp.zeros((many + 2 * span, SUB, LANES), f32)
            ext_ref[:, SUB + rows :, :] = jnp.zeros((many + 2 * span, SUB, LANES), f32)

        def put(t, value):
            ext_ref[t, SUB : SUB + rows, :] = value
            turned_ref[t] = pltpu.roll(value, half, 1)

        for t in range(many):
            at = slice(t * LANES, (t + 1) * LANES)
            put(span + t, flow_ref[0, :, at])
        for t in range(span):
            at = slice(t * LANES, (t + 1) * LANES)
            put(t, left_ref[0, :, at])
            put(span + many + t, right_ref[0, :, at])
        lane = lax.broadcasted_iota(jnp.int32, (ROWS, LANES), 1)

        @pl.when(pl.program_id(0) == 0)
        def _():
            whole.wait()

        def block(b, _):
            base = span * (b + 1)
            for top in range(0, rows, ROWS):
                these = slice(top, top + ROWS)

                def tall_at(t, s):
                    return ext_ref[t, SUB + top + s : SUB + top + s + ROWS, :]

                def side_at(t):
                    return jnp.where(lane < half, turned_ref[t, these, :], turned_ref[t + 1, these, :])

                own = [tall_at(base + k, 0) for k in range(span)]
                for k in range(span):
                    t = base + k
                    deep = 0.0
                    for i, s in enumerate((1, -1, 2, -2)):
                        value = pltpu.roll(own[k], (-s) % LANES, 1)
                        if s > 0 and k + 1 < span:
                            value = jnp.where(
                                lane < LANES - s, value, pltpu.roll(own[k + 1], (-s) % LANES, 1)
                            )
                        if s < 0 and k > 0:
                            value = jnp.where(
                                lane >= -s, value, pltpu.roll(own[k - 1], (-s) % LANES, 1)
                            )
                        deep = deep + weight_ref[4 * k + i : 4 * k + i + 1, :] * value
                    side = 8.0 * (side_at(t + 1) - side_at(t - 2)) - (
                        tall_at(t + span, 0) - tall_at(t - span, 0)
                    )
                    tall = 8.0 * (tall_at(t, 1) - tall_at(t, -1)) - (tall_at(t, 2) - tall_at(t, -2))
                    at = pl.ds(pl.multiple_of((span * b + k) * LANES, LANES), LANES)
                    out_ref[0, these, at] = field_ref[2, these, at] * deep + (1.0 / 12.0) * (
                        field_ref[1, these, at] * side + field_ref[0, these, at] * tall
                    )
            return 0

        lax.fori_loop(0, cols // 2, block, 0, unroll=2)

    def part(*shape):
        return pl.BlockSpec((1,) + shape, lambda i: (i, 0, 0))

    return pl.pallas_call(
        kernel,
        grid=(3,),
        out_shape=jax.ShapeDtypeStruct((3, rows, cols * G), f32),
        in_specs=[
            pl.BlockSpec(memory_space=pltpu.HBM),
            part(rows, cols * G),
            part(rows, 2 * G),
            part(rows, 2 * G),
            pl.BlockSpec((4 * span, LANES), lambda i: (0, 0)),
        ],
        out_specs=part(rows, cols * G),
        scratch_shapes=[
            pltpu.VMEM((3, rows, cols * G), f32),
            pltpu.SemaphoreType.DMA,
            pltpu.VMEM((many + 2 * span, rows + 2 * SUB, LANES), f32),
            pltpu.VMEM((many + 2 * span, rows, LANES), f32),
        ],
        cost_estimate=pl.CostEstimate(
            flops=60 * flow.size, bytes_accessed=12 * flow.size, transcendentals=0
        ),
        compiler_params=pltpu.CompilerParams(vmem_limit_bytes=MOST_VMEM),
        name="stretch",
    )(field, flow, left, right, jnp.asarray(depth_weights(G)))


def add_rows(field, part, up, down, size):
    rows, width = size.rows, size.cols * size.G
    last = rows // SUB - 1

    def kernel(field_ref, part_ref, up_ref, down_ref, out_ref):
        out_ref[...] = part_ref[...]

        def add(c, row, value):
            at = slice(row, row + 1)
            out_ref[c, at, :] = part_ref[c, at, :] + (1.0 / 12.0) * field_ref[0, at, :] * value

        @pl.when(pl.program_id(0) == 0)
        def _():
            for c in range(3):
                far, near = up_ref[c, 0:1, :], up_ref[c, 1:2, :]
                add(c, 0, far - 8.0 * near)
                add(c, 1, near)

        @pl.when(pl.program_id(0) == 1)
        def _():
            for c in range(3):
                near, far = down_ref[c, 0:1, :], down_ref[c, 1:2, :]
                add(c, SUB - 1, 8.0 * near - far)
                add(c, SUB - 2, -near)

    edge = pl.BlockSpec((3, SUB, width), lambda i: (0, i * last, 0))
    whole = pl.BlockSpec((3, 2, width), lambda i: (0, 0, 0))
    return pl.pallas_call(
        kernel,
        grid=(2,),
        out_shape=jax.ShapeDtypeStruct((3, rows, width), f32),
        in_specs=[pl.BlockSpec((1, SUB, width), lambda i: (0, i * last, 0)), edge, whole, whole],
        out_specs=edge,
        input_output_aliases={1: 0},
        cost_estimate=pl.CostEstimate(
            flops=60 * width, bytes_accessed=4 * 40 * 3 * width, transcendentals=0
        ),
        compiler_params=pltpu.CompilerParams(vmem_limit_bytes=MOST_VMEM),
        name="add_rows",
    )(field, part, up, down)


def triple(table, axis):
    high, low = split_table(table)
    return np.concatenate([high, high, low], axis=axis)


def fast(vorticity, size):
    rows, cols, G, devices, groups = size.rows, size.cols, size.G, size.devices, size.groups
    length, bands, others = size.length, size.bands, size.G // size.cols
    axes = ("px", "py")
    place = lax.axis_index(axes).astype(jnp.int32)

    cells = np.array([
        q * cols + band * SUB + s for band in range(bands) for q in range(others) for s in range(SUB)
    ])
    lane_modes, lane_kinds = lane_order(G)
    row_modes = np.concatenate([np.arange(G)] * 2)
    row_kinds = np.repeat([0, 1], G)
    line_basis = basis(G, lane_modes, lane_kinds, length)[cells]
    wide_basis = basis(G, row_modes, row_kinds, length)
    line = split_table(line_basis)
    wide = triple(wide_basis.T, 1)
    inv_wide = triple(wide_basis * weights(row_modes, length), 1)
    inv_line = triple(line_basis * weights(lane_modes, length), 1)
    kx = np.broadcast_to(waves(np.arange(G), length)[:, None], (G, LANES)).astype(np.float32)
    signs = np.where(lane_kinds == 0, 1.0, -1.0)
    signs[: 2 * (G // LANES * LANES)] = 1.0
    ky = (waves(lane_modes, length) * signs).astype(np.float32)
    waves_of = np.zeros((G, LANES + length), np.float32)
    waves_of[:, :LANES] = kx
    waves_of[:, LANES:] = ky
    narrow = np.concatenate([inv_wide, inv_line, *line], axis=1)
    tables = tuple(jnp.asarray(t) for t in (narrow, wide, waves_of))

    def depth_tables(start, kept):
        modes = np.array([
            (start + j) * devices + d
            for j in range(kept) for k in (0, 1) for d in range(devices)
        ])
        kinds = np.array([k for j in range(kept) for k in (0, 1) for d in range(devices)])
        table = basis(G, modes, kinds, length)
        spare = ((0, 0), (0, size.spare)), ((0, 0), (size.spare, 0))

        def both(rows_of):
            return jnp.asarray(np.stack([np.stack(split_table(np.pad(rows_of, pad))) for pad in spare]))

        return both(table.T), both((table * weights(modes, length)).T)

    def exchange(value):
        value = value.reshape(devices, -1, LANES)
        return lax.all_to_all(value, axes, split_axis=0, concat_axis=0, tiled=True)

    arrived = []
    for start, kept in size.chunks:
        arrived.append(exchange(depth_forward(vorticity, depth_tables(start, kept)[0], size, kept)))
    returned = []
    for (start, kept), lines in zip(size.chunks, arrived):
        lines = lines.reshape(groups, others, size.tiles(kept), SUB, LANES)
        where = jnp.stack([place, jnp.int32(start)])
        returned.append(exchange(planes(lines, where, tables, size, kept)))
    flow = None
    for (start, kept), lines in zip(size.chunks, returned):
        last = start + kept == G // devices
        flow, *slabs = depth_inverse(
            lines.reshape(-1, LANES), depth_tables(start, kept)[1], flow, size, kept, last
        )
    left, right, up, down = halo(slabs)
    part = stretch(vorticity, flow, left, right, size)
    return flow, add_rows(vorticity, part, up, down, size)


def with_halo(shard, sides, width):
    for axis, dim in sides:
        devices, length = (lax.axis_size(axis), shard.shape[dim])
        up = [(i, (i + 1) % devices) for i in range(devices - 1)]
        down = [(j, i) for i, j in up]
        last = lax.slice_in_dim(shard, length - width, length, axis=dim)
        leading = lax.slice_in_dim(shard, 0, width, axis=dim)
        before = lax.ppermute(last, axis, up)
        after = lax.ppermute(leading, axis, down)
        shard = jnp.concatenate([before, shard, after], axis=dim)
    return shard


def twiddle(count_in, count_out, length, factor):
    source = lax.broadcasted_iota(jnp.int32, (count_in, count_out), 0)
    target = lax.broadcasted_iota(jnp.int32, (count_in, count_out), 1)
    angle = (source * target % length).astype(jnp.float32) * (2.0 * math.pi / length)
    cosine = jnp.cos(angle) * factor
    sine = jnp.sin(angle) * factor
    return (
        jnp.broadcast_to(cosine, (3, count_in, count_out)),
        jnp.broadcast_to(sine, (3, count_in, count_out)),
    )


def product(einsum_form, first, second):
    return jnp.einsum(einsum_form, first, second, precision=highest)


def forward_left(pair, einsum_form, tables):
    real_part, imag_part = pair
    cosine_table, sine_table = tables
    return (
        product(einsum_form, cosine_table, real_part) + product(einsum_form, sine_table, imag_part),
        product(einsum_form, cosine_table, imag_part) - product(einsum_form, sine_table, real_part),
    )


def forward_right(pair, einsum_form, tables):
    real_part, imag_part = pair
    cosine_table, sine_table = tables
    return (
        product(einsum_form, real_part, cosine_table) + product(einsum_form, imag_part, sine_table),
        product(einsum_form, imag_part, cosine_table) - product(einsum_form, real_part, sine_table),
    )


def backward_left(pair, einsum_form, tables):
    real_part, imag_part = pair
    cosine_table, sine_table = tables
    return (
        product(einsum_form, cosine_table, real_part) - product(einsum_form, sine_table, imag_part),
        product(einsum_form, cosine_table, imag_part) + product(einsum_form, sine_table, real_part),
    )


def wavenumbers(start, count, length, position):
    index = start + lax.iota(jnp.int32, count)
    signed = jnp.where(index < length // 2, index, index - length)
    wave = signed.astype(jnp.float32) * (2.0 * math.pi / length)
    slope = jnp.where(index == length // 2, 0.0, wave)
    keep = jnp.where(index == length // 2, 0.0, 1.0)
    shape = [1, 1, 1, 1]
    shape[position] = count
    return (wave.reshape(shape), slope.reshape(shape), keep.reshape(shape))


def velocity_spectrum(pair, waves_x, waves_y, waves_z):
    square = waves_x[0] ** 2 + waves_y[0] ** 2 + waves_z[0] ** 2
    mask = waves_x[2] * waves_y[2] * waves_z[2]
    green = (
        mask
        * jnp.exp(-0.5 * smoothing * smoothing * square)
        / (square + jnp.where(square == 0.0, 1.0, 0.0))
    )
    slope_x, slope_y, slope_z = (waves_x[1][0], waves_y[1][0], waves_z[1][0])

    def curl(field):
        return jnp.stack(
            [
                slope_y * field[2] - slope_z * field[1],
                slope_z * field[0] - slope_x * field[2],
                slope_x * field[1] - slope_y * field[0],
            ]
        )

    real_part = pair[0] * green
    imag_part = pair[1] * green
    return (jnp.swapaxes(-curl(imag_part), 1, 2), jnp.swapaxes(curl(real_part), 1, 2))


def window(padded, axis, offset):
    starts = [0, 2, 2, 2]
    limits = [padded.shape[0], padded.shape[1] - 2, padded.shape[2] - 2, padded.shape[3] - 2]
    starts[axis] = starts[axis] + offset
    limits[axis] = limits[axis] + offset
    return lax.slice(padded, starts, limits)


def derivative(padded, axis):
    near = window(padded, axis, 1) - window(padded, axis, -1)
    far = window(padded, axis, 2) - window(padded, axis, -2)
    return (8.0 * near - far) / 12.0


def general(vorticity):
    block_rows = vorticity.shape[1]
    G = block_rows * lax.axis_size("px")
    block_cols = vorticity.shape[2] // G
    field = vorticity.reshape(3, block_rows, block_cols, G)
    length = 2 * G
    depth_tables = twiddle(G, G, length, 1.0)
    line_tables = twiddle(G, length, length, 1.0)
    inverse_tables = twiddle(length, G, length, 1.0 / length)
    closing = twiddle(G, G, length, 1.0 / length)
    weights = jnp.where(lax.iota(jnp.int32, G) == 0, 1.0, 2.0)[None, :, None]
    closing_cos = closing[0] * weights
    closing_sin = closing[1] * weights
    pair = (
        product("czk,cxyz->ckxy", depth_tables[0], field),
        -product("czk,cxyz->ckxy", depth_tables[1], field),
    )
    pair = (
        lax.all_to_all(pair[0], "py", split_axis=1, concat_axis=3, tiled=True),
        lax.all_to_all(pair[1], "py", split_axis=1, concat_axis=3, tiled=True),
    )
    pair = forward_left(pair, "cyl,ckxy->clkx", line_tables)
    pair = (
        lax.all_to_all(pair[0], "px", split_axis=1, concat_axis=3, tiled=True),
        lax.all_to_all(pair[1], "px", split_axis=1, concat_axis=3, tiled=True),
    )
    pair = forward_right(pair, "clkx,cxm->clkm", line_tables)
    rows = pair[0].shape[1]
    depth = pair[0].shape[2]
    waves_y = wavenumbers(lax.axis_index("px") * rows, rows, length, 1)
    waves_z = wavenumbers(lax.axis_index("py") * depth, depth, length, 2)
    waves_x = wavenumbers(0, length, length, 3)
    pair = velocity_spectrum(pair, waves_x, waves_y, waves_z)
    pair = backward_left(pair, "cmx,cklm->cxkl", inverse_tables)
    pair = (
        lax.all_to_all(pair[0], "px", split_axis=1, concat_axis=3, tiled=True),
        lax.all_to_all(pair[1], "px", split_axis=1, concat_axis=3, tiled=True),
    )
    pair = backward_left(pair, "cly,cxkl->cyxk", inverse_tables)
    pair = (
        lax.all_to_all(pair[0], "py", split_axis=1, concat_axis=3, tiled=True),
        lax.all_to_all(pair[1], "py", split_axis=1, concat_axis=3, tiled=True),
    )
    flow = product("cyxk,ckz->cyxz", pair[0], closing_cos) - product(
        "cyxk,ckz->cyxz", pair[1], closing_sin
    )
    flow = jnp.swapaxes(flow, 1, 2)
    padded = with_halo(flow, (("px", 1), ("py", 2)), 2)
    padded = jnp.pad(padded, ((0, 0), (0, 0), (0, 0), (2, 2)))
    stretching = (
        field[0] * derivative(padded, 1)
        + field[1] * derivative(padded, 2)
        + field[2] * derivative(padded, 3)
    )
    return (
        flow.reshape(3, block_rows, block_cols * G),
        stretching.reshape(3, block_rows, block_cols * G),
    )


def on_device(vorticity):
    sizes = fast_sizes(vorticity)
    if sizes is None:
        return general(vorticity)
    return fast(vorticity, sizes)


def solution(mesh):
    in_specs = (P(None, "px", "py"),)
    out_specs = (P(None, "px", "py"), P(None, "px", "py"))
    return jax.shard_map(
        on_device, mesh=mesh, in_specs=in_specs, out_specs=out_specs, check_vma=False
    )
```

```python
import math

import jax
import jax.numpy as jnp
import numpy as np
from jax import lax
from jax.experimental import pallas as pl
from jax.experimental.pallas import tpu as pltpu
from jax.sharding import PartitionSpec as P


smoothing = 1.0
highest = lax.Precision.HIGHEST
f32 = jnp.float32
bf16 = jnp.bfloat16
LANES = 128
SUB = 8
ROWS = 16
ALL_VMEM, MOST_VMEM, LESS_VMEM = 67_000_000, 56_000_000, 50_000_000


def split_table(table):
    high = table.astype(np.float32).astype(jnp.bfloat16)
    low = (table - high.astype(np.float64)).astype(np.float32).astype(jnp.bfloat16)
    return high, low


def waves(modes, length):
    return np.asarray(modes, np.float64) * (2.0 * math.pi / length)


def basis(points, modes, kinds, length):
    angle = (np.arange(points)[:, None] * np.asarray(modes)[None, :] % length) * (
        2.0 * math.pi / length
    )
    return np.where(np.asarray(kinds)[None, :] == 0, np.cos(angle), np.sin(angle))


def weights(modes, length):
    return np.where(np.asarray(modes) == 0, 1.0, 2.0) / length


def lane_order(modes):
    full = modes // LANES * LANES
    index, kind = [], []
    for start in range(0, full, LANES):
        for k in (0, 1):
            index += list(range(start, start + LANES))
            kind += [k] * LANES
    for k in (0, 1):
        index += list(range(full, modes))
        kind += [k] * (modes - full)
    return np.array(index), np.array(kind)


def dot(first, second, dims):
    return lax.dot_general(first, second, (dims, ((), ())), preferred_element_type=f32)


NN = ((1,), (0,))
NT = ((1,), (1,))
TN = ((0,), (0,))


def halves(value):
    high = value.astype(bf16)
    low = (value - high.astype(f32)).astype(bf16)
    return high, low


class Sizes:
    def __init__(self, rows, cols, G, devices, groups):
        self.rows, self.cols, self.G = rows, cols, G
        self.devices, self.groups = devices, groups
        self.bands = cols // SUB
        self.spare = G % LANES
        self.span = G + self.spare
        self.side = -(-cols // 2 * rows // LANES) * LANES
        self.length = 2 * G
        total = G // devices
        first = max(1, total // 3)
        self.chunks = [(0, first), (first, total - first)] if total > first else [(0, first)]

    def line(self, y):
        return (y // 2 + SUB // 2 * (y % 2)) % (self.cols // 2) * self.rows

    def slot(self, y):
        return y % 2 * self.side + self.line(y)

    def units(self, kept):
        return 6 * kept

    def tiles(self, kept):
        return -(-self.bands * self.units(kept) * self.rows // LANES)


def fast_sizes(vorticity):
    rows = vorticity.shape[1]
    groups = lax.axis_size("px")
    G = rows * groups
    cols = vorticity.shape[2] // G
    devices = groups * lax.axis_size("py")
    if rows % 16 or rows * cols % LANES or cols % (2 * SUB) not in (0, SUB) or cols % SUB or cols % 2:
        return None
    if G % devices or devices % SUB or G % LANES != LANES // 2:
        return None
    return Sizes(rows, cols, G, devices, groups)


class LaneMoves:
    def __init__(self, fragments):
        self.merged = []
        self.wanted = {}
        open_groups = {}
        for dest, to, source, start, width in fragments:
            at = to
            shift = (to - start) % LANES
            while at < to + width:
                origin = at - to + start
                take = min(to + width - at, LANES - origin % LANES)
                group = self._place(open_groups, origin // LANES, shift, origin % LANES, take, source)
                end = at + take
                while at < end:
                    part = min(end - at, LANES - at % LANES)
                    self.wanted.setdefault((dest, at // LANES), []).append((at % LANES, group))
                    at += part

    def _place(self, open_groups, tile, shift, lane, width, source):
        for group in open_groups.setdefault((tile, shift), []):
            pieces = self.merged[group][2]
            if all(lane >= at + wide or at >= lane + width for at, wide, _ in pieces):
                pieces.append((lane, width, source))
                return group
        self.merged.append((tile, shift, [(lane, width, source)]))
        open_groups[tile, shift].append(len(self.merged) - 1)
        return len(self.merged) - 1

    def run(self, load, store, held, shape):
        lane = lax.broadcasted_iota(jnp.int32, shape, 1)

        def choose(parts):
            value = None
            for at, part in sorted(parts, key=lambda pair: pair[0]):
                value = part() if value is None else jnp.where(lane >= at, part(), value)
            return value

        for index, (tile, shift, pieces) in enumerate(self.merged):
            value = choose(
                [(at, lambda source=source, tile=tile: load(source, tile)) for at, _, source in pieces]
            )
            held[index] = pltpu.roll(value, shift, 1) if shift else value
        for (dest, tile), parts in self.wanted.items():
            store(dest, tile, choose([(at, lambda index=index: held[index]) for at, index in parts]))


def depth_forward(shard, table, size, kept):
    rows, cols, G, devices = size.rows, size.cols, size.G, size.devices
    units, tiles, bands = size.units(kept), size.tiles(kept), size.bands
    block = 2 * kept * devices
    half = cols // 2 * rows
    moves = LaneMoves([
        (s, (band * units + u) * rows, u, size.slot(SUB * band + s), rows)
        for s in range(SUB)
        for band in range(bands)
        for u in range(units)
    ])

    def kernel(shard_ref, table_ref, out_ref, held_ref, sems, high_ref, low_ref, mid_ref, turned_ref):
        def fetch(c):
            return pltpu.make_async_copy(shard_ref.at[c], held_ref.at[c], sems.at[c])

        for c in range(3):
            fetch(c).start()

        for c in range(3):
            fetch(c).wait()
            for y in range(cols):
                odd, to = y % 2, size.line(y)
                start = y * G - odd * size.spare
                high, low = halves(held_ref[c, :, start : start + size.span])
                high_ref[c, odd, to : to + rows, :] = high
                low_ref[c, odd, to : to + rows, :] = low
        for c in range(3):
            for odd in (0, 1):
                at = odd * size.side
                mid_ref[c * block : (c + 1) * block, at : at + half] = (
                    dot(table_ref[odd, 0], high_ref[c, odd], NT)
                    + dot(table_ref[odd, 0], low_ref[c, odd], NT)
                    + dot(table_ref[odd, 1], high_ref[c, odd], NT)
                )

        def load(u, t):
            return mid_ref[u * devices : (u + 1) * devices, t * LANES : (t + 1) * LANES]

        def store(s, t, value):
            out_ref[pl.ds(t * SUB + s, devices, stride=tiles * SUB), :] = value

        moves.run(load, store, turned_ref, (devices, LANES))

    return pl.pallas_call(
        kernel,
        out_shape=jax.ShapeDtypeStruct((devices * tiles * SUB, LANES), f32),
        in_specs=[pl.BlockSpec(memory_space=pltpu.HBM), pl.BlockSpec(memory_space=pltpu.VMEM)],
        out_specs=pl.BlockSpec(memory_space=pltpu.VMEM),
        scratch_shapes=[
            pltpu.VMEM((3, rows, cols * G), f32),
            pltpu.SemaphoreType.DMA((3,)),
            pltpu.VMEM((3, 2, half, size.span), bf16),
            pltpu.VMEM((3, 2, half, size.span), bf16),
            pltpu.VMEM((3 * block, 2 * size.side), f32),
            pltpu.VMEM((len(moves.merged), devices, LANES), f32),
        ],
        cost_estimate=pl.CostEstimate(
            flops=18 * block * G * rows * cols,
            bytes_accessed=4 * (3 * rows * cols * G + devices * tiles * SUB * LANES),
            transcendentals=0,
        ),
        compiler_params=pltpu.CompilerParams(vmem_limit_bytes=ALL_VMEM),
        name="depth_forward",
    )(shard, table)


def depth_inverse(lines, table, before, size, kept, slabs):
    rows, cols, G, devices = size.rows, size.cols, size.G, size.devices
    units, tiles, bands = size.units(kept), size.tiles(kept), size.bands
    block = 2 * kept * devices
    half = cols // 2 * rows
    share = SUB * tiles * SUB
    extra = [] if before is None else [before]
    anywhere = pl.BlockSpec(memory_space=pltpu.HBM)
    whole = pl.BlockSpec(memory_space=pltpu.VMEM)
    moves = LaneMoves([
        (u, size.slot(SUB * band + s), s, (band * units + u) * rows, rows)
        for u in range(units)
        for band in range(bands)
        for s in range(SUB)
    ])
    outs = [jax.ShapeDtypeStruct((3, rows, cols * G), f32)]
    if slabs:
        outs += [jax.ShapeDtypeStruct((3, 2, cols * G), f32)] * 2
        outs += [jax.ShapeDtypeStruct((3, rows, 2 * G), f32)] * 2

    def kernel(lines_ref, table_ref, *refs):
        out_ref, *slab_refs = refs[len(extra) : len(extra) + len(outs)]
        held_ref, ready_ref, mid_ref, turned_ref, done_ref, came, had, gone = refs[
            len(extra) + len(outs) :
        ]

        def arrive(g):
            at = pl.ds(g * share, share)
            return pltpu.make_async_copy(lines_ref.at[at], held_ref.at[at], came.at[g])

        def earlier(c):
            return pltpu.make_async_copy(refs[0].at[c], ready_ref.at[c], had.at[c])

        def leave(c):
            return pltpu.make_async_copy(ready_ref.at[c], out_ref.at[c], gone.at[c])

        for g in range(devices // SUB):
            arrive(g).start()
        for g in range(devices // SUB):
            arrive(g).wait()

            def load(s, t):
                return held_ref[pl.ds(g * share + t * SUB + s, SUB, stride=tiles * SUB), :]

            def store(u, t, value):
                to = u * devices + g * SUB
                mid_ref[to : to + SUB, t * LANES : (t + 1) * LANES] = value

            moves.run(load, store, turned_ref.at[g], (SUB, LANES))

        if extra:
            for c in range(3):
                earlier(c).start()
        for c in range(3):
            for odd in (0, 1):
                at = odd * size.side
                high, low = halves(mid_ref[c * block : (c + 1) * block, at : at + half].T)
                done_ref[c, odd] = (
                    dot(high, table_ref[odd, 0], NN)
                    + dot(low, table_ref[odd, 0], NN)
                    + dot(high, table_ref[odd, 1], NN)
                )
        if extra:
            for c in range(3):
                earlier(c).wait()
        for c in range(3):
            for y in range(0, cols, 2):
                even = done_ref[c, 0, size.line(y) : size.line(y) + rows, :]
                odd = done_ref[c, 1, size.line(y + 1) : size.line(y + 1) + rows, :]
                shared = size.span - 2 * size.spare
                pair = jnp.concatenate(
                    [
                        even[:, :shared],
                        even[:, shared:] + odd[:, : 2 * size.spare],
                        odd[:, 2 * size.spare :],
                    ],
                    axis=1,
                )
                if extra:
                    pair = pair + ready_ref[c, :, y * G : (y + 2) * G]
                ready_ref[c, :, y * G : (y + 2) * G] = pair
                if slabs:
                    slab_refs[0][c, :, y * G : (y + 2) * G] = pair[rows - 2 :, :]
                    slab_refs[1][c, :, y * G : (y + 2) * G] = pair[:2, :]
                if slabs and y == cols - 2:
                    slab_refs[2][c] = pair
                if slabs and y == 0:
                    slab_refs[3][c] = pair
            leave(c).start()
        for c in range(3):
            leave(c).wait()

    return pl.pallas_call(
        kernel,
        out_shape=outs,
        in_specs=[anywhere, whole] + [anywhere] * len(extra),
        out_specs=[anywhere] + [whole] * (len(outs) - 1),
        scratch_shapes=[
            pltpu.VMEM((devices * tiles * SUB, LANES), f32),
            pltpu.VMEM((3, rows, cols * G), f32),
            pltpu.VMEM((3 * block, 2 * size.side), f32),
            pltpu.VMEM((devices // SUB, len(moves.merged), SUB, LANES), f32),
            pltpu.VMEM((3, 2, half, size.span), f32),
            pltpu.SemaphoreType.DMA((devices // SUB,)),
            pltpu.SemaphoreType.DMA((3,)),
            pltpu.SemaphoreType.DMA((3,)),
        ],
        cost_estimate=pl.CostEstimate(
            flops=18 * block * G * rows * cols,
            bytes_accessed=4 * (9 * rows * cols * G + devices * tiles * SUB * LANES),
            transcendentals=0,
        ),
        compiler_params=pltpu.CompilerParams(vmem_limit_bytes=LESS_VMEM),
        name="depth_inverse",
    )(lines, table, *extra)


def planes(lines, place, tables, size, kept):
    rows, cols, G, devices, groups = size.rows, size.cols, size.G, size.devices, size.groups
    units, tiles, bands, length = size.units(kept), size.tiles(kept), size.bands, size.length
    width = units * rows
    step = 16
    unit_wave = 2.0 * math.pi / length
    full = G // LANES * LANES
    others = G // cols

    def kernel(place_ref, lines_ref, narrow_hbm, wide_hbm, waves_hbm, out_ref, held_ref, narrow_ref,
               wide_ref, waves_ref, came, told, left_ref, spec_ref, turned_ref, back_ref):
        inv_wide_ref = narrow_ref.at[:, : 3 * length]
        inv_line_ref = narrow_ref.at[:, 3 * length : 6 * length]
        line_high = narrow_ref.at[:, 6 * length : 7 * length]
        line_low = narrow_ref.at[:, 7 * length :]
        kx_ref = waves_ref.at[:, :LANES]
        ky_ref = waves_ref.at[:, LANES:]

        def come(p):
            return pltpu.make_async_copy(lines_ref.at[p], held_ref.at[p], came.at[p])

        def tell(i):
            source = (narrow_hbm, wide_hbm, waves_hbm)[i]
            return pltpu.make_async_copy(source, (narrow_ref, wide_ref, waves_ref)[i], told.at[i])

        tell(0).start()
        for p in range(groups):
            come(p).start()
        tell(1).start()
        tell(2).start()
        tell(0).wait()

        def arrive(p, _):
            come(p).wait()
            flat = jnp.concatenate(
                [held_ref[p, :, t].reshape(others * SUB, LANES).T for t in range(tiles)], axis=0
            )
            side = jnp.concatenate(
                [flat[band * width : (band + 1) * width, :] for band in range(bands)], axis=1
            )
            high, low = halves(side)
            done = (
                dot(high, line_high[...], NN)
                + dot(low, line_high[...], NN)
                + dot(high, line_low[...], NN)
            )
            for u in range(units):
                c, j, k = u // (2 * kept), u // 2 % kept, u % 2
                at = (2 * c + k) * length
                high, low = halves(done[u * rows : (u + 1) * rows, :])
                for part, value in ((0, high), (1, low)):
                    target = pl.ds(pl.multiple_of(part * G + p * rows, 16), rows)
                    left_ref[j, target, at : at + length] = value
            return 0

        lax.fori_loop(0, groups, arrive, 0)
        tell(1).wait()
        tell(2).wait()

        def one_depth(j, _):
            index = (place_ref[1] + j) * devices + place_ref[0]
            kz = index.astype(f32) * unit_wave

            def widen(u, _):
                at = pl.ds(pl.multiple_of(u * length, LANES), length)
                spec_ref[:, at] = dot(wide_ref[:, :length], left_ref[j, :, at], NN) + dot(
                    wide_ref[:, length:], left_ref[j, :G, at], NN
                )
                return 0

            lax.fori_loop(0, 6, widen, 0)

            def turn(r, _):
                top = pl.multiple_of(r * step, step)
                kx = kx_ref[pl.ds(top, step), :]

                def store(c, k, half, lane, value):
                    at = (2 * c + k) * length + lane
                    for part, piece in zip((0, 1), halves(value)):
                        target = pl.ds(pl.multiple_of(part * length + half * G + top, step), step)
                        turned_ref[target, at : at + LANES] = piece

                def green_of(lane):
                    ky = ky_ref[0:1, lane : lane + LANES]
                    square = kx * kx + ky * ky + kz * kz
                    return jnp.exp(-0.5 * smoothing * smoothing * square) / (
                        square + jnp.where(square == 0.0, 1.0, 0.0)
                    )

                def load(c, k, half, lane):
                    at = (2 * c + k) * length + lane
                    target = pl.ds(pl.multiple_of(half * G + top, step), step)
                    return spec_ref[target, at : at + LANES]

                def curl(lane_of, dy_of, green):
                    gx = green * kx
                    gz = green * kz
                    many = range(len(lane_of))
                    got = {
                        (c, k, h, t): load(c, k, h, lane_of[t])
                        for c in range(3) for k in (0, 1) for h in (0, 1) for t in many
                    }

                    def dx(c, k, h, t):
                        value = gx * got[c, k, 1 - h, t]
                        return value if h == 0 else -value

                    def dz(c, k, h, t):
                        value = gz * got[c, 1 - k, h, t]
                        return value if k == 0 else -value

                    def dy(c, k, h, t):
                        return dy_of(got, c, k, h, t)

                    for k in (0, 1):
                        for h in (0, 1):
                            for t in many:
                                store(0, k, h, lane_of[t], dy(2, k, h, t) - dz(1, k, h, t))
                                store(1, k, h, lane_of[t], dz(0, k, h, t) - dx(2, k, h, t))
                                store(2, k, h, lane_of[t], dx(1, k, h, t) - dy(0, k, h, t))

                for tile in range(full // LANES):
                    lane = 2 * tile * LANES
                    green = green_of(lane)
                    gy = green * ky_ref[0:1, lane : lane + LANES]

                    def dy_pair(got, c, k, h, t, gy=gy):
                        value = gy * got[c, k, h, 1 - t]
                        return value if t == 0 else -value

                    curl((lane, lane + LANES), dy_pair, green)
                if full < G:
                    lane = 2 * full
                    green = green_of(lane)
                    gy = green * ky_ref[0:1, lane : lane + LANES]

                    def dy_roll(got, c, k, h, t):
                        return gy * pltpu.roll(got[c, k, h, t], LANES // 2, 1)

                    curl((lane,), dy_roll, green)
                return 0

            lax.fori_loop(0, G // step, turn, 0)

            def narrow(u, _):
                at = pl.ds(pl.multiple_of(u * length, LANES), length)
                done = dot(inv_wide_ref[:, : 2 * length], turned_ref[:, at], NN) + dot(
                    inv_wide_ref[:, 2 * length :], turned_ref[:length, at], NN
                )
                high, low = halves(done)
                unit = (u // 2) * (2 * kept) + 2 * j + u % 2
                target = pl.ds(pl.multiple_of(unit * rows, 16), rows)
                for p in range(groups):
                    for part, value in ((0, high), (1, low)):
                        back_ref[p, target, part * length : (part + 1) * length] = value[
                            p * rows : (p + 1) * rows, :
                        ]
                return 0

            lax.fori_loop(0, 6, narrow, 0)
            return 0

        lax.fori_loop(0, kept, one_depth, 0)

        def depart(p):
            return pltpu.make_async_copy(held_ref.at[p], out_ref.at[p], came.at[p])

        def leave(p, _):
            done = dot(inv_line_ref[:, : 2 * length], back_ref[p], NT) + dot(
                inv_line_ref[:, 2 * length :], back_ref[p, :, :length], NT
            )
            pieces = [
                done[band * others * SUB : (band + 1) * others * SUB, :] for band in range(bands)
            ]
            if tiles * LANES > bands * width:
                pieces += [jnp.zeros((others * SUB, tiles * LANES - bands * width), f32)]
            line = jnp.concatenate(pieces, axis=1)
            for t in range(tiles):
                held_ref[p, :, t] = line[:, t * LANES : (t + 1) * LANES].reshape(others, SUB, LANES)
            depart(p).start()
            return 0

        lax.fori_loop(0, groups, leave, 0)
        for p in range(groups):
            depart(p).wait()

    anywhere = pl.BlockSpec(memory_space=pltpu.HBM)
    flops = 6 * (4 * groups * width * G * length + 24 * kept * length * G * length)
    return pl.pallas_call(
        kernel,
        out_shape=jax.ShapeDtypeStruct(lines.shape, f32),
        in_specs=[pl.BlockSpec(memory_space=pltpu.SMEM)] + [anywhere] * 4,
        out_specs=anywhere,
        scratch_shapes=[
            pltpu.VMEM(lines.shape, f32),
            *(pltpu.VMEM(table.shape, table.dtype) for table in tables),
            pltpu.SemaphoreType.DMA((groups,)),
            pltpu.SemaphoreType.DMA((3,)),
            pltpu.VMEM((kept, 2 * G, 6 * length), bf16),
            pltpu.VMEM((length, 6 * length), f32),
            pltpu.VMEM((2 * length, 6 * length), bf16),
            pltpu.VMEM((groups, width, 2 * length), bf16),
        ],
        cost_estimate=pl.CostEstimate(
            flops=flops, bytes_accessed=8 * lines.size, transcendentals=kept * G * G
        ),
        compiler_params=pltpu.CompilerParams(vmem_limit_bytes=ALL_VMEM),
        name="planes",
    )(place, lines, *tables)


def halo(slabs):
    def shifted(piece, axis, up):
        devices = lax.axis_size(axis)
        pairs = [(i, i + 1) for i in range(devices - 1)]
        if not up:
            pairs = [(j, i) for i, j in pairs]
        return lax.ppermute(piece, axis, pairs)

    last_rows, first_rows, last_cols, first_cols = slabs
    return (
        shifted(last_cols, "py", True),
        shifted(first_cols, "py", False),
        shifted(last_rows, "px", True),
        shifted(first_rows, "px", False),
    )


def depth_weights(G):
    width = 2 * G
    at = np.arange(width) % G
    rows = []
    for k in range(width // LANES):
        for shift, weight in ((1, 8.0), (-1, -8.0), (2, -1.0), (-2, 1.0)):
            inside = (at + shift >= 0) & (at + shift < G)
            rows.append(np.where(inside, weight / 12.0, 0.0)[k * LANES : (k + 1) * LANES])
    return np.stack(rows).astype(np.float32)


def stretch(field, flow, left, right, size):
    rows, cols, G = size.rows, size.cols, size.G
    span = 2 * G // LANES
    many = cols * G // LANES
    half = LANES // 2

    def kernel(field_hbm, flow_ref, left_ref, right_ref, weight_ref, out_ref, field_ref, sem,
               ext_ref, turned_ref):
        whole = pltpu.make_async_copy(field_hbm, field_ref, sem)

        @pl.when(pl.program_id(0) == 0)
        def _():
            whole.start()
            ext_ref[:, 0:SUB, :] = jnp.zeros((many + 2 * span, SUB, LANES), f32)
            ext_ref[:, SUB + rows :, :] = jnp.zeros((many + 2 * span, SUB, LANES), f32)

        def put(t, value):
            ext_ref[t, SUB : SUB + rows, :] = value
            turned_ref[t] = pltpu.roll(value, half, 1)

        for t in range(many):
            at = slice(t * LANES, (t + 1) * LANES)
            put(span + t, flow_ref[0, :, at])
        for t in range(span):
            at = slice(t * LANES, (t + 1) * LANES)
            put(t, left_ref[0, :, at])
            put(span + many + t, right_ref[0, :, at])
        lane = lax.broadcasted_iota(jnp.int32, (ROWS, LANES), 1)

        @pl.when(pl.program_id(0) == 0)
        def _():
            whole.wait()

        def block(b, _):
            base = span * (b + 1)
            for top in range(0, rows, ROWS):
                these = slice(top, top + ROWS)

                def tall_at(t, s):
                    return ext_ref[t, SUB + top + s : SUB + top + s + ROWS, :]

                def side_at(t):
                    return jnp.where(lane < half, turned_ref[t, these, :], turned_ref[t + 1, these, :])

                own = [tall_at(base + k, 0) for k in range(span)]
                for k in range(span):
                    t = base + k
                    deep = 0.0
                    for i, s in enumerate((1, -1, 2, -2)):
                        value = pltpu.roll(own[k], (-s) % LANES, 1)
                        if s > 0 and k + 1 < span:
                            value = jnp.where(
                                lane < LANES - s, value, pltpu.roll(own[k + 1], (-s) % LANES, 1)
                            )
                        if s < 0 and k > 0:
                            value = jnp.where(
                                lane >= -s, value, pltpu.roll(own[k - 1], (-s) % LANES, 1)
                            )
                        deep = deep + weight_ref[4 * k + i : 4 * k + i + 1, :] * value
                    side = 8.0 * (side_at(t + 1) - side_at(t - 2)) - (
                        tall_at(t + span, 0) - tall_at(t - span, 0)
                    )
                    tall = 8.0 * (tall_at(t, 1) - tall_at(t, -1)) - (tall_at(t, 2) - tall_at(t, -2))
                    at = pl.ds(pl.multiple_of((span * b + k) * LANES, LANES), LANES)
                    out_ref[0, these, at] = field_ref[2, these, at] * deep + (1.0 / 12.0) * (
                        field_ref[1, these, at] * side + field_ref[0, these, at] * tall
                    )
            return 0

        lax.fori_loop(0, cols // 2, block, 0, unroll=2)

    def part(*shape):
        return pl.BlockSpec((1,) + shape, lambda i: (i, 0, 0))

    return pl.pallas_call(
        kernel,
        grid=(3,),
        out_shape=jax.ShapeDtypeStruct((3, rows, cols * G), f32),
        in_specs=[
            pl.BlockSpec(memory_space=pltpu.HBM),
            part(rows, cols * G),
            part(rows, 2 * G),
            part(rows, 2 * G),
            pl.BlockSpec((4 * span, LANES), lambda i: (0, 0)),
        ],
        out_specs=part(rows, cols * G),
        scratch_shapes=[
            pltpu.VMEM((3, rows, cols * G), f32),
            pltpu.SemaphoreType.DMA,
            pltpu.VMEM((many + 2 * span, rows + 2 * SUB, LANES), f32),
            pltpu.VMEM((many + 2 * span, rows, LANES), f32),
        ],
        cost_estimate=pl.CostEstimate(
            flops=60 * flow.size, bytes_accessed=12 * flow.size, transcendentals=0
        ),
        compiler_params=pltpu.CompilerParams(vmem_limit_bytes=MOST_VMEM),
        name="stretch",
    )(field, flow, left, right, jnp.asarray(depth_weights(G)))


def add_rows(field, part, up, down, size):
    rows, width = size.rows, size.cols * size.G
    last = rows // SUB - 1

    def kernel(field_ref, part_ref, up_ref, down_ref, out_ref):
        out_ref[...] = part_ref[...]

        def add(c, row, value):
            at = slice(row, row + 1)
            out_ref[c, at, :] = part_ref[c, at, :] + (1.0 / 12.0) * field_ref[0, at, :] * value

        @pl.when(pl.program_id(0) == 0)
        def _():
            for c in range(3):
                far, near = up_ref[c, 0:1, :], up_ref[c, 1:2, :]
                add(c, 0, far - 8.0 * near)
                add(c, 1, near)

        @pl.when(pl.program_id(0) == 1)
        def _():
            for c in range(3):
                near, far = down_ref[c, 0:1, :], down_ref[c, 1:2, :]
                add(c, SUB - 1, 8.0 * near - far)
                add(c, SUB - 2, -near)

    edge = pl.BlockSpec((3, SUB, width), lambda i: (0, i * last, 0))
    whole = pl.BlockSpec((3, 2, width), lambda i: (0, 0, 0))
    return pl.pallas_call(
        kernel,
        grid=(2,),
        out_shape=jax.ShapeDtypeStruct((3, rows, width), f32),
        in_specs=[pl.BlockSpec((1, SUB, width), lambda i: (0, i * last, 0)), edge, whole, whole],
        out_specs=edge,
        input_output_aliases={1: 0},
        cost_estimate=pl.CostEstimate(
            flops=60 * width, bytes_accessed=4 * 40 * 3 * width, transcendentals=0
        ),
        compiler_params=pltpu.CompilerParams(vmem_limit_bytes=MOST_VMEM),
        name="add_rows",
    )(field, part, up, down)


def triple(table, axis):
    high, low = split_table(table)
    return np.concatenate([high, high, low], axis=axis)


def fast(vorticity, size):
    rows, cols, G, devices, groups = size.rows, size.cols, size.G, size.devices, size.groups
    length, bands, others = size.length, size.bands, size.G // size.cols
    axes = ("px", "py")
    place = lax.axis_index(axes).astype(jnp.int32)

    cells = np.array([
        q * cols + band * SUB + s for band in range(bands) for q in range(others) for s in range(SUB)
    ])
    lane_modes, lane_kinds = lane_order(G)
    row_modes = np.concatenate([np.arange(G)] * 2)
    row_kinds = np.repeat([0, 1], G)
    line_basis = basis(G, lane_modes, lane_kinds, length)[cells]
    wide_basis = basis(G, row_modes, row_kinds, length)
    line = split_table(line_basis)
    wide = triple(wide_basis.T, 1)
    inv_wide = triple(wide_basis * weights(row_modes, length), 1)
    inv_line = triple(line_basis * weights(lane_modes, length), 1)
    kx = np.broadcast_to(waves(np.arange(G), length)[:, None], (G, LANES)).astype(np.float32)
    signs = np.where(lane_kinds == 0, 1.0, -1.0)
    signs[: 2 * (G // LANES * LANES)] = 1.0
    ky = (waves(lane_modes, length) * signs).astype(np.float32)
    waves_of = np.zeros((G, LANES + length), np.float32)
    waves_of[:, :LANES] = kx
    waves_of[:, LANES:] = ky
    narrow = np.concatenate([inv_wide, inv_line, *line], axis=1)
    tables = tuple(jnp.asarray(t) for t in (narrow, wide, waves_of))

    def depth_tables(start, kept):
        modes = np.array([
            (start + j) * devices + d
            for j in range(kept) for k in (0, 1) for d in range(devices)
        ])
        kinds = np.array([k for j in range(kept) for k in (0, 1) for d in range(devices)])
        table = basis(G, modes, kinds, length)
        spare = ((0, 0), (0, size.spare)), ((0, 0), (size.spare, 0))

        def both(rows_of):
            return jnp.asarray(np.stack([np.stack(split_table(np.pad(rows_of, pad))) for pad in spare]))

        return both(table.T), both((table * weights(modes, length)).T)

    def exchange(value):
        value = value.reshape(devices, -1, LANES)
        return lax.all_to_all(value, axes, split_axis=0, concat_axis=0, tiled=True)

    arrived = []
    for start, kept in size.chunks:
        arrived.append(exchange(depth_forward(vorticity, depth_tables(start, kept)[0], size, kept)))
    returned = []
    for (start, kept), lines in zip(size.chunks, arrived):
        lines = lines.reshape(groups, others, size.tiles(kept), SUB, LANES)
        where = jnp.stack([place, jnp.int32(start)])
        returned.append(exchange(planes(lines, where, tables, size, kept)))
    flow = None
    for (start, kept), lines in zip(size.chunks, returned):
        last = start + kept == G // devices
        flow, *slabs = depth_inverse(
            lines.reshape(-1, LANES), depth_tables(start, kept)[1], flow, size, kept, last
        )
    left, right, up, down = halo(slabs)
    part = stretch(vorticity, flow, left, right, size)
    return flow, add_rows(vorticity, part, up, down, size)


def with_halo(shard, sides, width):
    for axis, dim in sides:
        devices, length = (lax.axis_size(axis), shard.shape[dim])
        up = [(i, (i + 1) % devices) for i in range(devices - 1)]
        down = [(j, i) for i, j in up]
        last = lax.slice_in_dim(shard, length - width, length, axis=dim)
        leading = lax.slice_in_dim(shard, 0, width, axis=dim)
        before = lax.ppermute(last, axis, up)
        after = lax.ppermute(leading, axis, down)
        shard = jnp.concatenate([before, shard, after], axis=dim)
    return shard


def twiddle(count_in, count_out, length, factor):
    source = lax.broadcasted_iota(jnp.int32, (count_in, count_out), 0)
    target = lax.broadcasted_iota(jnp.int32, (count_in, count_out), 1)
    angle = (source * target % length).astype(jnp.float32) * (2.0 * math.pi / length)
    cosine = jnp.cos(angle) * factor
    sine = jnp.sin(angle) * factor
    return (
        jnp.broadcast_to(cosine, (3, count_in, count_out)),
        jnp.broadcast_to(sine, (3, count_in, count_out)),
    )


def product(einsum_form, first, second):
    return jnp.einsum(einsum_form, first, second, precision=highest)


def forward_left(pair, einsum_form, tables):
    real_part, imag_part = pair
    cosine_table, sine_table = tables
    return (
        product(einsum_form, cosine_table, real_part) + product(einsum_form, sine_table, imag_part),
        product(einsum_form, cosine_table, imag_part) - product(einsum_form, sine_table, real_part),
    )


def forward_right(pair, einsum_form, tables):
    real_part, imag_part = pair
    cosine_table, sine_table = tables
    return (
        product(einsum_form, real_part, cosine_table) + product(einsum_form, imag_part, sine_table),
        product(einsum_form, imag_part, cosine_table) - product(einsum_form, real_part, sine_table),
    )


def backward_left(pair, einsum_form, tables):
    real_part, imag_part = pair
    cosine_table, sine_table = tables
    return (
        product(einsum_form, cosine_table, real_part) - product(einsum_form, sine_table, imag_part),
        product(einsum_form, cosine_table, imag_part) + product(einsum_form, sine_table, real_part),
    )


def wavenumbers(start, count, length, position):
    index = start + lax.iota(jnp.int32, count)
    signed = jnp.where(index < length // 2, index, index - length)
    wave = signed.astype(jnp.float32) * (2.0 * math.pi / length)
    slope = jnp.where(index == length // 2, 0.0, wave)
    keep = jnp.where(index == length // 2, 0.0, 1.0)
    shape = [1, 1, 1, 1]
    shape[position] = count
    return (wave.reshape(shape), slope.reshape(shape), keep.reshape(shape))


def velocity_spectrum(pair, waves_x, waves_y, waves_z):
    square = waves_x[0] ** 2 + waves_y[0] ** 2 + waves_z[0] ** 2
    mask = waves_x[2] * waves_y[2] * waves_z[2]
    green = (
        mask
        * jnp.exp(-0.5 * smoothing * smoothing * square)
        / (square + jnp.where(square == 0.0, 1.0, 0.0))
    )
    slope_x, slope_y, slope_z = (waves_x[1][0], waves_y[1][0], waves_z[1][0])

    def curl(field):
        return jnp.stack(
            [
                slope_y * field[2] - slope_z * field[1],
                slope_z * field[0] - slope_x * field[2],
                slope_x * field[1] - slope_y * field[0],
            ]
        )

    real_part = pair[0] * green
    imag_part = pair[1] * green
    return (jnp.swapaxes(-curl(imag_part), 1, 2), jnp.swapaxes(curl(real_part), 1, 2))


def window(padded, axis, offset):
    starts = [0, 2, 2, 2]
    limits = [padded.shape[0], padded.shape[1] - 2, padded.shape[2] - 2, padded.shape[3] - 2]
    starts[axis] = starts[axis] + offset
    limits[axis] = limits[axis] + offset
    return lax.slice(padded, starts, limits)


def derivative(padded, axis):
    near = window(padded, axis, 1) - window(padded, axis, -1)
    far = window(padded, axis, 2) - window(padded, axis, -2)
    return (8.0 * near - far) / 12.0


def general(vorticity):
    block_rows = vorticity.shape[1]
    G = block_rows * lax.axis_size("px")
    block_cols = vorticity.shape[2] // G
    field = vorticity.reshape(3, block_rows, block_cols, G)
    length = 2 * G
    depth_tables = twiddle(G, G, length, 1.0)
    line_tables = twiddle(G, length, length, 1.0)
    inverse_tables = twiddle(length, G, length, 1.0 / length)
    closing = twiddle(G, G, length, 1.0 / length)
    weights = jnp.where(lax.iota(jnp.int32, G) == 0, 1.0, 2.0)[None, :, None]
    closing_cos = closing[0] * weights
    closing_sin = closing[1] * weights
    pair = (
        product("czk,cxyz->ckxy", depth_tables[0], field),
        -product("czk,cxyz->ckxy", depth_tables[1], field),
    )
    pair = (
        lax.all_to_all(pair[0], "py", split_axis=1, concat_axis=3, tiled=True),
        lax.all_to_all(pair[1], "py", split_axis=1, concat_axis=3, tiled=True),
    )
    pair = forward_left(pair, "cyl,ckxy->clkx", line_tables)
    pair = (
        lax.all_to_all(pair[0], "px", split_axis=1, concat_axis=3, tiled=True),
        lax.all_to_all(pair[1], "px", split_axis=1, concat_axis=3, tiled=True),
    )
    pair = forward_right(pair, "clkx,cxm->clkm", line_tables)
    rows = pair[0].shape[1]
    depth = pair[0].shape[2]
    waves_y = wavenumbers(lax.axis_index("px") * rows, rows, length, 1)
    waves_z = wavenumbers(lax.axis_index("py") * depth, depth, length, 2)
    waves_x = wavenumbers(0, length, length, 3)
    pair = velocity_spectrum(pair, waves_x, waves_y, waves_z)
    pair = backward_left(pair, "cmx,cklm->cxkl", inverse_tables)
    pair = (
        lax.all_to_all(pair[0], "px", split_axis=1, concat_axis=3, tiled=True),
        lax.all_to_all(pair[1], "px", split_axis=1, concat_axis=3, tiled=True),
    )
    pair = backward_left(pair, "cly,cxkl->cyxk", inverse_tables)
    pair = (
        lax.all_to_all(pair[0], "py", split_axis=1, concat_axis=3, tiled=True),
        lax.all_to_all(pair[1], "py", split_axis=1, concat_axis=3, tiled=True),
    )
    flow = product("cyxk,ckz->cyxz", pair[0], closing_cos) - product(
        "cyxk,ckz->cyxz", pair[1], closing_sin
    )
    flow = jnp.swapaxes(flow, 1, 2)
    padded = with_halo(flow, (("px", 1), ("py", 2)), 2)
    padded = jnp.pad(padded, ((0, 0), (0, 0), (0, 0), (2, 2)))
    stretching = (
        field[0] * derivative(padded, 1)
        + field[1] * derivative(padded, 2)
        + field[2] * derivative(padded, 3)
    )
    return (
        flow.reshape(3, block_rows, block_cols * G),
        stretching.reshape(3, block_rows, block_cols * G),
    )


def on_device(vorticity):
    sizes = fast_sizes(vorticity)
    if sizes is None:
        return general(vorticity)
    return fast(vorticity, sizes)


def solution(mesh):
    in_specs = (P(None, "px", "py"),)
    out_specs = (P(None, "px", "py"), P(None, "px", "py"))
    return jax.shard_map(
        on_device, mesh=mesh, in_specs=in_specs, out_specs=out_specs, check_vma=False
    )
```

```python
import math

import jax
import jax.numpy as jnp
import numpy as np
from jax import lax
from jax.experimental import pallas as pl
from jax.experimental.pallas import tpu as pltpu
from jax.sharding import PartitionSpec as P


smoothing = 1.0
highest = lax.Precision.HIGHEST
f32 = jnp.float32
bf16 = jnp.bfloat16
LANES = 128
SUB = 8
ROWS = 16
ALL_VMEM, MOST_VMEM, LESS_VMEM = 67_000_000, 50_000_000, 50_000_000


def split_table(table):
    high = table.astype(np.float32).astype(jnp.bfloat16)
    low = (table - high.astype(np.float64)).astype(np.float32).astype(jnp.bfloat16)
    return high, low


def waves(modes, length):
    return np.asarray(modes, np.float64) * (2.0 * math.pi / length)


def basis(points, modes, kinds, length):
    angle = (np.arange(points)[:, None] * np.asarray(modes)[None, :] % length) * (
        2.0 * math.pi / length
    )
    return np.where(np.asarray(kinds)[None, :] == 0, np.cos(angle), np.sin(angle))


def weights(modes, length):
    return np.where(np.asarray(modes) == 0, 1.0, 2.0) / length


def lane_order(modes):
    full = modes // LANES * LANES
    index, kind = [], []
    for start in range(0, full, LANES):
        for k in (0, 1):
            index += list(range(start, start + LANES))
            kind += [k] * LANES
    for k in (0, 1):
        index += list(range(full, modes))
        kind += [k] * (modes - full)
    return np.array(index), np.array(kind)


def dot(first, second, dims):
    return lax.dot_general(first, second, (dims, ((), ())), preferred_element_type=f32)


NN = ((1,), (0,))
NT = ((1,), (1,))
TN = ((0,), (0,))


def halves(value):
    high = value.astype(bf16)
    low = (value - high.astype(f32)).astype(bf16)
    return high, low


class Sizes:
    def __init__(self, rows, cols, G, devices, groups):
        self.rows, self.cols, self.G = rows, cols, G
        self.devices, self.groups = devices, groups
        self.bands = cols // SUB
        self.spare = G % LANES
        self.span = G + self.spare
        self.side = -(-cols // 2 * rows // LANES) * LANES
        self.length = 2 * G
        total = G // devices
        first = max(1, total // 3)
        self.chunks = [(0, first), (first, total - first)] if total > first else [(0, first)]

    def line(self, y):
        return (y // 2 + SUB // 2 * (y % 2)) % (self.cols // 2) * self.rows

    def slot(self, y):
        return y % 2 * self.side + self.line(y)

    def units(self, kept):
        return 6 * kept

    def tiles(self, kept):
        return -(-self.bands * self.units(kept) * self.rows // LANES)


def fast_sizes(vorticity):
    rows = vorticity.shape[1]
    groups = lax.axis_size("px")
    G = rows * groups
    cols = vorticity.shape[2] // G
    devices = groups * lax.axis_size("py")
    if rows % 16 or rows * cols % LANES or cols % (2 * SUB) not in (0, SUB) or cols % SUB or cols % 2:
        return None
    if G % devices or devices % SUB or G % LANES != LANES // 2:
        return None
    return Sizes(rows, cols, G, devices, groups)


class LaneMoves:
    def __init__(self, fragments):
        self.merged = []
        self.wanted = {}
        open_groups = {}
        for dest, to, source, start, width in fragments:
            at = to
            shift = (to - start) % LANES
            while at < to + width:
                origin = at - to + start
                take = min(to + width - at, LANES - origin % LANES)
                group = self._place(open_groups, origin // LANES, shift, origin % LANES, take, source)
                end = at + take
                while at < end:
                    part = min(end - at, LANES - at % LANES)
                    self.wanted.setdefault((dest, at // LANES), []).append((at % LANES, group))
                    at += part

    def _place(self, open_groups, tile, shift, lane, width, source):
        for group in open_groups.setdefault((tile, shift), []):
            pieces = self.merged[group][2]
            if all(lane >= at + wide or at >= lane + width for at, wide, _ in pieces):
                pieces.append((lane, width, source))
                return group
        self.merged.append((tile, shift, [(lane, width, source)]))
        open_groups[tile, shift].append(len(self.merged) - 1)
        return len(self.merged) - 1

    def run(self, load, store, held, shape):
        lane = lax.broadcasted_iota(jnp.int32, shape, 1)

        def choose(parts):
            value = None
            for at, part in sorted(parts, key=lambda pair: pair[0]):
                value = part() if value is None else jnp.where(lane >= at, part(), value)
            return value

        for index, (tile, shift, pieces) in enumerate(self.merged):
            value = choose(
                [(at, lambda source=source, tile=tile: load(source, tile)) for at, _, source in pieces]
            )
            held[index] = pltpu.roll(value, shift, 1) if shift else value
        for (dest, tile), parts in self.wanted.items():
            store(dest, tile, choose([(at, lambda index=index: held[index]) for at, index in parts]))


def depth_forward(shard, table, size, kept):
    rows, cols, G, devices = size.rows, size.cols, size.G, size.devices
    units, tiles, bands = size.units(kept), size.tiles(kept), size.bands
    block = 2 * kept * devices
    half = cols // 2 * rows
    moves = LaneMoves([
        (s, (band * units + u) * rows, u, size.slot(SUB * band + s), rows)
        for s in range(SUB)
        for band in range(bands)
        for u in range(units)
    ])

    def kernel(shard_ref, table_ref, out_ref, held_ref, sems, high_ref, low_ref, mid_ref, turned_ref):
        def fetch(c):
            return pltpu.make_async_copy(shard_ref.at[c], held_ref.at[c], sems.at[c])

        for c in range(3):
            fetch(c).start()

        for c in range(3):
            fetch(c).wait()
            for y in range(cols):
                odd, to = y % 2, size.line(y)
                start = y * G - odd * size.spare
                high, low = halves(held_ref[c, :, start : start + size.span])
                high_ref[c, odd, to : to + rows, :] = high
                low_ref[c, odd, to : to + rows, :] = low
        for c in range(3):
            for odd in (0, 1):
                at = odd * size.side
                mid_ref[c * block : (c + 1) * block, at : at + half] = (
                    dot(table_ref[odd, 0], high_ref[c, odd], NT)
                    + dot(table_ref[odd, 0], low_ref[c, odd], NT)
                    + dot(table_ref[odd, 1], high_ref[c, odd], NT)
                )

        def load(u, t):
            return mid_ref[u * devices : (u + 1) * devices, t * LANES : (t + 1) * LANES]

        def store(s, t, value):
            out_ref[pl.ds(t * SUB + s, devices, stride=tiles * SUB), :] = value

        moves.run(load, store, turned_ref, (devices, LANES))

    return pl.pallas_call(
        kernel,
        out_shape=jax.ShapeDtypeStruct((devices * tiles * SUB, LANES), f32),
        in_specs=[pl.BlockSpec(memory_space=pltpu.HBM), pl.BlockSpec(memory_space=pltpu.VMEM)],
        out_specs=pl.BlockSpec(memory_space=pltpu.VMEM),
        scratch_shapes=[
            pltpu.VMEM((3, rows, cols * G), f32),
            pltpu.SemaphoreType.DMA((3,)),
            pltpu.VMEM((3, 2, half, size.span), bf16),
            pltpu.VMEM((3, 2, half, size.span), bf16),
            pltpu.VMEM((3 * block, 2 * size.side), f32),
            pltpu.VMEM((len(moves.merged), devices, LANES), f32),
        ],
        cost_estimate=pl.CostEstimate(
            flops=18 * block * G * rows * cols,
            bytes_accessed=4 * (3 * rows * cols * G + devices * tiles * SUB * LANES),
            transcendentals=0,
        ),
        compiler_params=pltpu.CompilerParams(vmem_limit_bytes=ALL_VMEM),
        name="depth_forward",
    )(shard, table)


def depth_inverse(lines, table, before, size, kept, slabs):
    rows, cols, G, devices = size.rows, size.cols, size.G, size.devices
    units, tiles, bands = size.units(kept), size.tiles(kept), size.bands
    block = 2 * kept * devices
    half = cols // 2 * rows
    share = SUB * tiles * SUB
    extra = [] if before is None else [before]
    anywhere = pl.BlockSpec(memory_space=pltpu.HBM)
    whole = pl.BlockSpec(memory_space=pltpu.VMEM)
    moves = LaneMoves([
        (u, size.slot(SUB * band + s), s, (band * units + u) * rows, rows)
        for u in range(units)
        for band in range(bands)
        for s in range(SUB)
    ])
    outs = [jax.ShapeDtypeStruct((3, rows, cols * G), f32)]
    if slabs:
        outs += [jax.ShapeDtypeStruct((3, 2, cols * G), f32)] * 2
        outs += [jax.ShapeDtypeStruct((3, rows, 2 * G), f32)] * 2
    outs += [jax.ShapeDtypeStruct((3, rows, cols * G), f32)]

    def kernel(lines_ref, table_ref, *refs):
        out_ref, *slab_refs, ready_ref = refs[len(extra) : len(extra) + len(outs)]
        held_ref, mid_ref, turned_ref, done_ref, came, had, gone = refs[len(extra) + len(outs) :]

        def arrive(g):
            at = pl.ds(g * share, share)
            return pltpu.make_async_copy(lines_ref.at[at], held_ref.at[at], came.at[g])

        def earlier(c):
            return pltpu.make_async_copy(refs[0].at[c], ready_ref.at[c], had.at[c])

        def leave(c):
            return pltpu.make_async_copy(ready_ref.at[c], out_ref.at[c], gone.at[c])

        for g in range(devices // SUB):
            arrive(g).start()
        for g in range(devices // SUB):
            arrive(g).wait()

            def load(s, t):
                return held_ref[pl.ds(g * share + t * SUB + s, SUB, stride=tiles * SUB), :]

            def store(u, t, value):
                to = u * devices + g * SUB
                mid_ref[to : to + SUB, t * LANES : (t + 1) * LANES] = value

            moves.run(load, store, turned_ref.at[g], (SUB, LANES))

        if extra:
            for c in range(3):
                earlier(c).start()
        for c in range(3):
            for odd in (0, 1):
                at = odd * size.side
                high, low = halves(mid_ref[c * block : (c + 1) * block, at : at + half].T)
                done_ref[c, odd] = (
                    dot(high, table_ref[odd, 0], NN)
                    + dot(low, table_ref[odd, 0], NN)
                    + dot(high, table_ref[odd, 1], NN)
                )
        if extra:
            for c in range(3):
                earlier(c).wait()
        for c in range(3):
            for y in range(0, cols, 2):
                even = done_ref[c, 0, size.line(y) : size.line(y) + rows, :]
                odd = done_ref[c, 1, size.line(y + 1) : size.line(y + 1) + rows, :]
                shared = size.span - 2 * size.spare
                pair = jnp.concatenate(
                    [
                        even[:, :shared],
                        even[:, shared:] + odd[:, : 2 * size.spare],
                        odd[:, 2 * size.spare :],
                    ],
                    axis=1,
                )
                if extra:
                    pair = pair + ready_ref[c, :, y * G : (y + 2) * G]
                ready_ref[c, :, y * G : (y + 2) * G] = pair
                if slabs:
                    slab_refs[0][c, :, y * G : (y + 2) * G] = pair[rows - 2 :, :]
                    slab_refs[1][c, :, y * G : (y + 2) * G] = pair[:2, :]
                if slabs and y == cols - 2:
                    slab_refs[2][c] = pair
                if slabs and y == 0:
                    slab_refs[3][c] = pair
            leave(c).start()
        for c in range(3):
            leave(c).wait()

    return pl.pallas_call(
        kernel,
        out_shape=outs,
        in_specs=[anywhere, whole] + [anywhere] * len(extra),
        out_specs=[anywhere] + [whole] * (len(outs) - 1),
        scratch_shapes=[
            pltpu.VMEM((devices * tiles * SUB, LANES), f32),
            pltpu.VMEM((3 * block, 2 * size.side), f32),
            pltpu.VMEM((devices // SUB, len(moves.merged), SUB, LANES), f32),
            pltpu.VMEM((3, 2, half, size.span), f32),
            pltpu.SemaphoreType.DMA((devices // SUB,)),
            pltpu.SemaphoreType.DMA((3,)),
            pltpu.SemaphoreType.DMA((3,)),
        ],
        cost_estimate=pl.CostEstimate(
            flops=18 * block * G * rows * cols,
            bytes_accessed=4 * (9 * rows * cols * G + devices * tiles * SUB * LANES),
            transcendentals=0,
        ),
        compiler_params=pltpu.CompilerParams(vmem_limit_bytes=LESS_VMEM),
        name="depth_inverse",
    )(lines, table, *extra)


def planes(lines, place, tables, size, kept):
    rows, cols, G, devices, groups = size.rows, size.cols, size.G, size.devices, size.groups
    units, tiles, bands, length = size.units(kept), size.tiles(kept), size.bands, size.length
    width = units * rows
    step = 16
    unit_wave = 2.0 * math.pi / length
    full = G // LANES * LANES
    others = G // cols

    def kernel(place_ref, lines_ref, narrow_hbm, wide_hbm, waves_hbm, out_ref, held_ref, narrow_ref,
               wide_ref, waves_ref, came, told, left_ref, spec_ref, turned_ref, back_ref):
        inv_wide_ref = narrow_ref.at[:, : 3 * length]
        inv_line_ref = narrow_ref.at[:, 3 * length : 6 * length]
        line_high = narrow_ref.at[:, 6 * length : 7 * length]
        line_low = narrow_ref.at[:, 7 * length :]
        kx_ref = waves_ref.at[:, :LANES]
        ky_ref = waves_ref.at[:, LANES:]

        def come(p):
            return pltpu.make_async_copy(lines_ref.at[p], held_ref.at[p], came.at[p])

        def tell(i):
            source = (narrow_hbm, wide_hbm, waves_hbm)[i]
            return pltpu.make_async_copy(source, (narrow_ref, wide_ref, waves_ref)[i], told.at[i])

        tell(0).start()
        for p in range(groups):
            come(p).start()
        tell(1).start()
        tell(2).start()
        tell(0).wait()

        def arrive(p, _):
            come(p).wait()
            flat = jnp.concatenate(
                [held_ref[p, :, t].reshape(others * SUB, LANES).T for t in range(tiles)], axis=0
            )
            side = jnp.concatenate(
                [flat[band * width : (band + 1) * width, :] for band in range(bands)], axis=1
            )
            high, low = halves(side)
            done = (
                dot(high, line_high[...], NN)
                + dot(low, line_high[...], NN)
                + dot(high, line_low[...], NN)
            )
            for u in range(units):
                c, j, k = u // (2 * kept), u // 2 % kept, u % 2
                at = (2 * c + k) * length
                high, low = halves(done[u * rows : (u + 1) * rows, :])
                for part, value in ((0, high), (1, low)):
                    target = pl.ds(pl.multiple_of(part * G + p * rows, 16), rows)
                    left_ref[j, target, at : at + length] = value
            return 0

        lax.fori_loop(0, groups, arrive, 0)
        tell(1).wait()
        tell(2).wait()

        def one_depth(j, _):
            index = (place_ref[1] + j) * devices + place_ref[0]
            kz = index.astype(f32) * unit_wave

            def widen(u, _):
                at = pl.ds(pl.multiple_of(u * length, LANES), length)
                spec_ref[:, at] = dot(wide_ref[:, :length], left_ref[j, :, at], NN) + dot(
                    wide_ref[:, length:], left_ref[j, :G, at], NN
                )
                return 0

            lax.fori_loop(0, 6, widen, 0)

            def turn(r, _):
                top = pl.multiple_of(r * step, step)
                kx = kx_ref[pl.ds(top, step), :]

                def store(c, k, half, lane, value):
                    at = (2 * c + k) * length + lane
                    for part, piece in zip((0, 1), halves(value)):
                        target = pl.ds(pl.multiple_of(part * length + half * G + top, step), step)
                        turned_ref[target, at : at + LANES] = piece

                def green_of(lane):
                    ky = ky_ref[0:1, lane : lane + LANES]
                    square = kx * kx + ky * ky + kz * kz
                    return jnp.exp(-0.5 * smoothing * smoothing * square) / (
                        square + jnp.where(square == 0.0, 1.0, 0.0)
                    )

                def load(c, k, half, lane):
                    at = (2 * c + k) * length + lane
                    target = pl.ds(pl.multiple_of(half * G + top, step), step)
                    return spec_ref[target, at : at + LANES]

                def curl(lane_of, dy_of, green):
                    gx = green * kx
                    gz = green * kz
                    many = range(len(lane_of))
                    got = {
                        (c, k, h, t): load(c, k, h, lane_of[t])
                        for c in range(3) for k in (0, 1) for h in (0, 1) for t in many
                    }

                    def dx(c, k, h, t):
                        value = gx * got[c, k, 1 - h, t]
                        return value if h == 0 else -value

                    def dz(c, k, h, t):
                        value = gz * got[c, 1 - k, h, t]
                        return value if k == 0 else -value

                    def dy(c, k, h, t):
                        return dy_of(got, c, k, h, t)

                    for k in (0, 1):
                        for h in (0, 1):
                            for t in many:
                                store(0, k, h, lane_of[t], dy(2, k, h, t) - dz(1, k, h, t))
                                store(1, k, h, lane_of[t], dz(0, k, h, t) - dx(2, k, h, t))
                                store(2, k, h, lane_of[t], dx(1, k, h, t) - dy(0, k, h, t))

                for tile in range(full // LANES):
                    lane = 2 * tile * LANES
                    green = green_of(lane)
                    gy = green * ky_ref[0:1, lane : lane + LANES]

                    def dy_pair(got, c, k, h, t, gy=gy):
                        value = gy * got[c, k, h, 1 - t]
                        return value if t == 0 else -value

                    curl((lane, lane + LANES), dy_pair, green)
                if full < G:
                    lane = 2 * full
                    green = green_of(lane)
                    gy = green * ky_ref[0:1, lane : lane + LANES]

                    def dy_roll(got, c, k, h, t):
                        return gy * pltpu.roll(got[c, k, h, t], LANES // 2, 1)

                    curl((lane,), dy_roll, green)
                return 0

            lax.fori_loop(0, G // step, turn, 0)

            def narrow(u, _):
                at = pl.ds(pl.multiple_of(u * length, LANES), length)
                done = dot(inv_wide_ref[:, : 2 * length], turned_ref[:, at], NN) + dot(
                    inv_wide_ref[:, 2 * length :], turned_ref[:length, at], NN
                )
                high, low = halves(done)
                unit = (u // 2) * (2 * kept) + 2 * j + u % 2
                target = pl.ds(pl.multiple_of(unit * rows, 16), rows)
                for p in range(groups):
                    for part, value in ((0, high), (1, low)):
                        back_ref[p, target, part * length : (part + 1) * length] = value[
                            p * rows : (p + 1) * rows, :
                        ]
                return 0

            lax.fori_loop(0, 6, narrow, 0)
            return 0

        lax.fori_loop(0, kept, one_depth, 0)

        def depart(p):
            return pltpu.make_async_copy(held_ref.at[p], out_ref.at[p], came.at[p])

        def leave(p, _):
            done = dot(inv_line_ref[:, : 2 * length], back_ref[p], NT) + dot(
                inv_line_ref[:, 2 * length :], back_ref[p, :, :length], NT
            )
            pieces = [
                done[band * others * SUB : (band + 1) * others * SUB, :] for band in range(bands)
            ]
            if tiles * LANES > bands * width:
                pieces += [jnp.zeros((others * SUB, tiles * LANES - bands * width), f32)]
            line = jnp.concatenate(pieces, axis=1)
            for t in range(tiles):
                held_ref[p, :, t] = line[:, t * LANES : (t + 1) * LANES].reshape(others, SUB, LANES)
            depart(p).start()
            return 0

        lax.fori_loop(0, groups, leave, 0)
        for p in range(groups):
            depart(p).wait()

    anywhere = pl.BlockSpec(memory_space=pltpu.HBM)
    flops = 6 * (4 * groups * width * G * length + 24 * kept * length * G * length)
    return pl.pallas_call(
        kernel,
        out_shape=jax.ShapeDtypeStruct(lines.shape, f32),
        in_specs=[pl.BlockSpec(memory_space=pltpu.SMEM)] + [anywhere] * 4,
        out_specs=anywhere,
        scratch_shapes=[
            pltpu.VMEM(lines.shape, f32),
            *(pltpu.VMEM(table.shape, table.dtype) for table in tables),
            pltpu.SemaphoreType.DMA((groups,)),
            pltpu.SemaphoreType.DMA((3,)),
            pltpu.VMEM((kept, 2 * G, 6 * length), bf16),
            pltpu.VMEM((length, 6 * length), f32),
            pltpu.VMEM((2 * length, 6 * length), bf16),
            pltpu.VMEM((groups, width, 2 * length), bf16),
        ],
        cost_estimate=pl.CostEstimate(
            flops=flops, bytes_accessed=8 * lines.size, transcendentals=kept * G * G
        ),
        compiler_params=pltpu.CompilerParams(vmem_limit_bytes=ALL_VMEM),
        name="planes",
    )(place, lines, *tables)


def halo(slabs):
    def shifted(piece, axis, up):
        devices = lax.axis_size(axis)
        pairs = [(i, i + 1) for i in range(devices - 1)]
        if not up:
            pairs = [(j, i) for i, j in pairs]
        return lax.ppermute(piece, axis, pairs)

    last_rows, first_rows, last_cols, first_cols = slabs
    return (
        shifted(last_cols, "py", True),
        shifted(first_cols, "py", False),
        shifted(last_rows, "px", True),
        shifted(first_rows, "px", False),
    )


def depth_weights(G):
    width = 2 * G
    at = np.arange(width) % G
    rows = []
    for k in range(width // LANES):
        for shift, weight in ((1, 8.0), (-1, -8.0), (2, -1.0), (-2, 1.0)):
            inside = (at + shift >= 0) & (at + shift < G)
            rows.append(np.where(inside, weight / 12.0, 0.0)[k * LANES : (k + 1) * LANES])
    return np.stack(rows).astype(np.float32)


def stretch(field, flow, left, right, size):
    rows, cols, G = size.rows, size.cols, size.G
    span = 2 * G // LANES
    many = cols * G // LANES
    half = LANES // 2

    def kernel(field_hbm, flow_ref, left_ref, right_ref, weight_ref, out_ref, field_ref, sem,
               ext_ref, turned_ref):
        whole = pltpu.make_async_copy(field_hbm, field_ref, sem)

        @pl.when(pl.program_id(0) == 0)
        def _():
            whole.start()
            ext_ref[:, 0:SUB, :] = jnp.zeros((many + 2 * span, SUB, LANES), f32)
            ext_ref[:, SUB + rows :, :] = jnp.zeros((many + 2 * span, SUB, LANES), f32)

        def put(t, value):
            ext_ref[t, SUB : SUB + rows, :] = value
            turned_ref[t] = pltpu.roll(value, half, 1)

        for t in range(many):
            at = slice(t * LANES, (t + 1) * LANES)
            put(span + t, flow_ref[0, :, at])
        for t in range(span):
            at = slice(t * LANES, (t + 1) * LANES)
            put(t, left_ref[0, :, at])
            put(span + many + t, right_ref[0, :, at])
        lane = lax.broadcasted_iota(jnp.int32, (ROWS, LANES), 1)

        @pl.when(pl.program_id(0) == 0)
        def _():
            whole.wait()

        def block(b, _):
            base = span * (b + 1)
            for top in range(0, rows, ROWS):
                these = slice(top, top + ROWS)

                def tall_at(t, s):
                    return ext_ref[t, SUB + top + s : SUB + top + s + ROWS, :]

                def side_at(t):
                    return jnp.where(lane < half, turned_ref[t, these, :], turned_ref[t + 1, these, :])

                own = [tall_at(base + k, 0) for k in range(span)]
                for k in range(span):
                    t = base + k
                    deep = 0.0
                    for i, s in enumerate((1, -1, 2, -2)):
                        value = pltpu.roll(own[k], (-s) % LANES, 1)
                        if s > 0 and k + 1 < span:
                            value = jnp.where(
                                lane < LANES - s, value, pltpu.roll(own[k + 1], (-s) % LANES, 1)
                            )
                        if s < 0 and k > 0:
                            value = jnp.where(
                                lane >= -s, value, pltpu.roll(own[k - 1], (-s) % LANES, 1)
                            )
                        deep = deep + weight_ref[4 * k + i : 4 * k + i + 1, :] * value
                    side = 8.0 * (side_at(t + 1) - side_at(t - 2)) - (
                        tall_at(t + span, 0) - tall_at(t - span, 0)
                    )
                    tall = 8.0 * (tall_at(t, 1) - tall_at(t, -1)) - (tall_at(t, 2) - tall_at(t, -2))
                    at = pl.ds(pl.multiple_of((span * b + k) * LANES, LANES), LANES)
                    out_ref[0, these, at] = field_ref[2, these, at] * deep + (1.0 / 12.0) * (
                        field_ref[1, these, at] * side + field_ref[0, these, at] * tall
                    )
            return 0

        lax.fori_loop(0, cols // 2, block, 0, unroll=2)

    def part(*shape):
        return pl.BlockSpec((1,) + shape, lambda i: (i, 0, 0))

    return pl.pallas_call(
        kernel,
        grid=(3,),
        out_shape=jax.ShapeDtypeStruct((3, rows, cols * G), f32),
        in_specs=[
            pl.BlockSpec(memory_space=pltpu.HBM),
            part(rows, cols * G),
            part(rows, 2 * G),
            part(rows, 2 * G),
            pl.BlockSpec((4 * span, LANES), lambda i: (0, 0)),
        ],
        out_specs=part(rows, cols * G),
        scratch_shapes=[
            pltpu.VMEM((3, rows, cols * G), f32),
            pltpu.SemaphoreType.DMA,
            pltpu.VMEM((many + 2 * span, rows + 2 * SUB, LANES), f32),
            pltpu.VMEM((many + 2 * span, rows, LANES), f32),
        ],
        cost_estimate=pl.CostEstimate(
            flops=60 * flow.size, bytes_accessed=12 * flow.size, transcendentals=0
        ),
        compiler_params=pltpu.CompilerParams(vmem_limit_bytes=MOST_VMEM),
        name="stretch",
    )(field, flow, left, right, jnp.asarray(depth_weights(G)))


def add_rows(field, part, up, down, size):
    rows, width = size.rows, size.cols * size.G
    last = rows // SUB - 1

    def kernel(field_ref, part_ref, up_ref, down_ref, out_ref):
        out_ref[...] = part_ref[...]

        def add(c, row, value):
            at = slice(row, row + 1)
            out_ref[c, at, :] = part_ref[c, at, :] + (1.0 / 12.0) * field_ref[0, at, :] * value

        @pl.when(pl.program_id(0) == 0)
        def _():
            for c in range(3):
                far, near = up_ref[c, 0:1, :], up_ref[c, 1:2, :]
                add(c, 0, far - 8.0 * near)
                add(c, 1, near)

        @pl.when(pl.program_id(0) == 1)
        def _():
            for c in range(3):
                near, far = down_ref[c, 0:1, :], down_ref[c, 1:2, :]
                add(c, SUB - 1, 8.0 * near - far)
                add(c, SUB - 2, -near)

    edge = pl.BlockSpec((3, SUB, width), lambda i: (0, i * last, 0))
    whole = pl.BlockSpec((3, 2, width), lambda i: (0, 0, 0))
    return pl.pallas_call(
        kernel,
        grid=(2,),
        out_shape=jax.ShapeDtypeStruct((3, rows, width), f32),
        in_specs=[pl.BlockSpec((1, SUB, width), lambda i: (0, i * last, 0)), edge, whole, whole],
        out_specs=edge,
        input_output_aliases={1: 0},
        cost_estimate=pl.CostEstimate(
            flops=60 * width, bytes_accessed=4 * 40 * 3 * width, transcendentals=0
        ),
        compiler_params=pltpu.CompilerParams(vmem_limit_bytes=MOST_VMEM),
        name="add_rows",
    )(field, part, up, down)


def triple(table, axis):
    high, low = split_table(table)
    return np.concatenate([high, high, low], axis=axis)


def fast(vorticity, size):
    rows, cols, G, devices, groups = size.rows, size.cols, size.G, size.devices, size.groups
    length, bands, others = size.length, size.bands, size.G // size.cols
    axes = ("px", "py")
    place = lax.axis_index(axes).astype(jnp.int32)

    cells = np.array([
        q * cols + band * SUB + s for band in range(bands) for q in range(others) for s in range(SUB)
    ])
    lane_modes, lane_kinds = lane_order(G)
    row_modes = np.concatenate([np.arange(G)] * 2)
    row_kinds = np.repeat([0, 1], G)
    line_basis = basis(G, lane_modes, lane_kinds, length)[cells]
    wide_basis = basis(G, row_modes, row_kinds, length)
    line = split_table(line_basis)
    wide = triple(wide_basis.T, 1)
    inv_wide = triple(wide_basis * weights(row_modes, length), 1)
    inv_line = triple(line_basis * weights(lane_modes, length), 1)
    kx = np.broadcast_to(waves(np.arange(G), length)[:, None], (G, LANES)).astype(np.float32)
    signs = np.where(lane_kinds == 0, 1.0, -1.0)
    signs[: 2 * (G // LANES * LANES)] = 1.0
    ky = (waves(lane_modes, length) * signs).astype(np.float32)
    waves_of = np.zeros((G, LANES + length), np.float32)
    waves_of[:, :LANES] = kx
    waves_of[:, LANES:] = ky
    narrow = np.concatenate([inv_wide, inv_line, *line], axis=1)
    tables = tuple(jnp.asarray(t) for t in (narrow, wide, waves_of))

    def depth_tables(start, kept):
        modes = np.array([
            (start + j) * devices + d
            for j in range(kept) for k in (0, 1) for d in range(devices)
        ])
        kinds = np.array([k for j in range(kept) for k in (0, 1) for d in range(devices)])
        table = basis(G, modes, kinds, length)
        spare = ((0, 0), (0, size.spare)), ((0, 0), (size.spare, 0))

        def both(rows_of):
            return jnp.asarray(np.stack([np.stack(split_table(np.pad(rows_of, pad))) for pad in spare]))

        return both(table.T), both((table * weights(modes, length)).T)

    def exchange(value):
        value = value.reshape(devices, -1, LANES)
        return lax.all_to_all(value, axes, split_axis=0, concat_axis=0, tiled=True)

    arrived = []
    for start, kept in size.chunks:
        arrived.append(exchange(depth_forward(vorticity, depth_tables(start, kept)[0], size, kept)))
    returned = []
    for (start, kept), lines in zip(size.chunks, arrived):
        lines = lines.reshape(groups, others, size.tiles(kept), SUB, LANES)
        where = jnp.stack([place, jnp.int32(start)])
        returned.append(exchange(planes(lines, where, tables, size, kept)))
    flow = None
    for (start, kept), lines in zip(size.chunks, returned):
        last = start + kept == G // devices
        flow, *slabs, held = depth_inverse(
            lines.reshape(-1, LANES), depth_tables(start, kept)[1], flow, size, kept, last
        )
    left, right, up, down = halo(slabs)
    part = stretch(vorticity, held, left, right, size)
    return flow, add_rows(vorticity, part, up, down, size)


def with_halo(shard, sides, width):
    for axis, dim in sides:
        devices, length = (lax.axis_size(axis), shard.shape[dim])
        up = [(i, (i + 1) % devices) for i in range(devices - 1)]
        down = [(j, i) for i, j in up]
        last = lax.slice_in_dim(shard, length - width, length, axis=dim)
        leading = lax.slice_in_dim(shard, 0, width, axis=dim)
        before = lax.ppermute(last, axis, up)
        after = lax.ppermute(leading, axis, down)
        shard = jnp.concatenate([before, shard, after], axis=dim)
    return shard


def twiddle(count_in, count_out, length, factor):
    source = lax.broadcasted_iota(jnp.int32, (count_in, count_out), 0)
    target = lax.broadcasted_iota(jnp.int32, (count_in, count_out), 1)
    angle = (source * target % length).astype(jnp.float32) * (2.0 * math.pi / length)
    cosine = jnp.cos(angle) * factor
    sine = jnp.sin(angle) * factor
    return (
        jnp.broadcast_to(cosine, (3, count_in, count_out)),
        jnp.broadcast_to(sine, (3, count_in, count_out)),
    )


def product(einsum_form, first, second):
    return jnp.einsum(einsum_form, first, second, precision=highest)


def forward_left(pair, einsum_form, tables):
    real_part, imag_part = pair
    cosine_table, sine_table = tables
    return (
        product(einsum_form, cosine_table, real_part) + product(einsum_form, sine_table, imag_part),
        product(einsum_form, cosine_table, imag_part) - product(einsum_form, sine_table, real_part),
    )


def forward_right(pair, einsum_form, tables):
    real_part, imag_part = pair
    cosine_table, sine_table = tables
    return (
        product(einsum_form, real_part, cosine_table) + product(einsum_form, imag_part, sine_table),
        product(einsum_form, imag_part, cosine_table) - product(einsum_form, real_part, sine_table),
    )


def backward_left(pair, einsum_form, tables):
    real_part, imag_part = pair
    cosine_table, sine_table = tables
    return (
        product(einsum_form, cosine_table, real_part) - product(einsum_form, sine_table, imag_part),
        product(einsum_form, cosine_table, imag_part) + product(einsum_form, sine_table, real_part),
    )


def wavenumbers(start, count, length, position):
    index = start + lax.iota(jnp.int32, count)
    signed = jnp.where(index < length // 2, index, index - length)
    wave = signed.astype(jnp.float32) * (2.0 * math.pi / length)
    slope = jnp.where(index == length // 2, 0.0, wave)
    keep = jnp.where(index == length // 2, 0.0, 1.0)
    shape = [1, 1, 1, 1]
    shape[position] = count
    return (wave.reshape(shape), slope.reshape(shape), keep.reshape(shape))


def velocity_spectrum(pair, waves_x, waves_y, waves_z):
    square = waves_x[0] ** 2 + waves_y[0] ** 2 + waves_z[0] ** 2
    mask = waves_x[2] * waves_y[2] * waves_z[2]
    green = (
        mask
        * jnp.exp(-0.5 * smoothing * smoothing * square)
        / (square + jnp.where(square == 0.0, 1.0, 0.0))
    )
    slope_x, slope_y, slope_z = (waves_x[1][0], waves_y[1][0], waves_z[1][0])

    def curl(field):
        return jnp.stack(
            [
                slope_y * field[2] - slope_z * field[1],
                slope_z * field[0] - slope_x * field[2],
                slope_x * field[1] - slope_y * field[0],
            ]
        )

    real_part = pair[0] * green
    imag_part = pair[1] * green
    return (jnp.swapaxes(-curl(imag_part), 1, 2), jnp.swapaxes(curl(real_part), 1, 2))


def window(padded, axis, offset):
    starts = [0, 2, 2, 2]
    limits = [padded.shape[0], padded.shape[1] - 2, padded.shape[2] - 2, padded.shape[3] - 2]
    starts[axis] = starts[axis] + offset
    limits[axis] = limits[axis] + offset
    return lax.slice(padded, starts, limits)


def derivative(padded, axis):
    near = window(padded, axis, 1) - window(padded, axis, -1)
    far = window(padded, axis, 2) - window(padded, axis, -2)
    return (8.0 * near - far) / 12.0


def general(vorticity):
    block_rows = vorticity.shape[1]
    G = block_rows * lax.axis_size("px")
    block_cols = vorticity.shape[2] // G
    field = vorticity.reshape(3, block_rows, block_cols, G)
    length = 2 * G
    depth_tables = twiddle(G, G, length, 1.0)
    line_tables = twiddle(G, length, length, 1.0)
    inverse_tables = twiddle(length, G, length, 1.0 / length)
    closing = twiddle(G, G, length, 1.0 / length)
    weights = jnp.where(lax.iota(jnp.int32, G) == 0, 1.0, 2.0)[None, :, None]
    closing_cos = closing[0] * weights
    closing_sin = closing[1] * weights
    pair = (
        product("czk,cxyz->ckxy", depth_tables[0], field),
        -product("czk,cxyz->ckxy", depth_tables[1], field),
    )
    pair = (
        lax.all_to_all(pair[0], "py", split_axis=1, concat_axis=3, tiled=True),
        lax.all_to_all(pair[1], "py", split_axis=1, concat_axis=3, tiled=True),
    )
    pair = forward_left(pair, "cyl,ckxy->clkx", line_tables)
    pair = (
        lax.all_to_all(pair[0], "px", split_axis=1, concat_axis=3, tiled=True),
        lax.all_to_all(pair[1], "px", split_axis=1, concat_axis=3, tiled=True),
    )
    pair = forward_right(pair, "clkx,cxm->clkm", line_tables)
    rows = pair[0].shape[1]
    depth = pair[0].shape[2]
    waves_y = wavenumbers(lax.axis_index("px") * rows, rows, length, 1)
    waves_z = wavenumbers(lax.axis_index("py") * depth, depth, length, 2)
    waves_x = wavenumbers(0, length, length, 3)
    pair = velocity_spectrum(pair, waves_x, waves_y, waves_z)
    pair = backward_left(pair, "cmx,cklm->cxkl", inverse_tables)
    pair = (
        lax.all_to_all(pair[0], "px", split_axis=1, concat_axis=3, tiled=True),
        lax.all_to_all(pair[1], "px", split_axis=1, concat_axis=3, tiled=True),
    )
    pair = backward_left(pair, "cly,cxkl->cyxk", inverse_tables)
    pair = (
        lax.all_to_all(pair[0], "py", split_axis=1, concat_axis=3, tiled=True),
        lax.all_to_all(pair[1], "py", split_axis=1, concat_axis=3, tiled=True),
    )
    flow = product("cyxk,ckz->cyxz", pair[0], closing_cos) - product(
        "cyxk,ckz->cyxz", pair[1], closing_sin
    )
    flow = jnp.swapaxes(flow, 1, 2)
    padded = with_halo(flow, (("px", 1), ("py", 2)), 2)
    padded = jnp.pad(padded, ((0, 0), (0, 0), (0, 0), (2, 2)))
    stretching = (
        field[0] * derivative(padded, 1)
        + field[1] * derivative(padded, 2)
        + field[2] * derivative(padded, 3)
    )
    return (
        flow.reshape(3, block_rows, block_cols * G),
        stretching.reshape(3, block_rows, block_cols * G),
    )


def on_device(vorticity):
    sizes = fast_sizes(vorticity)
    if sizes is None:
        return general(vorticity)
    return fast(vorticity, sizes)


def solution(mesh):
    in_specs = (P(None, "px", "py"),)
    out_specs = (P(None, "px", "py"), P(None, "px", "py"))
    return jax.shard_map(
        on_device, mesh=mesh, in_specs=in_specs, out_specs=out_specs, check_vma=False
    )
```

```python
import math

import jax
import jax.numpy as jnp
import numpy as np
from jax import lax
from jax.experimental import pallas as pl
from jax.experimental.pallas import tpu as pltpu
from jax.sharding import PartitionSpec as P


smoothing = 1.0
highest = lax.Precision.HIGHEST
f32 = jnp.float32
bf16 = jnp.bfloat16
LANES = 128
SUB = 8
ROWS = 16
ALL_VMEM, MOST_VMEM, LESS_VMEM = 67_000_000, 50_000_000, 50_000_000


def split_table(table):
    high = table.astype(np.float32).astype(jnp.bfloat16)
    low = (table - high.astype(np.float64)).astype(np.float32).astype(jnp.bfloat16)
    return high, low


def waves(modes, length):
    return np.asarray(modes, np.float64) * (2.0 * math.pi / length)


def basis(points, modes, kinds, length):
    angle = (np.arange(points)[:, None] * np.asarray(modes)[None, :] % length) * (
        2.0 * math.pi / length
    )
    return np.where(np.asarray(kinds)[None, :] == 0, np.cos(angle), np.sin(angle))


def weights(modes, length):
    return np.where(np.asarray(modes) == 0, 1.0, 2.0) / length


def lane_order(modes):
    full = modes // LANES * LANES
    index, kind = [], []
    for start in range(0, full, LANES):
        for k in (0, 1):
            index += list(range(start, start + LANES))
            kind += [k] * LANES
    for k in (0, 1):
        index += list(range(full, modes))
        kind += [k] * (modes - full)
    return np.array(index), np.array(kind)


def dot(first, second, dims):
    return lax.dot_general(first, second, (dims, ((), ())), preferred_element_type=f32)


NN = ((1,), (0,))
NT = ((1,), (1,))
TN = ((0,), (0,))


def halves(value):
    high = value.astype(bf16)
    low = (value - high.astype(f32)).astype(bf16)
    return high, low


class Sizes:
    def __init__(self, rows, cols, G, devices, groups):
        self.rows, self.cols, self.G = rows, cols, G
        self.devices, self.groups = devices, groups
        self.bands = cols // SUB
        self.spare = G % LANES
        self.span = G + self.spare
        self.side = -(-cols // 2 * rows // LANES) * LANES
        self.length = 2 * G
        total = G // devices
        first = max(1, total // 3)
        self.chunks = [(0, first), (first, total - first)] if total > first else [(0, first)]

    def line(self, y):
        return (y // 2 + SUB // 2 * (y % 2)) % (self.cols // 2) * self.rows

    def slot(self, y):
        return y % 2 * self.side + self.line(y)

    def units(self, kept):
        return 6 * kept

    def tiles(self, kept):
        return -(-self.bands * self.units(kept) * self.rows // LANES)


def fast_sizes(vorticity):
    rows = vorticity.shape[1]
    groups = lax.axis_size("px")
    G = rows * groups
    cols = vorticity.shape[2] // G
    devices = groups * lax.axis_size("py")
    if rows % 16 or rows * cols % LANES or cols % (2 * SUB) not in (0, SUB) or cols % SUB or cols % 2:
        return None
    if G % devices or devices % SUB or G % LANES != LANES // 2:
        return None
    return Sizes(rows, cols, G, devices, groups)


class LaneMoves:
    def __init__(self, fragments):
        self.merged = []
        self.wanted = {}
        open_groups = {}
        for dest, to, source, start, width in fragments:
            at = to
            shift = (to - start) % LANES
            while at < to + width:
                origin = at - to + start
                take = min(to + width - at, LANES - origin % LANES)
                group = self._place(open_groups, origin // LANES, shift, origin % LANES, take, source)
                end = at + take
                while at < end:
                    part = min(end - at, LANES - at % LANES)
                    self.wanted.setdefault((dest, at // LANES), []).append((at % LANES, group))
                    at += part

    def _place(self, open_groups, tile, shift, lane, width, source):
        for group in open_groups.setdefault((tile, shift), []):
            pieces = self.merged[group][2]
            if all(lane >= at + wide or at >= lane + width for at, wide, _ in pieces):
                pieces.append((lane, width, source))
                return group
        self.merged.append((tile, shift, [(lane, width, source)]))
        open_groups[tile, shift].append(len(self.merged) - 1)
        return len(self.merged) - 1

    def run(self, load, store, held, shape):
        lane = lax.broadcasted_iota(jnp.int32, shape, 1)

        def choose(parts):
            value = None
            for at, part in sorted(parts, key=lambda pair: pair[0]):
                value = part() if value is None else jnp.where(lane >= at, part(), value)
            return value

        for index, (tile, shift, pieces) in enumerate(self.merged):
            value = choose(
                [(at, lambda source=source, tile=tile: load(source, tile)) for at, _, source in pieces]
            )
            held[index] = pltpu.roll(value, shift, 1) if shift else value
        for (dest, tile), parts in self.wanted.items():
            store(dest, tile, choose([(at, lambda index=index: held[index]) for at, index in parts]))


def depth_forward(shard, table, size, kept):
    rows, cols, G, devices = size.rows, size.cols, size.G, size.devices
    units, tiles, bands = size.units(kept), size.tiles(kept), size.bands
    block = 2 * kept * devices
    half = cols // 2 * rows
    moves = LaneMoves([
        (s, (band * units + u) * rows, u, size.slot(SUB * band + s), rows)
        for s in range(SUB)
        for band in range(bands)
        for u in range(units)
    ])

    def kernel(shard_ref, table_ref, out_ref, held_ref, sems, high_ref, low_ref, mid_ref, turned_ref):
        def fetch(c):
            return pltpu.make_async_copy(shard_ref.at[c], held_ref.at[c], sems.at[c])

        for c in range(3):
            fetch(c).start()

        for c in range(3):
            fetch(c).wait()
            for y in range(cols):
                odd, to = y % 2, size.line(y)
                start = y * G - odd * size.spare
                high, low = halves(held_ref[c, :, start : start + size.span])
                high_ref[c, odd, to : to + rows, :] = high
                low_ref[c, odd, to : to + rows, :] = low
        for c in range(3):
            for odd in (0, 1):
                at = odd * size.side
                mid_ref[c * block : (c + 1) * block, at : at + half] = (
                    dot(table_ref[odd, 0], high_ref[c, odd], NT)
                    + dot(table_ref[odd, 0], low_ref[c, odd], NT)
                    + dot(table_ref[odd, 1], high_ref[c, odd], NT)
                )

        def load(u, t):
            return mid_ref[u * devices : (u + 1) * devices, t * LANES : (t + 1) * LANES]

        def store(s, t, value):
            out_ref[pl.ds(t * SUB + s, devices, stride=tiles * SUB), :] = value

        moves.run(load, store, turned_ref, (devices, LANES))

    return pl.pallas_call(
        kernel,
        out_shape=jax.ShapeDtypeStruct((devices * tiles * SUB, LANES), f32),
        in_specs=[pl.BlockSpec(memory_space=pltpu.HBM), pl.BlockSpec(memory_space=pltpu.VMEM)],
        out_specs=pl.BlockSpec(memory_space=pltpu.VMEM),
        scratch_shapes=[
            pltpu.VMEM((3, rows, cols * G), f32),
            pltpu.SemaphoreType.DMA((3,)),
            pltpu.VMEM((3, 2, half, size.span), bf16),
            pltpu.VMEM((3, 2, half, size.span), bf16),
            pltpu.VMEM((3 * block, 2 * size.side), f32),
            pltpu.VMEM((len(moves.merged), devices, LANES), f32),
        ],
        cost_estimate=pl.CostEstimate(
            flops=18 * block * G * rows * cols,
            bytes_accessed=4 * (3 * rows * cols * G + devices * tiles * SUB * LANES),
            transcendentals=0,
        ),
        compiler_params=pltpu.CompilerParams(vmem_limit_bytes=ALL_VMEM),
        name="depth_forward",
    )(shard, table)


def depth_inverse(lines, table, before, size, kept, slabs):
    rows, cols, G, devices = size.rows, size.cols, size.G, size.devices
    units, tiles, bands = size.units(kept), size.tiles(kept), size.bands
    block = 2 * kept * devices
    half = cols // 2 * rows
    share = SUB * tiles * SUB
    extra = [] if before is None else [before]
    anywhere = pl.BlockSpec(memory_space=pltpu.HBM)
    whole = pl.BlockSpec(memory_space=pltpu.VMEM)
    moves = LaneMoves([
        (u, size.slot(SUB * band + s), s, (band * units + u) * rows, rows)
        for u in range(units)
        for band in range(bands)
        for s in range(SUB)
    ])
    outs = [jax.ShapeDtypeStruct((3, rows, cols * G), f32)]
    if slabs:
        outs += [jax.ShapeDtypeStruct((3, 2, cols * G), f32)] * 2
        outs += [jax.ShapeDtypeStruct((3, rows, 2 * G), f32)] * 2
    outs += [jax.ShapeDtypeStruct((3, rows, cols * G), f32)]

    def kernel(lines_ref, table_ref, *refs):
        out_ref, *slab_refs, ready_ref = refs[len(extra) : len(extra) + len(outs)]
        held_ref, mid_ref, turned_ref, done_ref, came, had, gone = refs[len(extra) + len(outs) :]

        def arrive(g):
            at = pl.ds(g * share, share)
            return pltpu.make_async_copy(lines_ref.at[at], held_ref.at[at], came.at[g])

        def earlier(c):
            return pltpu.make_async_copy(refs[0].at[c], ready_ref.at[c], had.at[c])

        def leave(c):
            return pltpu.make_async_copy(ready_ref.at[c], out_ref.at[c], gone.at[c])

        for g in range(devices // SUB):
            arrive(g).start()
        for g in range(devices // SUB):
            arrive(g).wait()

            def load(s, t):
                return held_ref[pl.ds(g * share + t * SUB + s, SUB, stride=tiles * SUB), :]

            def store(u, t, value):
                to = u * devices + g * SUB
                mid_ref[to : to + SUB, t * LANES : (t + 1) * LANES] = value

            moves.run(load, store, turned_ref.at[g], (SUB, LANES))

        if extra:
            for c in range(3):
                earlier(c).start()
        for c in range(3):
            for odd in (0, 1):
                at = odd * size.side
                high, low = halves(mid_ref[c * block : (c + 1) * block, at : at + half].T)
                done_ref[c, odd] = (
                    dot(high, table_ref[odd, 0], NN)
                    + dot(low, table_ref[odd, 0], NN)
                    + dot(high, table_ref[odd, 1], NN)
                )
        if extra:
            for c in range(3):
                earlier(c).wait()
        for c in range(3):
            for y in range(0, cols, 2):
                even = done_ref[c, 0, size.line(y) : size.line(y) + rows, :]
                odd = done_ref[c, 1, size.line(y + 1) : size.line(y + 1) + rows, :]
                shared = size.span - 2 * size.spare
                pair = jnp.concatenate(
                    [
                        even[:, :shared],
                        even[:, shared:] + odd[:, : 2 * size.spare],
                        odd[:, 2 * size.spare :],
                    ],
                    axis=1,
                )
                if extra:
                    pair = pair + ready_ref[c, :, y * G : (y + 2) * G]
                ready_ref[c, :, y * G : (y + 2) * G] = pair
                if slabs:
                    slab_refs[0][c, :, y * G : (y + 2) * G] = pair[rows - 2 :, :]
                    slab_refs[1][c, :, y * G : (y + 2) * G] = pair[:2, :]
                if slabs and y == cols - 2:
                    slab_refs[2][c] = pair
                if slabs and y == 0:
                    slab_refs[3][c] = pair
            leave(c).start()
        for c in range(3):
            leave(c).wait()

    return pl.pallas_call(
        kernel,
        out_shape=outs,
        in_specs=[anywhere, whole] + [anywhere] * len(extra),
        out_specs=[anywhere] + [whole] * (len(outs) - 1),
        scratch_shapes=[
            pltpu.VMEM((devices * tiles * SUB, LANES), f32),
            pltpu.VMEM((3 * block, 2 * size.side), f32),
            pltpu.VMEM((devices // SUB, len(moves.merged), SUB, LANES), f32),
            pltpu.VMEM((3, 2, half, size.span), f32),
            pltpu.SemaphoreType.DMA((devices // SUB,)),
            pltpu.SemaphoreType.DMA((3,)),
            pltpu.SemaphoreType.DMA((3,)),
        ],
        cost_estimate=pl.CostEstimate(
            flops=18 * block * G * rows * cols,
            bytes_accessed=4 * (9 * rows * cols * G + devices * tiles * SUB * LANES),
            transcendentals=0,
        ),
        compiler_params=pltpu.CompilerParams(vmem_limit_bytes=LESS_VMEM),
        name="depth_inverse",
    )(lines, table, *extra)


def planes(lines, place, tables, size, kept):
    rows, cols, G, devices, groups = size.rows, size.cols, size.G, size.devices, size.groups
    units, tiles, bands, length = size.units(kept), size.tiles(kept), size.bands, size.length
    width = units * rows
    step = 16
    unit_wave = 2.0 * math.pi / length
    full = G // LANES * LANES
    others = G // cols

    def kernel(place_ref, lines_ref, narrow_hbm, wide_hbm, waves_hbm, out_ref, held_ref, narrow_ref,
               wide_ref, waves_ref, came, told, left_ref, spec_ref, turned_ref, back_ref):
        inv_wide_ref = narrow_ref.at[:, : 3 * length]
        inv_line_ref = narrow_ref.at[:, 3 * length : 6 * length]
        line_high = narrow_ref.at[:, 6 * length : 7 * length]
        line_low = narrow_ref.at[:, 7 * length :]
        kx_ref = waves_ref.at[:, :LANES]
        ky_ref = waves_ref.at[:, LANES:]

        def come(p):
            return pltpu.make_async_copy(lines_ref.at[p], held_ref.at[p], came.at[p])

        def tell(i):
            source = (narrow_hbm, wide_hbm, waves_hbm)[i]
            return pltpu.make_async_copy(source, (narrow_ref, wide_ref, waves_ref)[i], told.at[i])

        tell(0).start()
        for p in range(groups):
            come(p).start()
        tell(1).start()
        tell(2).start()
        tell(0).wait()

        def arrive(p, _):
            come(p).wait()
            flat = jnp.concatenate(
                [held_ref[p, :, t].reshape(others * SUB, LANES).T for t in range(tiles)], axis=0
            )
            side = jnp.concatenate(
                [flat[band * width : (band + 1) * width, :] for band in range(bands)], axis=1
            )
            high, low = halves(side)
            done = (
                dot(high, line_high[...], NN)
                + dot(low, line_high[...], NN)
                + dot(high, line_low[...], NN)
            )
            for u in range(units):
                c, j, k = u // (2 * kept), u // 2 % kept, u % 2
                at = (2 * c + k) * length
                high, low = halves(done[u * rows : (u + 1) * rows, :])
                for part, value in ((0, high), (1, low)):
                    target = pl.ds(pl.multiple_of(part * G + p * rows, 16), rows)
                    left_ref[j, target, at : at + length] = value
            return 0

        lax.fori_loop(0, groups, arrive, 0)
        tell(1).wait()
        tell(2).wait()

        def one_depth(j, _):
            index = (place_ref[1] + j) * devices + place_ref[0]
            kz = index.astype(f32) * unit_wave

            def widen(u, _):
                at = pl.ds(pl.multiple_of(u * length, LANES), length)
                spec_ref[:, at] = dot(wide_ref[:, :length], left_ref[j, :, at], NN) + dot(
                    wide_ref[:, length:], left_ref[j, :G, at], NN
                )
                return 0

            lax.fori_loop(0, 6, widen, 0)

            def turn(r, _):
                top = pl.multiple_of(r * step, step)
                kx = kx_ref[pl.ds(top, step), :]

                def store(c, k, half, lane, value):
                    at = (2 * c + k) * length + lane
                    for part, piece in zip((0, 1), halves(value)):
                        target = pl.ds(pl.multiple_of(part * length + half * G + top, step), step)
                        turned_ref[target, at : at + LANES] = piece

                def green_of(lane):
                    ky = ky_ref[0:1, lane : lane + LANES]
                    square = kx * kx + ky * ky + kz * kz
                    return jnp.exp(-0.5 * smoothing * smoothing * square) / (
                        square + jnp.where(square == 0.0, 1.0, 0.0)
                    )

                def load(c, k, half, lane):
                    at = (2 * c + k) * length + lane
                    target = pl.ds(pl.multiple_of(half * G + top, step), step)
                    return spec_ref[target, at : at + LANES]

                def curl(lane_of, dy_of, green):
                    gx = green * kx
                    gz = green * kz
                    many = range(len(lane_of))
                    got = {
                        (c, k, h, t): load(c, k, h, lane_of[t])
                        for c in range(3) for k in (0, 1) for h in (0, 1) for t in many
                    }

                    def dx(c, k, h, t):
                        value = gx * got[c, k, 1 - h, t]
                        return value if h == 0 else -value

                    def dz(c, k, h, t):
                        value = gz * got[c, 1 - k, h, t]
                        return value if k == 0 else -value

                    def dy(c, k, h, t):
                        return dy_of(got, c, k, h, t)

                    for k in (0, 1):
                        for h in (0, 1):
                            for t in many:
                                store(0, k, h, lane_of[t], dy(2, k, h, t) - dz(1, k, h, t))
                                store(1, k, h, lane_of[t], dz(0, k, h, t) - dx(2, k, h, t))
                                store(2, k, h, lane_of[t], dx(1, k, h, t) - dy(0, k, h, t))

                for tile in range(full // LANES):
                    lane = 2 * tile * LANES
                    green = green_of(lane)
                    gy = green * ky_ref[0:1, lane : lane + LANES]

                    def dy_pair(got, c, k, h, t, gy=gy):
                        value = gy * got[c, k, h, 1 - t]
                        return value if t == 0 else -value

                    curl((lane, lane + LANES), dy_pair, green)
                if full < G:
                    lane = 2 * full
                    green = green_of(lane)
                    gy = green * ky_ref[0:1, lane : lane + LANES]

                    def dy_roll(got, c, k, h, t):
                        return gy * pltpu.roll(got[c, k, h, t], LANES // 2, 1)

                    curl((lane,), dy_roll, green)
                return 0

            lax.fori_loop(0, G // step, turn, 0)

            def narrow(u, _):
                at = pl.ds(pl.multiple_of(u * length, LANES), length)
                done = dot(inv_wide_ref[:, : 2 * length], turned_ref[:, at], NN) + dot(
                    inv_wide_ref[:, 2 * length :], turned_ref[:length, at], NN
                )
                high, low = halves(done)
                unit = (u // 2) * (2 * kept) + 2 * j + u % 2
                target = pl.ds(pl.multiple_of(unit * rows, 16), rows)
                for p in range(groups):
                    for part, value in ((0, high), (1, low)):
                        back_ref[p, target, part * length : (part + 1) * length] = value[
                            p * rows : (p + 1) * rows, :
                        ]
                return 0

            lax.fori_loop(0, 6, narrow, 0)
            return 0

        lax.fori_loop(0, kept, one_depth, 0)

        def depart(p):
            return pltpu.make_async_copy(held_ref.at[p], out_ref.at[p], came.at[p])

        def leave(p, _):
            done = dot(inv_line_ref[:, : 2 * length], back_ref[p], NT) + dot(
                inv_line_ref[:, 2 * length :], back_ref[p, :, :length], NT
            )
            pieces = [
                done[band * others * SUB : (band + 1) * others * SUB, :] for band in range(bands)
            ]
            if tiles * LANES > bands * width:
                pieces += [jnp.zeros((others * SUB, tiles * LANES - bands * width), f32)]
            line = jnp.concatenate(pieces, axis=1)
            for t in range(tiles):
                held_ref[p, :, t] = line[:, t * LANES : (t + 1) * LANES].reshape(others, SUB, LANES)
            depart(p).start()
            return 0

        lax.fori_loop(0, groups, leave, 0)
        for p in range(groups):
            depart(p).wait()

    anywhere = pl.BlockSpec(memory_space=pltpu.HBM)
    flops = 6 * (4 * groups * width * G * length + 24 * kept * length * G * length)
    return pl.pallas_call(
        kernel,
        out_shape=jax.ShapeDtypeStruct(lines.shape, f32),
        in_specs=[pl.BlockSpec(memory_space=pltpu.SMEM)] + [anywhere] * 4,
        out_specs=anywhere,
        scratch_shapes=[
            pltpu.VMEM(lines.shape, f32),
            *(pltpu.VMEM(table.shape, table.dtype) for table in tables),
            pltpu.SemaphoreType.DMA((groups,)),
            pltpu.SemaphoreType.DMA((3,)),
            pltpu.VMEM((kept, 2 * G, 6 * length), bf16),
            pltpu.VMEM((length, 6 * length), f32),
            pltpu.VMEM((2 * length, 6 * length), bf16),
            pltpu.VMEM((groups, width, 2 * length), bf16),
        ],
        cost_estimate=pl.CostEstimate(
            flops=flops, bytes_accessed=8 * lines.size, transcendentals=kept * G * G
        ),
        compiler_params=pltpu.CompilerParams(vmem_limit_bytes=ALL_VMEM),
        name="planes",
    )(place, lines, *tables)


def halo(slabs):
    def shifted(piece, axis, up):
        devices = lax.axis_size(axis)
        pairs = [(i, i + 1) for i in range(devices - 1)]
        if not up:
            pairs = [(j, i) for i, j in pairs]
        return lax.ppermute(piece, axis, pairs)

    last_rows, first_rows, last_cols, first_cols = slabs
    return (
        shifted(last_cols, "py", True),
        shifted(first_cols, "py", False),
        shifted(last_rows, "px", True),
        shifted(first_rows, "px", False),
    )


def depth_weights(G):
    width = 2 * G
    at = np.arange(width) % G
    rows = []
    for k in range(width // LANES):
        for shift, weight in ((1, 8.0), (-1, -8.0), (2, -1.0), (-2, 1.0)):
            inside = (at + shift >= 0) & (at + shift < G)
            rows.append(np.where(inside, weight / 12.0, 0.0)[k * LANES : (k + 1) * LANES])
    return np.stack(rows).astype(np.float32)


def stretch(field, flow, left, right, size):
    rows, cols, G = size.rows, size.cols, size.G
    span = 2 * G // LANES
    many = cols * G // LANES
    half = LANES // 2

    def kernel(field_hbm, flow_ref, left_ref, right_ref, weight_ref, out_ref, field_ref, sem,
               ext_ref, turned_ref):
        whole = pltpu.make_async_copy(field_hbm, field_ref, sem)

        @pl.when(pl.program_id(0) == 0)
        def _():
            whole.start()
            ext_ref[:, 0:SUB, :] = jnp.zeros((many + 2 * span, SUB, LANES), f32)
            ext_ref[:, SUB + rows :, :] = jnp.zeros((many + 2 * span, SUB, LANES), f32)

        def put(t, value):
            ext_ref[t, SUB : SUB + rows, :] = value
            turned_ref[t] = pltpu.roll(value, half, 1)

        for t in range(many):
            at = slice(t * LANES, (t + 1) * LANES)
            put(span + t, flow_ref[0, :, at])
        for t in range(span):
            at = slice(t * LANES, (t + 1) * LANES)
            put(t, left_ref[0, :, at])
            put(span + many + t, right_ref[0, :, at])
        lane = lax.broadcasted_iota(jnp.int32, (ROWS, LANES), 1)

        @pl.when(pl.program_id(0) == 0)
        def _():
            whole.wait()

        def block(b, _):
            base = span * (b + 1)
            for top in range(0, rows, ROWS):
                these = slice(top, top + ROWS)

                def tall_at(t, s):
                    return ext_ref[t, SUB + top + s : SUB + top + s + ROWS, :]

                def side_at(t):
                    return jnp.where(lane < half, turned_ref[t, these, :], turned_ref[t + 1, these, :])

                own = [tall_at(base + k, 0) for k in range(span)]
                for k in range(span):
                    t = base + k
                    deep = 0.0
                    for i, s in enumerate((1, -1, 2, -2)):
                        value = pltpu.roll(own[k], (-s) % LANES, 1)
                        if s > 0 and k + 1 < span:
                            value = jnp.where(
                                lane < LANES - s, value, pltpu.roll(own[k + 1], (-s) % LANES, 1)
                            )
                        if s < 0 and k > 0:
                            value = jnp.where(
                                lane >= -s, value, pltpu.roll(own[k - 1], (-s) % LANES, 1)
                            )
                        deep = deep + weight_ref[4 * k + i : 4 * k + i + 1, :] * value
                    side = 8.0 * (side_at(t + 1) - side_at(t - 2)) - (
                        tall_at(t + span, 0) - tall_at(t - span, 0)
                    )
                    tall = 8.0 * (tall_at(t, 1) - tall_at(t, -1)) - (tall_at(t, 2) - tall_at(t, -2))
                    at = pl.ds(pl.multiple_of((span * b + k) * LANES, LANES), LANES)
                    out_ref[0, these, at] = field_ref[2, these, at] * deep + (1.0 / 12.0) * (
                        field_ref[1, these, at] * side + field_ref[0, these, at] * tall
                    )
            return 0

        lax.fori_loop(0, cols // 2, block, 0, unroll=4)

    def part(*shape):
        return pl.BlockSpec((1,) + shape, lambda i: (i, 0, 0))

    return pl.pallas_call(
        kernel,
        grid=(3,),
        out_shape=jax.ShapeDtypeStruct((3, rows, cols * G), f32),
        in_specs=[
            pl.BlockSpec(memory_space=pltpu.HBM),
            part(rows, cols * G),
            part(rows, 2 * G),
            part(rows, 2 * G),
            pl.BlockSpec((4 * span, LANES), lambda i: (0, 0)),
        ],
        out_specs=part(rows, cols * G),
        scratch_shapes=[
            pltpu.VMEM((3, rows, cols * G), f32),
            pltpu.SemaphoreType.DMA,
            pltpu.VMEM((many + 2 * span, rows + 2 * SUB, LANES), f32),
            pltpu.VMEM((many + 2 * span, rows, LANES), f32),
        ],
        cost_estimate=pl.CostEstimate(
            flops=60 * flow.size, bytes_accessed=12 * flow.size, transcendentals=0
        ),
        compiler_params=pltpu.CompilerParams(vmem_limit_bytes=MOST_VMEM),
        name="stretch",
    )(field, flow, left, right, jnp.asarray(depth_weights(G)))


def add_rows(field, part, up, down, size):
    rows, width = size.rows, size.cols * size.G
    last = rows // SUB - 1

    def kernel(field_ref, part_ref, up_ref, down_ref, out_ref):
        out_ref[...] = part_ref[...]

        def add(c, row, value):
            at = slice(row, row + 1)
            out_ref[c, at, :] = part_ref[c, at, :] + (1.0 / 12.0) * field_ref[0, at, :] * value

        @pl.when(pl.program_id(0) == 0)
        def _():
            for c in range(3):
                far, near = up_ref[c, 0:1, :], up_ref[c, 1:2, :]
                add(c, 0, far - 8.0 * near)
                add(c, 1, near)

        @pl.when(pl.program_id(0) == 1)
        def _():
            for c in range(3):
                near, far = down_ref[c, 0:1, :], down_ref[c, 1:2, :]
                add(c, SUB - 1, 8.0 * near - far)
                add(c, SUB - 2, -near)

    edge = pl.BlockSpec((3, SUB, width), lambda i: (0, i * last, 0))
    whole = pl.BlockSpec((3, 2, width), lambda i: (0, 0, 0))
    return pl.pallas_call(
        kernel,
        grid=(2,),
        out_shape=jax.ShapeDtypeStruct((3, rows, width), f32),
        in_specs=[pl.BlockSpec((1, SUB, width), lambda i: (0, i * last, 0)), edge, whole, whole],
        out_specs=edge,
        input_output_aliases={1: 0},
        cost_estimate=pl.CostEstimate(
            flops=60 * width, bytes_accessed=4 * 40 * 3 * width, transcendentals=0
        ),
        compiler_params=pltpu.CompilerParams(vmem_limit_bytes=MOST_VMEM),
        name="add_rows",
    )(field, part, up, down)


def triple(table, axis):
    high, low = split_table(table)
    return np.concatenate([high, high, low], axis=axis)


def fast(vorticity, size):
    rows, cols, G, devices, groups = size.rows, size.cols, size.G, size.devices, size.groups
    length, bands, others = size.length, size.bands, size.G // size.cols
    axes = ("px", "py")
    place = lax.axis_index(axes).astype(jnp.int32)

    cells = np.array([
        q * cols + band * SUB + s for band in range(bands) for q in range(others) for s in range(SUB)
    ])
    lane_modes, lane_kinds = lane_order(G)
    row_modes = np.concatenate([np.arange(G)] * 2)
    row_kinds = np.repeat([0, 1], G)
    line_basis = basis(G, lane_modes, lane_kinds, length)[cells]
    wide_basis = basis(G, row_modes, row_kinds, length)
    line = split_table(line_basis)
    wide = triple(wide_basis.T, 1)
    inv_wide = triple(wide_basis * weights(row_modes, length), 1)
    inv_line = triple(line_basis * weights(lane_modes, length), 1)
    kx = np.broadcast_to(waves(np.arange(G), length)[:, None], (G, LANES)).astype(np.float32)
    signs = np.where(lane_kinds == 0, 1.0, -1.0)
    signs[: 2 * (G // LANES * LANES)] = 1.0
    ky = (waves(lane_modes, length) * signs).astype(np.float32)
    waves_of = np.zeros((G, LANES + length), np.float32)
    waves_of[:, :LANES] = kx
    waves_of[:, LANES:] = ky
    narrow = np.concatenate([inv_wide, inv_line, *line], axis=1)
    tables = tuple(jnp.asarray(t) for t in (narrow, wide, waves_of))

    def depth_tables(start, kept):
        modes = np.array([
            (start + j) * devices + d
            for j in range(kept) for k in (0, 1) for d in range(devices)
        ])
        kinds = np.array([k for j in range(kept) for k in (0, 1) for d in range(devices)])
        table = basis(G, modes, kinds, length)
        spare = ((0, 0), (0, size.spare)), ((0, 0), (size.spare, 0))

        def both(rows_of):
            return jnp.asarray(np.stack([np.stack(split_table(np.pad(rows_of, pad))) for pad in spare]))

        return both(table.T), both((table * weights(modes, length)).T)

    def exchange(value):
        value = value.reshape(devices, -1, LANES)
        return lax.all_to_all(value, axes, split_axis=0, concat_axis=0, tiled=True)

    arrived = []
    for start, kept in size.chunks:
        arrived.append(exchange(depth_forward(vorticity, depth_tables(start, kept)[0], size, kept)))
    returned = []
    for (start, kept), lines in zip(size.chunks, arrived):
        lines = lines.reshape(groups, others, size.tiles(kept), SUB, LANES)
        where = jnp.stack([place, jnp.int32(start)])
        returned.append(exchange(planes(lines, where, tables, size, kept)))
    flow = None
    for (start, kept), lines in zip(size.chunks, returned):
        last = start + kept == G // devices
        flow, *slabs, held = depth_inverse(
            lines.reshape(-1, LANES), depth_tables(start, kept)[1], flow, size, kept, last
        )
    left, right, up, down = halo(slabs)
    part = stretch(vorticity, held, left, right, size)
    return flow, add_rows(vorticity, part, up, down, size)


def with_halo(shard, sides, width):
    for axis, dim in sides:
        devices, length = (lax.axis_size(axis), shard.shape[dim])
        up = [(i, (i + 1) % devices) for i in range(devices - 1)]
        down = [(j, i) for i, j in up]
        last = lax.slice_in_dim(shard, length - width, length, axis=dim)
        leading = lax.slice_in_dim(shard, 0, width, axis=dim)
        before = lax.ppermute(last, axis, up)
        after = lax.ppermute(leading, axis, down)
        shard = jnp.concatenate([before, shard, after], axis=dim)
    return shard


def twiddle(count_in, count_out, length, factor):
    source = lax.broadcasted_iota(jnp.int32, (count_in, count_out), 0)
    target = lax.broadcasted_iota(jnp.int32, (count_in, count_out), 1)
    angle = (source * target % length).astype(jnp.float32) * (2.0 * math.pi / length)
    cosine = jnp.cos(angle) * factor
    sine = jnp.sin(angle) * factor
    return (
        jnp.broadcast_to(cosine, (3, count_in, count_out)),
        jnp.broadcast_to(sine, (3, count_in, count_out)),
    )


def product(einsum_form, first, second):
    return jnp.einsum(einsum_form, first, second, precision=highest)


def forward_left(pair, einsum_form, tables):
    real_part, imag_part = pair
    cosine_table, sine_table = tables
    return (
        product(einsum_form, cosine_table, real_part) + product(einsum_form, sine_table, imag_part),
        product(einsum_form, cosine_table, imag_part) - product(einsum_form, sine_table, real_part),
    )


def forward_right(pair, einsum_form, tables):
    real_part, imag_part = pair
    cosine_table, sine_table = tables
    return (
        product(einsum_form, real_part, cosine_table) + product(einsum_form, imag_part, sine_table),
        product(einsum_form, imag_part, cosine_table) - product(einsum_form, real_part, sine_table),
    )


def backward_left(pair, einsum_form, tables):
    real_part, imag_part = pair
    cosine_table, sine_table = tables
    return (
        product(einsum_form, cosine_table, real_part) - product(einsum_form, sine_table, imag_part),
        product(einsum_form, cosine_table, imag_part) + product(einsum_form, sine_table, real_part),
    )


def wavenumbers(start, count, length, position):
    index = start + lax.iota(jnp.int32, count)
    signed = jnp.where(index < length // 2, index, index - length)
    wave = signed.astype(jnp.float32) * (2.0 * math.pi / length)
    slope = jnp.where(index == length // 2, 0.0, wave)
    keep = jnp.where(index == length // 2, 0.0, 1.0)
    shape = [1, 1, 1, 1]
    shape[position] = count
    return (wave.reshape(shape), slope.reshape(shape), keep.reshape(shape))


def velocity_spectrum(pair, waves_x, waves_y, waves_z):
    square = waves_x[0] ** 2 + waves_y[0] ** 2 + waves_z[0] ** 2
    mask = waves_x[2] * waves_y[2] * waves_z[2]
    green = (
        mask
        * jnp.exp(-0.5 * smoothing * smoothing * square)
        / (square + jnp.where(square == 0.0, 1.0, 0.0))
    )
    slope_x, slope_y, slope_z = (waves_x[1][0], waves_y[1][0], waves_z[1][0])

    def curl(field):
        return jnp.stack(
            [
                slope_y * field[2] - slope_z * field[1],
                slope_z * field[0] - slope_x * field[2],
                slope_x * field[1] - slope_y * field[0],
            ]
        )

    real_part = pair[0] * green
    imag_part = pair[1] * green
    return (jnp.swapaxes(-curl(imag_part), 1, 2), jnp.swapaxes(curl(real_part), 1, 2))


def window(padded, axis, offset):
    starts = [0, 2, 2, 2]
    limits = [padded.shape[0], padded.shape[1] - 2, padded.shape[2] - 2, padded.shape[3] - 2]
    starts[axis] = starts[axis] + offset
    limits[axis] = limits[axis] + offset
    return lax.slice(padded, starts, limits)


def derivative(padded, axis):
    near = window(padded, axis, 1) - window(padded, axis, -1)
    far = window(padded, axis, 2) - window(padded, axis, -2)
    return (8.0 * near - far) / 12.0


def general(vorticity):
    block_rows = vorticity.shape[1]
    G = block_rows * lax.axis_size("px")
    block_cols = vorticity.shape[2] // G
    field = vorticity.reshape(3, block_rows, block_cols, G)
    length = 2 * G
    depth_tables = twiddle(G, G, length, 1.0)
    line_tables = twiddle(G, length, length, 1.0)
    inverse_tables = twiddle(length, G, length, 1.0 / length)
    closing = twiddle(G, G, length, 1.0 / length)
    weights = jnp.where(lax.iota(jnp.int32, G) == 0, 1.0, 2.0)[None, :, None]
    closing_cos = closing[0] * weights
    closing_sin = closing[1] * weights
    pair = (
        product("czk,cxyz->ckxy", depth_tables[0], field),
        -product("czk,cxyz->ckxy", depth_tables[1], field),
    )
    pair = (
        lax.all_to_all(pair[0], "py", split_axis=1, concat_axis=3, tiled=True),
        lax.all_to_all(pair[1], "py", split_axis=1, concat_axis=3, tiled=True),
    )
    pair = forward_left(pair, "cyl,ckxy->clkx", line_tables)
    pair = (
        lax.all_to_all(pair[0], "px", split_axis=1, concat_axis=3, tiled=True),
        lax.all_to_all(pair[1], "px", split_axis=1, concat_axis=3, tiled=True),
    )
    pair = forward_right(pair, "clkx,cxm->clkm", line_tables)
    rows = pair[0].shape[1]
    depth = pair[0].shape[2]
    waves_y = wavenumbers(lax.axis_index("px") * rows, rows, length, 1)
    waves_z = wavenumbers(lax.axis_index("py") * depth, depth, length, 2)
    waves_x = wavenumbers(0, length, length, 3)
    pair = velocity_spectrum(pair, waves_x, waves_y, waves_z)
    pair = backward_left(pair, "cmx,cklm->cxkl", inverse_tables)
    pair = (
        lax.all_to_all(pair[0], "px", split_axis=1, concat_axis=3, tiled=True),
        lax.all_to_all(pair[1], "px", split_axis=1, concat_axis=3, tiled=True),
    )
    pair = backward_left(pair, "cly,cxkl->cyxk", inverse_tables)
    pair = (
        lax.all_to_all(pair[0], "py", split_axis=1, concat_axis=3, tiled=True),
        lax.all_to_all(pair[1], "py", split_axis=1, concat_axis=3, tiled=True),
    )
    flow = product("cyxk,ckz->cyxz", pair[0], closing_cos) - product(
        "cyxk,ckz->cyxz", pair[1], closing_sin
    )
    flow = jnp.swapaxes(flow, 1, 2)
    padded = with_halo(flow, (("px", 1), ("py", 2)), 2)
    padded = jnp.pad(padded, ((0, 0), (0, 0), (0, 0), (2, 2)))
    stretching = (
        field[0] * derivative(padded, 1)
        + field[1] * derivative(padded, 2)
        + field[2] * derivative(padded, 3)
    )
    return (
        flow.reshape(3, block_rows, block_cols * G),
        stretching.reshape(3, block_rows, block_cols * G),
    )


def on_device(vorticity):
    sizes = fast_sizes(vorticity)
    if sizes is None:
        return general(vorticity)
    return fast(vorticity, sizes)


def solution(mesh):
    in_specs = (P(None, "px", "py"),)
    out_specs = (P(None, "px", "py"), P(None, "px", "py"))
    return jax.shard_map(
        on_device, mesh=mesh, in_specs=in_specs, out_specs=out_specs, check_vma=False
    )
```

```python
import math

import jax
import jax.numpy as jnp
import numpy as np
from jax import lax
from jax.experimental import pallas as pl
from jax.experimental.pallas import tpu as pltpu
from jax.sharding import PartitionSpec as P


smoothing = 1.0
highest = lax.Precision.HIGHEST
f32 = jnp.float32
bf16 = jnp.bfloat16
LANES = 128
SUB = 8
ROWS = 16
ALL_VMEM, MOST_VMEM, LESS_VMEM = 67_000_000, 50_000_000, 50_000_000


def split_table(table):
    high = table.astype(np.float32).astype(jnp.bfloat16)
    low = (table - high.astype(np.float64)).astype(np.float32).astype(jnp.bfloat16)
    return high, low


def waves(modes, length):
    return np.asarray(modes, np.float64) * (2.0 * math.pi / length)


def basis(points, modes, kinds, length):
    angle = (np.arange(points)[:, None] * np.asarray(modes)[None, :] % length) * (
        2.0 * math.pi / length
    )
    return np.where(np.asarray(kinds)[None, :] == 0, np.cos(angle), np.sin(angle))


def weights(modes, length):
    return np.where(np.asarray(modes) == 0, 1.0, 2.0) / length


def lane_order(modes):
    full = modes // LANES * LANES
    index, kind = [], []
    for start in range(0, full, LANES):
        for k in (0, 1):
            index += list(range(start, start + LANES))
            kind += [k] * LANES
    for k in (0, 1):
        index += list(range(full, modes))
        kind += [k] * (modes - full)
    return np.array(index), np.array(kind)


def dot(first, second, dims):
    return lax.dot_general(first, second, (dims, ((), ())), preferred_element_type=f32)


NN = ((1,), (0,))
NT = ((1,), (1,))
TN = ((0,), (0,))


def halves(value):
    high = value.astype(bf16)
    low = (value - high.astype(f32)).astype(bf16)
    return high, low


class Sizes:
    def __init__(self, rows, cols, G, devices, groups):
        self.rows, self.cols, self.G = rows, cols, G
        self.devices, self.groups = devices, groups
        self.bands = cols // SUB
        self.spare = G % LANES
        self.span = G + self.spare
        self.side = -(-cols // 2 * rows // LANES) * LANES
        self.length = 2 * G
        total = G // devices
        first = max(1, total * 2 // 3)
        self.chunks = [(0, first), (first, total - first)] if total > first else [(0, first)]

    def line(self, y):
        return (y // 2 + SUB // 2 * (y % 2)) % (self.cols // 2) * self.rows

    def slot(self, y):
        return y % 2 * self.side + self.line(y)

    def units(self, kept):
        return 6 * kept

    def tiles(self, kept):
        return -(-self.bands * self.units(kept) * self.rows // LANES)


def fast_sizes(vorticity):
    rows = vorticity.shape[1]
    groups = lax.axis_size("px")
    G = rows * groups
    cols = vorticity.shape[2] // G
    devices = groups * lax.axis_size("py")
    if rows % 16 or rows * cols % LANES or cols % (2 * SUB) not in (0, SUB) or cols % SUB or cols % 2:
        return None
    if G % devices or devices % SUB or G % LANES != LANES // 2:
        return None
    return Sizes(rows, cols, G, devices, groups)


class LaneMoves:
    def __init__(self, fragments):
        self.merged = []
        self.wanted = {}
        open_groups = {}
        for dest, to, source, start, width in fragments:
            at = to
            shift = (to - start) % LANES
            while at < to + width:
                origin = at - to + start
                take = min(to + width - at, LANES - origin % LANES)
                group = self._place(open_groups, origin // LANES, shift, origin % LANES, take, source)
                end = at + take
                while at < end:
                    part = min(end - at, LANES - at % LANES)
                    self.wanted.setdefault((dest, at // LANES), []).append((at % LANES, group))
                    at += part

    def _place(self, open_groups, tile, shift, lane, width, source):
        for group in open_groups.setdefault((tile, shift), []):
            pieces = self.merged[group][2]
            if all(lane >= at + wide or at >= lane + width for at, wide, _ in pieces):
                pieces.append((lane, width, source))
                return group
        self.merged.append((tile, shift, [(lane, width, source)]))
        open_groups[tile, shift].append(len(self.merged) - 1)
        return len(self.merged) - 1

    def run(self, load, store, held, shape):
        lane = lax.broadcasted_iota(jnp.int32, shape, 1)

        def choose(parts):
            value = None
            for at, part in sorted(parts, key=lambda pair: pair[0]):
                value = part() if value is None else jnp.where(lane >= at, part(), value)
            return value

        for index, (tile, shift, pieces) in enumerate(self.merged):
            value = choose(
                [(at, lambda source=source, tile=tile: load(source, tile)) for at, _, source in pieces]
            )
            held[index] = pltpu.roll(value, shift, 1) if shift else value
        for (dest, tile), parts in self.wanted.items():
            store(dest, tile, choose([(at, lambda index=index: held[index]) for at, index in parts]))


def depth_forward(shard, table, size, kept):
    rows, cols, G, devices = size.rows, size.cols, size.G, size.devices
    units, tiles, bands = size.units(kept), size.tiles(kept), size.bands
    block = 2 * kept * devices
    half = cols // 2 * rows
    moves = LaneMoves([
        (s, (band * units + u) * rows, u, size.slot(SUB * band + s), rows)
        for s in range(SUB)
        for band in range(bands)
        for u in range(units)
    ])

    def kernel(shard_ref, table_ref, out_ref, held_ref, sems, high_ref, low_ref, mid_ref, turned_ref):
        def fetch(c):
            return pltpu.make_async_copy(shard_ref.at[c], held_ref.at[c], sems.at[c])

        for c in range(3):
            fetch(c).start()

        for c in range(3):
            fetch(c).wait()
            for y in range(cols):
                odd, to = y % 2, size.line(y)
                start = y * G - odd * size.spare
                high, low = halves(held_ref[c, :, start : start + size.span])
                high_ref[c, odd, to : to + rows, :] = high
                low_ref[c, odd, to : to + rows, :] = low
        for c in range(3):
            for odd in (0, 1):
                at = odd * size.side
                mid_ref[c * block : (c + 1) * block, at : at + half] = (
                    dot(table_ref[odd, 0], high_ref[c, odd], NT)
                    + dot(table_ref[odd, 0], low_ref[c, odd], NT)
                    + dot(table_ref[odd, 1], high_ref[c, odd], NT)
                )

        def load(u, t):
            return mid_ref[u * devices : (u + 1) * devices, t * LANES : (t + 1) * LANES]

        def store(s, t, value):
            out_ref[pl.ds(t * SUB + s, devices, stride=tiles * SUB), :] = value

        moves.run(load, store, turned_ref, (devices, LANES))

    return pl.pallas_call(
        kernel,
        out_shape=jax.ShapeDtypeStruct((devices * tiles * SUB, LANES), f32),
        in_specs=[pl.BlockSpec(memory_space=pltpu.HBM), pl.BlockSpec(memory_space=pltpu.VMEM)],
        out_specs=pl.BlockSpec(memory_space=pltpu.VMEM),
        scratch_shapes=[
            pltpu.VMEM((3, rows, cols * G), f32),
            pltpu.SemaphoreType.DMA((3,)),
            pltpu.VMEM((3, 2, half, size.span), bf16),
            pltpu.VMEM((3, 2, half, size.span), bf16),
            pltpu.VMEM((3 * block, 2 * size.side), f32),
            pltpu.VMEM((len(moves.merged), devices, LANES), f32),
        ],
        cost_estimate=pl.CostEstimate(
            flops=18 * block * G * rows * cols,
            bytes_accessed=4 * (3 * rows * cols * G + devices * tiles * SUB * LANES),
            transcendentals=0,
        ),
        compiler_params=pltpu.CompilerParams(vmem_limit_bytes=ALL_VMEM),
        name="depth_forward",
    )(shard, table)


def depth_inverse(lines, table, before, size, kept, slabs):
    rows, cols, G, devices = size.rows, size.cols, size.G, size.devices
    units, tiles, bands = size.units(kept), size.tiles(kept), size.bands
    block = 2 * kept * devices
    half = cols // 2 * rows
    share = SUB * tiles * SUB
    extra = [] if before is None else [before]
    anywhere = pl.BlockSpec(memory_space=pltpu.HBM)
    whole = pl.BlockSpec(memory_space=pltpu.VMEM)
    moves = LaneMoves([
        (u, size.slot(SUB * band + s), s, (band * units + u) * rows, rows)
        for u in range(units)
        for band in range(bands)
        for s in range(SUB)
    ])
    outs = [jax.ShapeDtypeStruct((3, rows, cols * G), f32)]
    if slabs:
        outs += [jax.ShapeDtypeStruct((3, 2, cols * G), f32)] * 2
        outs += [jax.ShapeDtypeStruct((3, rows, 2 * G), f32)] * 2
    outs += [jax.ShapeDtypeStruct((3, rows, cols * G), f32)]

    def kernel(lines_ref, table_ref, *refs):
        out_ref, *slab_refs, ready_ref = refs[len(extra) : len(extra) + len(outs)]
        held_ref, mid_ref, turned_ref, done_ref, came, had, gone = refs[len(extra) + len(outs) :]

        def arrive(g):
            at = pl.ds(g * share, share)
            return pltpu.make_async_copy(lines_ref.at[at], held_ref.at[at], came.at[g])

        def earlier(c):
            return pltpu.make_async_copy(refs[0].at[c], ready_ref.at[c], had.at[c])

        def leave(c):
            return pltpu.make_async_copy(ready_ref.at[c], out_ref.at[c], gone.at[c])

        for g in range(devices // SUB):
            arrive(g).start()
        for g in range(devices // SUB):
            arrive(g).wait()

            def load(s, t):
                return held_ref[pl.ds(g * share + t * SUB + s, SUB, stride=tiles * SUB), :]

            def store(u, t, value):
                to = u * devices + g * SUB
                mid_ref[to : to + SUB, t * LANES : (t + 1) * LANES] = value

            moves.run(load, store, turned_ref.at[g], (SUB, LANES))

        if extra:
            for c in range(3):
                earlier(c).start()
        for c in range(3):
            for odd in (0, 1):
                at = odd * size.side
                high, low = halves(mid_ref[c * block : (c + 1) * block, at : at + half].T)
                done_ref[c, odd] = (
                    dot(high, table_ref[odd, 0], NN)
                    + dot(low, table_ref[odd, 0], NN)
                    + dot(high, table_ref[odd, 1], NN)
                )
        if extra:
            for c in range(3):
                earlier(c).wait()
        for c in range(3):
            for y in range(0, cols, 2):
                even = done_ref[c, 0, size.line(y) : size.line(y) + rows, :]
                odd = done_ref[c, 1, size.line(y + 1) : size.line(y + 1) + rows, :]
                shared = size.span - 2 * size.spare
                pair = jnp.concatenate(
                    [
                        even[:, :shared],
                        even[:, shared:] + odd[:, : 2 * size.spare],
                        odd[:, 2 * size.spare :],
                    ],
                    axis=1,
                )
                if extra:
                    pair = pair + ready_ref[c, :, y * G : (y + 2) * G]
                ready_ref[c, :, y * G : (y + 2) * G] = pair
                if slabs:
                    slab_refs[0][c, :, y * G : (y + 2) * G] = pair[rows - 2 :, :]
                    slab_refs[1][c, :, y * G : (y + 2) * G] = pair[:2, :]
                if slabs and y == cols - 2:
                    slab_refs[2][c] = pair
                if slabs and y == 0:
                    slab_refs[3][c] = pair
            leave(c).start()
        for c in range(3):
            leave(c).wait()

    return pl.pallas_call(
        kernel,
        out_shape=outs,
        in_specs=[anywhere, whole] + [anywhere] * len(extra),
        out_specs=[anywhere] + [whole] * (len(outs) - 1),
        scratch_shapes=[
            pltpu.VMEM((devices * tiles * SUB, LANES), f32),
            pltpu.VMEM((3 * block, 2 * size.side), f32),
            pltpu.VMEM((devices // SUB, len(moves.merged), SUB, LANES), f32),
            pltpu.VMEM((3, 2, half, size.span), f32),
            pltpu.SemaphoreType.DMA((devices // SUB,)),
            pltpu.SemaphoreType.DMA((3,)),
            pltpu.SemaphoreType.DMA((3,)),
        ],
        cost_estimate=pl.CostEstimate(
            flops=18 * block * G * rows * cols,
            bytes_accessed=4 * (9 * rows * cols * G + devices * tiles * SUB * LANES),
            transcendentals=0,
        ),
        compiler_params=pltpu.CompilerParams(vmem_limit_bytes=LESS_VMEM),
        name="depth_inverse",
    )(lines, table, *extra)


def planes(lines, place, tables, size, kept):
    rows, cols, G, devices, groups = size.rows, size.cols, size.G, size.devices, size.groups
    units, tiles, bands, length = size.units(kept), size.tiles(kept), size.bands, size.length
    width = units * rows
    step = 16
    unit_wave = 2.0 * math.pi / length
    full = G // LANES * LANES
    others = G // cols

    def kernel(place_ref, lines_ref, narrow_hbm, wide_hbm, waves_hbm, out_ref, held_ref, narrow_ref,
               wide_ref, waves_ref, came, told, left_ref, spec_ref, turned_ref, back_ref):
        inv_wide_ref = narrow_ref.at[:, : 3 * length]
        inv_line_ref = narrow_ref.at[:, 3 * length : 6 * length]
        line_high = narrow_ref.at[:, 6 * length : 7 * length]
        line_low = narrow_ref.at[:, 7 * length :]
        kx_ref = waves_ref.at[:, :LANES]
        ky_ref = waves_ref.at[:, LANES:]

        def come(p):
            return pltpu.make_async_copy(lines_ref.at[p], held_ref.at[p], came.at[p])

        def tell(i):
            source = (narrow_hbm, wide_hbm, waves_hbm)[i]
            return pltpu.make_async_copy(source, (narrow_ref, wide_ref, waves_ref)[i], told.at[i])

        tell(0).start()
        for p in range(groups):
            come(p).start()
        tell(1).start()
        tell(2).start()
        tell(0).wait()

        def arrive(p, _):
            come(p).wait()
            flat = jnp.concatenate(
                [held_ref[p, :, t].reshape(others * SUB, LANES).T for t in range(tiles)], axis=0
            )
            side = jnp.concatenate(
                [flat[band * width : (band + 1) * width, :] for band in range(bands)], axis=1
            )
            high, low = halves(side)
            done = (
                dot(high, line_high[...], NN)
                + dot(low, line_high[...], NN)
                + dot(high, line_low[...], NN)
            )
            for u in range(units):
                c, j, k = u // (2 * kept), u // 2 % kept, u % 2
                at = (2 * c + k) * length
                high, low = halves(done[u * rows : (u + 1) * rows, :])
                for part, value in ((0, high), (1, low)):
                    target = pl.ds(pl.multiple_of(part * G + p * rows, 16), rows)
                    left_ref[j, target, at : at + length] = value
            return 0

        lax.fori_loop(0, groups, arrive, 0)
        tell(1).wait()
        tell(2).wait()

        def one_depth(j, _):
            index = (place_ref[1] + j) * devices + place_ref[0]
            kz = index.astype(f32) * unit_wave

            def widen(u, _):
                at = pl.ds(pl.multiple_of(u * length, LANES), length)
                spec_ref[:, at] = dot(wide_ref[:, :length], left_ref[j, :, at], NN) + dot(
                    wide_ref[:, length:], left_ref[j, :G, at], NN
                )
                return 0

            lax.fori_loop(0, 6, widen, 0)

            def turn(r, _):
                top = pl.multiple_of(r * step, step)
                kx = kx_ref[pl.ds(top, step), :]

                def store(c, k, half, lane, value):
                    at = (2 * c + k) * length + lane
                    for part, piece in zip((0, 1), halves(value)):
                        target = pl.ds(pl.multiple_of(part * length + half * G + top, step), step)
                        turned_ref[target, at : at + LANES] = piece

                def green_of(lane):
                    ky = ky_ref[0:1, lane : lane + LANES]
                    square = kx * kx + ky * ky + kz * kz
                    return jnp.exp(-0.5 * smoothing * smoothing * square) / (
                        square + jnp.where(square == 0.0, 1.0, 0.0)
                    )

                def load(c, k, half, lane):
                    at = (2 * c + k) * length + lane
                    target = pl.ds(pl.multiple_of(half * G + top, step), step)
                    return spec_ref[target, at : at + LANES]

                def curl(lane_of, dy_of, green):
                    gx = green * kx
                    gz = green * kz
                    many = range(len(lane_of))
                    got = {
                        (c, k, h, t): load(c, k, h, lane_of[t])
                        for c in range(3) for k in (0, 1) for h in (0, 1) for t in many
                    }

                    def dx(c, k, h, t):
                        value = gx * got[c, k, 1 - h, t]
                        return value if h == 0 else -value

                    def dz(c, k, h, t):
                        value = gz * got[c, 1 - k, h, t]
                        return value if k == 0 else -value

                    def dy(c, k, h, t):
                        return dy_of(got, c, k, h, t)

                    for k in (0, 1):
                        for h in (0, 1):
                            for t in many:
                                store(0, k, h, lane_of[t], dy(2, k, h, t) - dz(1, k, h, t))
                                store(1, k, h, lane_of[t], dz(0, k, h, t) - dx(2, k, h, t))
                                store(2, k, h, lane_of[t], dx(1, k, h, t) - dy(0, k, h, t))

                for tile in range(full // LANES):
                    lane = 2 * tile * LANES
                    green = green_of(lane)
                    gy = green * ky_ref[0:1, lane : lane + LANES]

                    def dy_pair(got, c, k, h, t, gy=gy):
                        value = gy * got[c, k, h, 1 - t]
                        return value if t == 0 else -value

                    curl((lane, lane + LANES), dy_pair, green)
                if full < G:
                    lane = 2 * full
                    green = green_of(lane)
                    gy = green * ky_ref[0:1, lane : lane + LANES]

                    def dy_roll(got, c, k, h, t):
                        return gy * pltpu.roll(got[c, k, h, t], LANES // 2, 1)

                    curl((lane,), dy_roll, green)
                return 0

            lax.fori_loop(0, G // step, turn, 0)

            def narrow(u, _):
                at = pl.ds(pl.multiple_of(u * length, LANES), length)
                done = dot(inv_wide_ref[:, : 2 * length], turned_ref[:, at], NN) + dot(
                    inv_wide_ref[:, 2 * length :], turned_ref[:length, at], NN
                )
                high, low = halves(done)
                unit = (u // 2) * (2 * kept) + 2 * j + u % 2
                target = pl.ds(pl.multiple_of(unit * rows, 16), rows)
                for p in range(groups):
                    for part, value in ((0, high), (1, low)):
                        back_ref[p, target, part * length : (part + 1) * length] = value[
                            p * rows : (p + 1) * rows, :
                        ]
                return 0

            lax.fori_loop(0, 6, narrow, 0)
            return 0

        lax.fori_loop(0, kept, one_depth, 0)

        def depart(p):
            return pltpu.make_async_copy(held_ref.at[p], out_ref.at[p], came.at[p])

        def leave(p, _):
            done = dot(inv_line_ref[:, : 2 * length], back_ref[p], NT) + dot(
                inv_line_ref[:, 2 * length :], back_ref[p, :, :length], NT
            )
            pieces = [
                done[band * others * SUB : (band + 1) * others * SUB, :] for band in range(bands)
            ]
            if tiles * LANES > bands * width:
                pieces += [jnp.zeros((others * SUB, tiles * LANES - bands * width), f32)]
            line = jnp.concatenate(pieces, axis=1)
            for t in range(tiles):
                held_ref[p, :, t] = line[:, t * LANES : (t + 1) * LANES].reshape(others, SUB, LANES)
            depart(p).start()
            return 0

        lax.fori_loop(0, groups, leave, 0)
        for p in range(groups):
            depart(p).wait()

    anywhere = pl.BlockSpec(memory_space=pltpu.HBM)
    flops = 6 * (4 * groups * width * G * length + 24 * kept * length * G * length)
    return pl.pallas_call(
        kernel,
        out_shape=jax.ShapeDtypeStruct(lines.shape, f32),
        in_specs=[pl.BlockSpec(memory_space=pltpu.SMEM)] + [anywhere] * 4,
        out_specs=anywhere,
        scratch_shapes=[
            pltpu.VMEM(lines.shape, f32),
            *(pltpu.VMEM(table.shape, table.dtype) for table in tables),
            pltpu.SemaphoreType.DMA((groups,)),
            pltpu.SemaphoreType.DMA((3,)),
            pltpu.VMEM((kept, 2 * G, 6 * length), bf16),
            pltpu.VMEM((length, 6 * length), f32),
            pltpu.VMEM((2 * length, 6 * length), bf16),
            pltpu.VMEM((groups, width, 2 * length), bf16),
        ],
        cost_estimate=pl.CostEstimate(
            flops=flops, bytes_accessed=8 * lines.size, transcendentals=kept * G * G
        ),
        compiler_params=pltpu.CompilerParams(vmem_limit_bytes=ALL_VMEM),
        name="planes",
    )(place, lines, *tables)


def halo(slabs):
    def shifted(piece, axis, up):
        devices = lax.axis_size(axis)
        pairs = [(i, i + 1) for i in range(devices - 1)]
        if not up:
            pairs = [(j, i) for i, j in pairs]
        return lax.ppermute(piece, axis, pairs)

    last_rows, first_rows, last_cols, first_cols = slabs
    return (
        shifted(last_cols, "py", True),
        shifted(first_cols, "py", False),
        shifted(last_rows, "px", True),
        shifted(first_rows, "px", False),
    )


def depth_weights(G):
    width = 2 * G
    at = np.arange(width) % G
    rows = []
    for k in range(width // LANES):
        for shift, weight in ((1, 8.0), (-1, -8.0), (2, -1.0), (-2, 1.0)):
            inside = (at + shift >= 0) & (at + shift < G)
            rows.append(np.where(inside, weight / 12.0, 0.0)[k * LANES : (k + 1) * LANES])
    return np.stack(rows).astype(np.float32)


def stretch(field, flow, left, right, size):
    rows, cols, G = size.rows, size.cols, size.G
    span = 2 * G // LANES
    many = cols * G // LANES
    half = LANES // 2

    def kernel(field_hbm, flow_ref, left_ref, right_ref, weight_ref, out_ref, field_ref, sem,
               ext_ref, turned_ref):
        whole = pltpu.make_async_copy(field_hbm, field_ref, sem)

        @pl.when(pl.program_id(0) == 0)
        def _():
            whole.start()
            ext_ref[:, 0:SUB, :] = jnp.zeros((many + 2 * span, SUB, LANES), f32)
            ext_ref[:, SUB + rows :, :] = jnp.zeros((many + 2 * span, SUB, LANES), f32)

        def put(t, value):
            ext_ref[t, SUB : SUB + rows, :] = value
            turned_ref[t] = pltpu.roll(value, half, 1)

        for t in range(many):
            at = slice(t * LANES, (t + 1) * LANES)
            put(span + t, flow_ref[0, :, at])
        for t in range(span):
            at = slice(t * LANES, (t + 1) * LANES)
            put(t, left_ref[0, :, at])
            put(span + many + t, right_ref[0, :, at])
        lane = lax.broadcasted_iota(jnp.int32, (ROWS, LANES), 1)

        @pl.when(pl.program_id(0) == 0)
        def _():
            whole.wait()

        def block(b, _):
            base = span * (b + 1)
            for top in range(0, rows, ROWS):
                these = slice(top, top + ROWS)

                def tall_at(t, s):
                    return ext_ref[t, SUB + top + s : SUB + top + s + ROWS, :]

                def side_at(t):
                    return jnp.where(lane < half, turned_ref[t, these, :], turned_ref[t + 1, these, :])

                own = [tall_at(base + k, 0) for k in range(span)]
                for k in range(span):
                    t = base + k
                    deep = 0.0
                    for i, s in enumerate((1, -1, 2, -2)):
                        value = pltpu.roll(own[k], (-s) % LANES, 1)
                        if s > 0 and k + 1 < span:
                            value = jnp.where(
                                lane < LANES - s, value, pltpu.roll(own[k + 1], (-s) % LANES, 1)
                            )
                        if s < 0 and k > 0:
                            value = jnp.where(
                                lane >= -s, value, pltpu.roll(own[k - 1], (-s) % LANES, 1)
                            )
                        deep = deep + weight_ref[4 * k + i : 4 * k + i + 1, :] * value
                    side = 8.0 * (side_at(t + 1) - side_at(t - 2)) - (
                        tall_at(t + span, 0) - tall_at(t - span, 0)
                    )
                    tall = 8.0 * (tall_at(t, 1) - tall_at(t, -1)) - (tall_at(t, 2) - tall_at(t, -2))
                    at = pl.ds(pl.multiple_of((span * b + k) * LANES, LANES), LANES)
                    out_ref[0, these, at] = field_ref[2, these, at] * deep + (1.0 / 12.0) * (
                        field_ref[1, these, at] * side + field_ref[0, these, at] * tall
                    )
            return 0

        lax.fori_loop(0, cols // 2, block, 0, unroll=2)

    def part(*shape):
        return pl.BlockSpec((1,) + shape, lambda i: (i, 0, 0))

    return pl.pallas_call(
        kernel,
        grid=(3,),
        out_shape=jax.ShapeDtypeStruct((3, rows, cols * G), f32),
        in_specs=[
            pl.BlockSpec(memory_space=pltpu.HBM),
            part(rows, cols * G),
            part(rows, 2 * G),
            part(rows, 2 * G),
            pl.BlockSpec((4 * span, LANES), lambda i: (0, 0)),
        ],
        out_specs=part(rows, cols * G),
        scratch_shapes=[
            pltpu.VMEM((3, rows, cols * G), f32),
            pltpu.SemaphoreType.DMA,
            pltpu.VMEM((many + 2 * span, rows + 2 * SUB, LANES), f32),
            pltpu.VMEM((many + 2 * span, rows, LANES), f32),
        ],
        cost_estimate=pl.CostEstimate(
            flops=60 * flow.size, bytes_accessed=12 * flow.size, transcendentals=0
        ),
        compiler_params=pltpu.CompilerParams(vmem_limit_bytes=MOST_VMEM),
        name="stretch",
    )(field, flow, left, right, jnp.asarray(depth_weights(G)))


def add_rows(field, part, up, down, size):
    rows, width = size.rows, size.cols * size.G
    last = rows // SUB - 1

    def kernel(field_ref, part_ref, up_ref, down_ref, out_ref):
        out_ref[...] = part_ref[...]

        def add(c, row, value):
            at = slice(row, row + 1)
            out_ref[c, at, :] = part_ref[c, at, :] + (1.0 / 12.0) * field_ref[0, at, :] * value

        @pl.when(pl.program_id(0) == 0)
        def _():
            for c in range(3):
                far, near = up_ref[c, 0:1, :], up_ref[c, 1:2, :]
                add(c, 0, far - 8.0 * near)
                add(c, 1, near)

        @pl.when(pl.program_id(0) == 1)
        def _():
            for c in range(3):
                near, far = down_ref[c, 0:1, :], down_ref[c, 1:2, :]
                add(c, SUB - 1, 8.0 * near - far)
                add(c, SUB - 2, -near)

    edge = pl.BlockSpec((3, SUB, width), lambda i: (0, i * last, 0))
    whole = pl.BlockSpec((3, 2, width), lambda i: (0, 0, 0))
    return pl.pallas_call(
        kernel,
        grid=(2,),
        out_shape=jax.ShapeDtypeStruct((3, rows, width), f32),
        in_specs=[pl.BlockSpec((1, SUB, width), lambda i: (0, i * last, 0)), edge, whole, whole],
        out_specs=edge,
        input_output_aliases={1: 0},
        cost_estimate=pl.CostEstimate(
            flops=60 * width, bytes_accessed=4 * 40 * 3 * width, transcendentals=0
        ),
        compiler_params=pltpu.CompilerParams(vmem_limit_bytes=MOST_VMEM),
        name="add_rows",
    )(field, part, up, down)


def triple(table, axis):
    high, low = split_table(table)
    return np.concatenate([high, high, low], axis=axis)


def fast(vorticity, size):
    rows, cols, G, devices, groups = size.rows, size.cols, size.G, size.devices, size.groups
    length, bands, others = size.length, size.bands, size.G // size.cols
    axes = ("px", "py")
    place = lax.axis_index(axes).astype(jnp.int32)

    cells = np.array([
        q * cols + band * SUB + s for band in range(bands) for q in range(others) for s in range(SUB)
    ])
    lane_modes, lane_kinds = lane_order(G)
    row_modes = np.concatenate([np.arange(G)] * 2)
    row_kinds = np.repeat([0, 1], G)
    line_basis = basis(G, lane_modes, lane_kinds, length)[cells]
    wide_basis = basis(G, row_modes, row_kinds, length)
    line = split_table(line_basis)
    wide = triple(wide_basis.T, 1)
    inv_wide = triple(wide_basis * weights(row_modes, length), 1)
    inv_line = triple(line_basis * weights(lane_modes, length), 1)
    kx = np.broadcast_to(waves(np.arange(G), length)[:, None], (G, LANES)).astype(np.float32)
    signs = np.where(lane_kinds == 0, 1.0, -1.0)
    signs[: 2 * (G // LANES * LANES)] = 1.0
    ky = (waves(lane_modes, length) * signs).astype(np.float32)
    waves_of = np.zeros((G, LANES + length), np.float32)
    waves_of[:, :LANES] = kx
    waves_of[:, LANES:] = ky
    narrow = np.concatenate([inv_wide, inv_line, *line], axis=1)
    tables = tuple(jnp.asarray(t) for t in (narrow, wide, waves_of))

    def depth_tables(start, kept):
        modes = np.array([
            (start + j) * devices + d
            for j in range(kept) for k in (0, 1) for d in range(devices)
        ])
        kinds = np.array([k for j in range(kept) for k in (0, 1) for d in range(devices)])
        table = basis(G, modes, kinds, length)
        spare = ((0, 0), (0, size.spare)), ((0, 0), (size.spare, 0))

        def both(rows_of):
            return jnp.asarray(np.stack([np.stack(split_table(np.pad(rows_of, pad))) for pad in spare]))

        return both(table.T), both((table * weights(modes, length)).T)

    def exchange(value):
        value = value.reshape(devices, -1, LANES)
        return lax.all_to_all(value, axes, split_axis=0, concat_axis=0, tiled=True)

    arrived = []
    for start, kept in size.chunks:
        arrived.append(exchange(depth_forward(vorticity, depth_tables(start, kept)[0], size, kept)))
    returned = []
    for (start, kept), lines in zip(size.chunks, arrived):
        lines = lines.reshape(groups, others, size.tiles(kept), SUB, LANES)
        where = jnp.stack([place, jnp.int32(start)])
        returned.append(exchange(planes(lines, where, tables, size, kept)))
    flow = None
    for (start, kept), lines in zip(size.chunks, returned):
        last = start + kept == G // devices
        flow, *slabs, held = depth_inverse(
            lines.reshape(-1, LANES), depth_tables(start, kept)[1], flow, size, kept, last
        )
    left, right, up, down = halo(slabs)
    part = stretch(vorticity, held, left, right, size)
    return flow, add_rows(vorticity, part, up, down, size)


def with_halo(shard, sides, width):
    for axis, dim in sides:
        devices, length = (lax.axis_size(axis), shard.shape[dim])
        up = [(i, (i + 1) % devices) for i in range(devices - 1)]
        down = [(j, i) for i, j in up]
        last = lax.slice_in_dim(shard, length - width, length, axis=dim)
        leading = lax.slice_in_dim(shard, 0, width, axis=dim)
        before = lax.ppermute(last, axis, up)
        after = lax.ppermute(leading, axis, down)
        shard = jnp.concatenate([before, shard, after], axis=dim)
    return shard


def twiddle(count_in, count_out, length, factor):
    source = lax.broadcasted_iota(jnp.int32, (count_in, count_out), 0)
    target = lax.broadcasted_iota(jnp.int32, (count_in, count_out), 1)
    angle = (source * target % length).astype(jnp.float32) * (2.0 * math.pi / length)
    cosine = jnp.cos(angle) * factor
    sine = jnp.sin(angle) * factor
    return (
        jnp.broadcast_to(cosine, (3, count_in, count_out)),
        jnp.broadcast_to(sine, (3, count_in, count_out)),
    )


def product(einsum_form, first, second):
    return jnp.einsum(einsum_form, first, second, precision=highest)


def forward_left(pair, einsum_form, tables):
    real_part, imag_part = pair
    cosine_table, sine_table = tables
    return (
        product(einsum_form, cosine_table, real_part) + product(einsum_form, sine_table, imag_part),
        product(einsum_form, cosine_table, imag_part) - product(einsum_form, sine_table, real_part),
    )


def forward_right(pair, einsum_form, tables):
    real_part, imag_part = pair
    cosine_table, sine_table = tables
    return (
        product(einsum_form, real_part, cosine_table) + product(einsum_form, imag_part, sine_table),
        product(einsum_form, imag_part, cosine_table) - product(einsum_form, real_part, sine_table),
    )


def backward_left(pair, einsum_form, tables):
    real_part, imag_part = pair
    cosine_table, sine_table = tables
    return (
        product(einsum_form, cosine_table, real_part) - product(einsum_form, sine_table, imag_part),
        product(einsum_form, cosine_table, imag_part) + product(einsum_form, sine_table, real_part),
    )


def wavenumbers(start, count, length, position):
    index = start + lax.iota(jnp.int32, count)
    signed = jnp.where(index < length // 2, index, index - length)
    wave = signed.astype(jnp.float32) * (2.0 * math.pi / length)
    slope = jnp.where(index == length // 2, 0.0, wave)
    keep = jnp.where(index == length // 2, 0.0, 1.0)
    shape = [1, 1, 1, 1]
    shape[position] = count
    return (wave.reshape(shape), slope.reshape(shape), keep.reshape(shape))


def velocity_spectrum(pair, waves_x, waves_y, waves_z):
    square = waves_x[0] ** 2 + waves_y[0] ** 2 + waves_z[0] ** 2
    mask = waves_x[2] * waves_y[2] * waves_z[2]
    green = (
        mask
        * jnp.exp(-0.5 * smoothing * smoothing * square)
        / (square + jnp.where(square == 0.0, 1.0, 0.0))
    )
    slope_x, slope_y, slope_z = (waves_x[1][0], waves_y[1][0], waves_z[1][0])

    def curl(field):
        return jnp.stack(
            [
                slope_y * field[2] - slope_z * field[1],
                slope_z * field[0] - slope_x * field[2],
                slope_x * field[1] - slope_y * field[0],
            ]
        )

    real_part = pair[0] * green
    imag_part = pair[1] * green
    return (jnp.swapaxes(-curl(imag_part), 1, 2), jnp.swapaxes(curl(real_part), 1, 2))


def window(padded, axis, offset):
    starts = [0, 2, 2, 2]
    limits = [padded.shape[0], padded.shape[1] - 2, padded.shape[2] - 2, padded.shape[3] - 2]
    starts[axis] = starts[axis] + offset
    limits[axis] = limits[axis] + offset
    return lax.slice(padded, starts, limits)


def derivative(padded, axis):
    near = window(padded, axis, 1) - window(padded, axis, -1)
    far = window(padded, axis, 2) - window(padded, axis, -2)
    return (8.0 * near - far) / 12.0


def general(vorticity):
    block_rows = vorticity.shape[1]
    G = block_rows * lax.axis_size("px")
    block_cols = vorticity.shape[2] // G
    field = vorticity.reshape(3, block_rows, block_cols, G)
    length = 2 * G
    depth_tables = twiddle(G, G, length, 1.0)
    line_tables = twiddle(G, length, length, 1.0)
    inverse_tables = twiddle(length, G, length, 1.0 / length)
    closing = twiddle(G, G, length, 1.0 / length)
    weights = jnp.where(lax.iota(jnp.int32, G) == 0, 1.0, 2.0)[None, :, None]
    closing_cos = closing[0] * weights
    closing_sin = closing[1] * weights
    pair = (
        product("czk,cxyz->ckxy", depth_tables[0], field),
        -product("czk,cxyz->ckxy", depth_tables[1], field),
    )
    pair = (
        lax.all_to_all(pair[0], "py", split_axis=1, concat_axis=3, tiled=True),
        lax.all_to_all(pair[1], "py", split_axis=1, concat_axis=3, tiled=True),
    )
    pair = forward_left(pair, "cyl,ckxy->clkx", line_tables)
    pair = (
        lax.all_to_all(pair[0], "px", split_axis=1, concat_axis=3, tiled=True),
        lax.all_to_all(pair[1], "px", split_axis=1, concat_axis=3, tiled=True),
    )
    pair = forward_right(pair, "clkx,cxm->clkm", line_tables)
    rows = pair[0].shape[1]
    depth = pair[0].shape[2]
    waves_y = wavenumbers(lax.axis_index("px") * rows, rows, length, 1)
    waves_z = wavenumbers(lax.axis_index("py") * depth, depth, length, 2)
    waves_x = wavenumbers(0, length, length, 3)
    pair = velocity_spectrum(pair, waves_x, waves_y, waves_z)
    pair = backward_left(pair, "cmx,cklm->cxkl", inverse_tables)
    pair = (
        lax.all_to_all(pair[0], "px", split_axis=1, concat_axis=3, tiled=True),
        lax.all_to_all(pair[1], "px", split_axis=1, concat_axis=3, tiled=True),
    )
    pair = backward_left(pair, "cly,cxkl->cyxk", inverse_tables)
    pair = (
        lax.all_to_all(pair[0], "py", split_axis=1, concat_axis=3, tiled=True),
        lax.all_to_all(pair[1], "py", split_axis=1, concat_axis=3, tiled=True),
    )
    flow = product("cyxk,ckz->cyxz", pair[0], closing_cos) - product(
        "cyxk,ckz->cyxz", pair[1], closing_sin
    )
    flow = jnp.swapaxes(flow, 1, 2)
    padded = with_halo(flow, (("px", 1), ("py", 2)), 2)
    padded = jnp.pad(padded, ((0, 0), (0, 0), (0, 0), (2, 2)))
    stretching = (
        field[0] * derivative(padded, 1)
        + field[1] * derivative(padded, 2)
        + field[2] * derivative(padded, 3)
    )
    return (
        flow.reshape(3, block_rows, block_cols * G),
        stretching.reshape(3, block_rows, block_cols * G),
    )


def on_device(vorticity):
    sizes = fast_sizes(vorticity)
    if sizes is None:
        return general(vorticity)
    return fast(vorticity, sizes)


def solution(mesh):
    in_specs = (P(None, "px", "py"),)
    out_specs = (P(None, "px", "py"), P(None, "px", "py"))
    return jax.shard_map(
        on_device, mesh=mesh, in_specs=in_specs, out_specs=out_specs, check_vma=False
    )
```
